32 devices in a mesh: seq: 4 (over y, x), batch: 8 (over z, core).
Axes of the slice: x: 2, y: 2, z: 4, core: 2. Of those that a mesh axis runs over, the one named last changes fastest.
Arguments:
- hidden_state: bfloat16 [8, 4096, 768], P('batch', 'seq'), may hold values from -6 to 6
- segment_ids: int32 [8, 4096], P('batch', 'seq'), may hold values from 0 to 2, as said below
- valid_mask: int32 [8, 4096], P('batch', 'seq'), may hold values from 0 to 1, as said below
- cotangent: bfloat16 [8, 4096, 768], P('batch', 'seq'), may hold values from -6 to 6
- norm_gain: bfloat16 [768], P(('seq', 'batch')), may hold values from 0.5 to 1.5
- pool_gain: bfloat16 [768], P(('seq', 'batch')), may hold values from 0.5 to 1.5
- feed_gain: bfloat16 [768], P(('seq', 'batch')), may hold values from 0.5 to 1.5
- query_weight: bfloat16 [768, 768], P(('seq', 'batch')), may hold values from -0.0546875 to 0.0546875
- key_weight: bfloat16 [768, 768], P(('seq', 'batch')), may hold values from -0.21875 to 0.21875
- value_weight: bfloat16 [768, 768], P(('seq', 'batch')), may hold values from -0.21875 to 0.21875
- output_weight: bfloat16 [768, 768], P(('seq', 'batch')), may hold values from -1.25 to 1.25
- local_bias: float32 [12, 32], replicated, may hold values from -4 to 4
- global_bias: float32 [12, 32], replicated, may hold values from -4 to 4
- gate_weight: bfloat16 [768, 2048], P(('seq', 'batch')), may hold values from -0.21875 to 0.21875
- up_weight: bfloat16 [768, 2048], P(('seq', 'batch')), may hold values from -0.21875 to 0.21875
- down_weight: bfloat16 [2048, 768], P(('seq', 'batch')), may hold values from -0.25 to 0.25
Outputs:
- layer_output: bfloat16 [8, 4096, 768], P('batch', 'seq')
- input_delta: float32 [8, 4096, 768], P('batch', 'seq')
- norm_delta: float32 [768], P(('seq', 'batch'))
- pool_delta: float32 [768], P(('seq', 'batch'))
- feed_delta: float32 [768], P(('seq', 'batch'))
- query_delta: float32 [768, 768], P(('seq', 'batch'))
- key_delta: float32 [768, 768], P(('seq', 'batch'))
- value_delta: float32 [768, 768], P(('seq', 'batch'))
- output_delta: float32 [768, 768], P(('seq', 'batch'))
- local_delta: float32 [12, 32], replicated
- global_delta: float32 [12, 32], replicated
- gate_delta: float32 [768, 2048], P(('seq', 'batch'))
- up_delta: float32 [768, 2048], P(('seq', 'batch'))
- down_delta: float32 [2048, 768], P(('seq', 'batch'))
The draws below stay inside these ranges and needn't reach their ends.
Inputs may be any that keep to these rules, and one draw needn't show every extreme that they name: `segment_ids`: each pack holds three documents with ids 0, 1, 2 in order; every document fills whole aligned 16-token slots; the first and the last take 1 to 63 slots each. `valid_mask`: padding stands only at the end of each document's last 16-token slot, which holds 1 to 15 real tokens; all other tokens are real.
All inputs are finite; a program needn't handle non-finite values.
Results may differ from the reference program's by a relative error of at most 0.028.
Values may be sent and summed in bfloat16 or wider, within the bound.
No kernel may reach another device: no remote copies, remote signals or barrier semaphores. Data moves between devices by JAX's collectives and lax.ppermute only.
A program may use at most 320 MiB of HBM per device.

```python
import jax
import jax.numpy as jnp
from jax import lax

D = 768
H = 12
DH = 64
FF = 2048
NBUCK = 32
TOK_DEV = 1024
NGROUP = 8
GTOK = 4096


def pack_layout(key):
    base = jax.random.fold_in(key, 17)
    first_key, last_key, keep_key = jax.random.split(base, 3)
    unit_count = GTOK // 16
    per_device = TOK_DEV // 16
    first_units = jax.random.randint(first_key, (NGROUP, 1), 1, per_device, dtype=jnp.int32)
    last_units = jax.random.randint(last_key, (NGROUP, 1), 1, per_device, dtype=jnp.int32)
    unit_index = jnp.arange(unit_count, dtype=jnp.int32)[None, :]
    unit_segment = (unit_index >= first_units).astype(jnp.int32) + (unit_index >= unit_count - last_units).astype(jnp.int32)
    final_unit = jnp.concatenate([first_units - 1, unit_count - last_units - 1, jnp.full((NGROUP, 1), unit_count - 1, jnp.int32)], axis=1)
    keep_count = jax.random.randint(keep_key, (NGROUP, 3), 1, 16, dtype=jnp.int32)
    position = jnp.arange(GTOK, dtype=jnp.int32)
    segments = jnp.repeat(unit_segment, 16, axis=1)
    token_unit = position // 16
    token_offset = position % 16
    doc_final = jnp.take_along_axis(final_unit, segments, axis=1)
    doc_keep = jnp.take_along_axis(keep_count, segments, axis=1)
    valid_rows = jnp.where(token_unit[None, :] == doc_final, (token_offset[None, :] < doc_keep).astype(jnp.int32), 1).astype(jnp.int32)
    return (segments, valid_rows)


def draw_segment_ids(key, part):
    return pack_layout(key)[0]


def draw_valid_mask(key, part):
    return pack_layout(key)[1]


def block_scale(rng, dims, cuts, low, high):
    loudness, own = 1.0, jax.random.fold_in(rng, 6)
    for dim, blocks in cuts:
        draws = jnp.exp(jax.random.uniform(jax.random.fold_in(own, dim), (blocks,), jnp.float32, low / len(cuts), high / len(cuts)))
        loudness = loudness * jnp.repeat(draws, dims[dim] // blocks).reshape([-1 if axis == dim else 1 for axis in range(len(dims))])
    return loudness


def noise(key, extent, deviation, bound, pieces=(), kind=jnp.bfloat16):
    drawn = deviation * jax.random.normal(key, extent, jnp.float32)
    if pieces:
        drawn = drawn * block_scale(key, extent, pieces, -0.22, 0.18)
    return jnp.clip(drawn, -bound, bound).astype(kind)


def setup_inputs(seed: int = 0) -> dict:
    keys = jax.random.split(jax.random.key(seed), 17)
    return {
        "hidden_state": noise(keys[0], (NGROUP, GTOK, D), 1.0, 6.0, ((0, 8), (1, 4))),
        "segment_ids": draw_segment_ids(jax.random.fold_in(keys[16], 71), 0),
        "valid_mask": draw_valid_mask(jax.random.fold_in(keys[16], 71), 0),
        "cotangent": noise(keys[3], (NGROUP, GTOK, D), 1.0, 6.0, ((0, 8), (1, 4))),
        "norm_gain": jnp.clip(1.0 + 0.1 * jax.random.normal(keys[4], (D,), jnp.float32), 0.5, 1.5).astype(jnp.bfloat16),
        "pool_gain": jnp.clip(1.0 + 0.1 * jax.random.normal(keys[5], (D,), jnp.float32), 0.5, 1.5).astype(jnp.bfloat16),
        "feed_gain": jnp.clip(1.0 + 0.1 * jax.random.normal(keys[6], (D,), jnp.float32), 0.5, 1.5).astype(jnp.bfloat16),
        "query_weight": noise(keys[7], (D, H * DH), (16 * D) ** -0.5, 0.0546875, ((0, 32),)),
        "key_weight": noise(keys[8], (D, H * DH), D ** -0.5, 0.21875, ((0, 32),)),
        "value_weight": noise(keys[9], (D, H * DH), D ** -0.5, 0.21875, ((0, 32),)),
        "output_weight": noise(keys[10], (H * DH, D), (H * DH // 32) ** -0.5, 1.25, ((0, 32),)),
        "local_bias": noise(keys[11], (H, NBUCK), 1.0, 4.0, (), jnp.float32),
        "global_bias": noise(keys[12], (H, NBUCK), 1.0, 4.0, (), jnp.float32),
        "gate_weight": noise(keys[13], (D, FF), D ** -0.5, 0.21875, ((0, 32),)),
        "up_weight": noise(keys[14], (D, FF), D ** -0.5, 0.21875, ((0, 32),)),
        "down_weight": noise(keys[15], (FF, D), (FF // 4) ** -0.5, 0.25, ((0, 32),)),
    }


@jax.custom_vjp
def low(v):
    return lax.optimization_barrier(v.astype(jnp.bfloat16)).astype(jnp.float32)

@jax.custom_vjp
def low_back(v):
    return v

def low_keep(v):
    return (low(v), None)

def low_pass(kept, grad):
    return (grad,)

def back_keep(v):
    return (v, None)

def back_low(kept, grad):
    return (low(grad),)
low.defvjp(low_keep, low_pass)
low_back.defvjp(back_keep, back_low)
epsilon = 1e-06
highest = lax.Precision.HIGHEST
boundaries = (12, 16, 23, 32, 46, 64, 91)

def bucket_of(offset):
    distance = jnp.abs(offset)
    far_part = 8 + sum(((distance >= boundary).astype(jnp.int32) for boundary in boundaries))
    return 16 * (offset > 0).astype(jnp.int32) + jnp.where(distance < 8, distance, far_part)

def scaled(values, gain_row):
    return values * lax.rsqrt(lax.optimization_barrier(jnp.mean(values * values, axis=-1, keepdims=True)) + epsilon) * gain_row

def matmul(left, right):
    return jnp.dot(left, right, precision=highest)

def pack_forward(hidden, params, segments, valid_rows):
    norm_gain, pool_gain, feed_gain, query_weight, key_weight, value_weight, output_weight, local_bias, global_bias, gate_weight, up_weight, down_weight = params
    tok_count = hidden.shape[0]
    slot_count = tok_count // 16
    step_rows = min(512, tok_count)
    head_count = local_bias.shape[0]
    head_size = query_weight.shape[1] // head_count
    normed = low(scaled(hidden, norm_gain))
    queries = low_back(low(matmul(normed, query_weight)))
    key_rows = low_back(low(matmul(normed, key_weight)))
    value_rows = low_back(low(matmul(normed, value_weight)))
    valid_float = valid_rows.astype(jnp.float32)
    pooled = lax.optimization_barrier(jnp.sum((normed * valid_float[:, None]).reshape(slot_count, 16, -1), axis=1))
    pooled = low(scaled(pooled, pool_gain))
    global_keys = low_back(low(matmul(pooled, key_weight))).reshape(slot_count, head_count, head_size)
    global_values = low_back(low(matmul(pooled, value_weight))).reshape(slot_count, head_count, head_size)
    slot_segments = segments.reshape(slot_count, 16)[:, 0]
    slot_live = lax.optimization_barrier(jnp.sum(valid_rows.reshape(slot_count, 16), axis=1)) > 0
    keys_padded = jnp.pad(key_rows, ((128, 128), (0, 0)))
    values_padded = jnp.pad(value_rows, ((128, 128), (0, 0)))
    segments_padded = jnp.pad(segments, 128, constant_values=-1)
    valid_padded = jnp.pad(valid_rows, 128)
    window = step_rows + 256
    local_offset = jnp.arange(window, dtype=jnp.int32)[None, :] - 128 - jnp.arange(step_rows, dtype=jnp.int32)[:, None]
    local_bucket = bucket_of(local_offset)
    band_mask = jnp.abs(local_offset) <= 127

    def attend(step_index):
        row_start = step_index * step_rows
        query_part = lax.dynamic_slice_in_dim(queries, row_start, step_rows).reshape(step_rows, head_count, head_size)
        key_part = lax.dynamic_slice_in_dim(keys_padded, row_start, window).reshape(window, head_count, head_size)
        value_part = lax.dynamic_slice_in_dim(values_padded, row_start, window).reshape(window, head_count, head_size)
        segment_part = lax.dynamic_slice_in_dim(segments_padded, row_start, window)
        live_part = lax.dynamic_slice_in_dim(valid_padded, row_start, window)
        query_segments = lax.dynamic_slice_in_dim(segments, row_start, step_rows)
        local_mask = band_mask & (query_segments[:, None] == segment_part[None, :]) & (live_part[None, :] > 0)
        local_scores = jnp.einsum('qhd,khd->hqk', query_part, key_part, precision=highest) + local_bias[:, local_bucket]
        query_slots = (row_start + jnp.arange(step_rows, dtype=jnp.int32)) // 16
        slot_offset = jnp.arange(slot_count, dtype=jnp.int32)[None, :] - query_slots[:, None]
        global_mask = (query_segments[:, None] == slot_segments[None, :]) & slot_live[None, :]
        global_scores = jnp.einsum('qhd,ghd->hqg', query_part, global_keys, precision=highest) + global_bias[:, bucket_of(slot_offset)]
        scores = low_back(jnp.concatenate([local_scores, global_scores], axis=2))
        allowed = jnp.concatenate([local_mask, global_mask], axis=1)
        scores = jnp.where(allowed[None], scores, -1e+30)
        probabilities = low(jax.nn.softmax(scores, axis=-1))
        mixture = jnp.einsum('hqk,khd->qhd', probabilities[:, :, :window], value_part, precision=highest)
        mixture = mixture + jnp.einsum('hqg,ghd->qhd', probabilities[:, :, window:], global_values, precision=highest)
        return mixture.reshape(step_rows, head_count * head_size)
    mixture = lax.map(jax.checkpoint(attend), jnp.arange(tok_count // step_rows, dtype=jnp.int32))
    mixture = low_back(low(mixture.reshape(tok_count, -1)))
    middle = hidden + low_back(matmul(mixture, output_weight))
    normed_two = low(scaled(middle, feed_gain))
    gate_pre = low_back(matmul(normed_two, gate_weight))
    lift_pre = low_back(matmul(normed_two, up_weight))
    product = low(jax.nn.gelu(gate_pre, approximate=True) * lift_pre)
    return middle + low_back(matmul(product, down_weight))

def reference(hidden_state, segment_ids, valid_mask, cotangent, norm_gain, pool_gain, feed_gain, query_weight, key_weight, value_weight, output_weight, local_bias, global_bias, gate_weight, up_weight, down_weight):
    params = tuple((weight.astype(jnp.float32) for weight in (norm_gain, pool_gain, feed_gain, query_weight, key_weight, value_weight, output_weight, local_bias, global_bias, gate_weight, up_weight, down_weight)))

    def one_pack(totals, inputs):
        hidden, segments, valid_rows, cotangent_rows = inputs

        def forward_fn(hidden_in, params_in):
            return pack_forward(hidden_in, params_in, segments, valid_rows)
        output, pullback = jax.vjp(forward_fn, hidden.astype(jnp.float32), params)
        hidden_delta, param_delta = pullback(cotangent_rows.astype(jnp.float32))
        totals = jax.tree.map(jnp.add, totals, param_delta)
        return (totals, (output.astype(jnp.bfloat16), hidden_delta))
    totals = jax.tree.map(jnp.zeros_like, params)
    totals, (outputs, deltas) = lax.scan(one_pack, totals, (hidden_state, segment_ids, valid_mask, cotangent))
    return (outputs, deltas, totals[0], totals[1], totals[2], totals[3], totals[4], totals[5], totals[6], totals[7], totals[8], totals[9], totals[10], totals[11])
```

```python
import functools

import jax
import jax.numpy as jnp
from jax import lax
from jax.experimental import pallas as pl
from jax.experimental.pallas import tpu as pltpu
from jax.sharding import PartitionSpec as P

epsilon = 1e-06
highest = lax.Precision.HIGHEST
boundaries = (12, 16, 23, 32, 46, 64, 91)
never = -1e30
both = ("seq", "batch")
bf16 = jnp.bfloat16
f32 = jnp.float32


def bucket_of(offset):
    distance = jnp.abs(offset)
    far_part = 8 + sum(((distance >= boundary).astype(jnp.int32) for boundary in boundaries))
    return 16 * (offset > 0).astype(jnp.int32) + jnp.where(distance < 8, distance, far_part)


def scaled(values, gain_row):
    return (
        values * lax.rsqrt(jnp.mean(values * values, axis=-1, keepdims=True) + epsilon) * gain_row
    )


def activate(gate_pre, lift_pre):
    return jax.nn.gelu(gate_pre, approximate=True) * lift_pre


def forward_product(left, right):
    return jnp.dot(left, right, preferred_element_type=f32)


def weight_sum(left, right):
    return jnp.einsum("ra,rb->ab", left, right, preferred_element_type=f32)


def back_product(left, right):
    return jnp.einsum("ra,ba->rb", left, right, preferred_element_type=f32)


def dot_nt(left, right):
    return lax.dot_general(left, right, (((1,), (1,)), ((), ())), preferred_element_type=f32)


def dot_nn(left, right):
    return lax.dot_general(left, right, (((1,), (0,)), ((), ())), preferred_element_type=f32)


def stack_heads(rows):
    lane = lax.broadcasted_iota(jnp.int32, rows.shape, 1)
    zero = jnp.zeros_like(rows)
    return jnp.concatenate(
        [jnp.where(lane < 64, rows, zero), jnp.where(lane < 64, zero, rows)], axis=0
    )


def unstack_heads(wide):
    row = lax.broadcasted_iota(jnp.int32, (128, 128), 0)
    return jnp.where(row < 64, wide[:, :128], wide[:, 128:]).T


def upper_band():
    key = lax.broadcasted_iota(jnp.int32, (128, 256), 0)
    query = lax.broadcasted_iota(jnp.int32, (128, 256), 1) & 127
    return key > query


def spread_band(upper, own, merged):
    zero = jnp.zeros_like(merged)
    return jnp.concatenate(
        [jnp.where(upper, merged, zero), own, jnp.where(upper, zero, merged)], axis=0
    ).astype(bf16)


def block_scores(block, upper, query_two, key_ref, gkey_ref, bias_ref, klocal_ref, kglobal_ref, qfeat_ref):
    window = pl.ds(pl.multiple_of(block * 128, 128), 384)
    query_wide = jnp.concatenate([query_two, qfeat_ref[block]], axis=1)
    key_wide = jnp.concatenate([key_ref[window, :], klocal_ref[window, :]], axis=1)
    local = dot_nt(key_wide, query_wide)
    own = local[128:256] + bias_ref[0, 0:128]
    merged = jnp.where(upper, local[0:128], local[256:384]) + bias_ref[0, 128:256]
    gkey_wide = jnp.concatenate([gkey_ref[...], kglobal_ref[0, block]], axis=1)
    return own, merged, dot_nt(gkey_wide, query_wide)


def attend_forward(
    query_ref, key_ref, value_ref, gkey_ref, gvalue_ref, bias_ref, klocal_ref, kglobal_ref, qfeat_ref,
    out_ref, log_ref, value_turned, gvalue_turned,
):
    value_turned[...] = value_ref[...].T
    gvalue_turned[...] = gvalue_ref[...].T
    upper = upper_band()

    def step(block, carry):
        rows = pl.ds(pl.multiple_of(block * 128, 128), 128)
        window = pl.ds(pl.multiple_of(block * 128, 128), 384)
        query_two = stack_heads(query_ref[rows, :])
        own, merged, far = block_scores(
            block, upper, query_two, key_ref, gkey_ref, bias_ref, klocal_ref, kglobal_ref, qfeat_ref
        )
        peak = jnp.maximum(
            jnp.maximum(
                jnp.max(own, axis=0, keepdims=True), jnp.max(merged, axis=0, keepdims=True)
            ),
            jnp.max(far, axis=0, keepdims=True),
        )
        own, merged, far = jnp.exp(own - peak), jnp.exp(merged - peak), jnp.exp(far - peak)
        total = (
            jnp.sum(own, axis=0, keepdims=True)
            + jnp.sum(merged, axis=0, keepdims=True)
            + jnp.sum(far, axis=0, keepdims=True)
        )
        scale = 1.0 / total
        near_low = spread_band(upper, own * scale, merged * scale)
        far_low = (far * scale).astype(bf16)
        wide = dot_nn(value_turned[:, window], near_low) + dot_nn(gvalue_turned[...], far_low)
        out_ref[rows, :] = unstack_heads(wide).astype(bf16)
        log_ref[0, pl.ds(block, 1), :] = peak + jnp.log(total)
        return carry

    lax.fori_loop(0, query_ref.shape[0] // 128, step, 0)


def attend_backward(
    query_ref, grad_ref, key_ref, value_ref, gkey_ref, gvalue_ref, bias_ref, klocal_ref, kglobal_ref, qfeat_ref, log_ref,
    dquery_ref, dkey_ref, dvalue_ref, dgkey_ref, dgvalue_ref, near_ref, far_ref,
    key_turned, gkey_turned, key_sum, value_sum, gkey_sum, gvalue_sum,
):
    key_turned[...] = key_ref[...].T
    gkey_turned[...] = gkey_ref[...].T
    for total_ref in (key_sum, value_sum, gkey_sum, gvalue_sum, near_ref, far_ref):
        total_ref[...] = jnp.zeros_like(total_ref)
    upper = upper_band()
    lane = lax.broadcasted_iota(jnp.int32, (256, 128), 0)
    column = lax.broadcasted_iota(jnp.int32, (256, 128), 1)
    slot_column = (lane // 128) * 8 + (lane % 128) // 16

    def step(block, carry):
        rows = pl.ds(pl.multiple_of(block * 128, 128), 128)
        window = pl.ds(pl.multiple_of(block * 128, 128), 384)
        query_two = stack_heads(query_ref[rows, :])
        grad_two = stack_heads(grad_ref[rows, :])
        own, merged, far = block_scores(
            block, upper, query_two, key_ref, gkey_ref, bias_ref, klocal_ref, kglobal_ref, qfeat_ref
        )
        logs = log_ref[0, pl.ds(block, 1), :]
        own, merged, far = jnp.exp(own - logs), jnp.exp(merged - logs), jnp.exp(far - logs)
        value_sum[window, :] += dot_nn(spread_band(upper, own, merged), grad_two)
        gvalue_sum[...] += dot_nn(far.astype(bf16), grad_two)
        near_dot = dot_nt(value_ref[window, :], grad_two)
        own_dot = near_dot[128:256]
        merged_dot = jnp.where(upper, near_dot[0:128], near_dot[256:384])
        far_dot = dot_nt(gvalue_ref[...], grad_two)
        centre = (
            jnp.sum(own * own_dot, axis=0, keepdims=True)
            + jnp.sum(merged * merged_dot, axis=0, keepdims=True)
            + jnp.sum(far * far_dot, axis=0, keepdims=True)
        )
        own = own * (own_dot - centre)
        merged = merged * (merged_dot - centre)
        far = (far * (far_dot - centre)).astype(bf16)
        near_ref[0, 0:128, :] += own
        near_ref[0, 128:256, :] += merged
        choose = (column == slot_column + block * 16).astype(bf16)
        far_ref[0] += dot_nn(far, choose)
        near_low = spread_band(upper, own, merged)
        key_sum[window, :] += dot_nn(near_low, query_two)
        gkey_sum[...] += dot_nn(far, query_two)
        wide = dot_nn(key_turned[:, window], near_low) + dot_nn(gkey_turned[...], far)
        dquery_ref[rows, :] = unstack_heads(wide).astype(bf16)
        return carry

    lax.fori_loop(0, query_ref.shape[0] // 128, step, 0)
    dkey_ref[...] = key_sum[...].astype(bf16)
    dvalue_ref[...] = value_sum[...].astype(bf16)
    dgkey_ref[...] = gkey_sum[...].astype(bf16)
    dgvalue_ref[...] = gvalue_sum[...].astype(bf16)


def column_block(rows):
    return pl.BlockSpec((rows, 128), lambda pair: (0, pair))


def pair_block(*shape):
    zeros = (0,) * len(shape)
    return pl.BlockSpec((1,) + shape, lambda pair: (pair,) + zeros)


def fixed_block(*shape):
    zeros = (0,) * len(shape)
    return pl.BlockSpec(shape, lambda pair: zeros)


def attention_specs(rows, slots):
    blocks = rows // 128
    return [
        column_block(rows + 256),
        column_block(rows + 256),
        column_block(slots),
        column_block(slots),
        pair_block(256, 256),
        fixed_block(rows + 256, 128),
        pair_block(blocks, slots, 128),
        fixed_block(blocks, 256, 128),
    ]


def attention_forward(queries, keys, values, gkeys, gvalues, bias, klocal, kglobal, qfeat):
    rows, width = queries.shape
    slots = gkeys.shape[0]
    pairs = width // 128
    return pl.pallas_call(
        attend_forward,
        grid=(pairs,),
        in_specs=[column_block(rows)] + attention_specs(rows, slots),
        out_specs=[column_block(rows), pair_block(rows // 128, 256)],
        out_shape=[
            jax.ShapeDtypeStruct((rows, width), bf16),
            jax.ShapeDtypeStruct((pairs, rows // 128, 256), f32),
        ],
        scratch_shapes=[pltpu.VMEM((128, rows + 256), bf16), pltpu.VMEM((128, slots), bf16)],
        compiler_params=pltpu.CompilerParams(vmem_limit_bytes=48 << 20),
        cost_estimate=pl.CostEstimate(
            flops=8 * rows * (384 + slots) * width, bytes_accessed=16 << 20, transcendentals=0
        ),
    )(queries, keys, values, gkeys, gvalues, bias, klocal, kglobal, qfeat)


def attention_backward(queries, grads, keys, values, gkeys, gvalues, bias, klocal, kglobal, qfeat, logs):
    rows, width = queries.shape
    slots = gkeys.shape[0]
    pairs = width // 128
    return pl.pallas_call(
        attend_backward,
        grid=(pairs,),
        in_specs=[column_block(rows), column_block(rows)]
        + attention_specs(rows, slots)
        + [pair_block(rows // 128, 256)],
        out_specs=[
            column_block(rows),
            column_block(rows + 256),
            column_block(rows + 256),
            column_block(slots),
            column_block(slots),
            pair_block(256, 256),
            pair_block(slots, 128),
        ],
        out_shape=[
            jax.ShapeDtypeStruct((rows, width), bf16),
            jax.ShapeDtypeStruct((rows + 256, width), bf16),
            jax.ShapeDtypeStruct((rows + 256, width), bf16),
            jax.ShapeDtypeStruct((slots, width), bf16),
            jax.ShapeDtypeStruct((slots, width), bf16),
            jax.ShapeDtypeStruct((pairs, 256, 256), f32),
            jax.ShapeDtypeStruct((pairs, slots, 128), f32),
        ],
        scratch_shapes=[
            pltpu.VMEM((128, rows + 256), bf16),
            pltpu.VMEM((128, slots), bf16),
            pltpu.VMEM((rows + 256, 128), f32),
            pltpu.VMEM((rows + 256, 128), f32),
            pltpu.VMEM((slots, 128), f32),
            pltpu.VMEM((slots, 128), f32),
        ],
        compiler_params=pltpu.CompilerParams(vmem_limit_bytes=48 << 20),
        cost_estimate=pl.CostEstimate(
            flops=20 * rows * (384 + slots) * width, bytes_accessed=24 << 20, transcendentals=0
        ),
    )(queries, grads, keys, values, gkeys, gvalues, bias, klocal, kglobal, qfeat, logs)


def choose_bias(bucket, table):
    chosen = jnp.zeros((), f32)
    for index in range(table.shape[0]):
        chosen = jnp.where(bucket == index, table[index], chosen)
    return chosen


def near_offset():
    place = lax.broadcasted_iota(jnp.int32, (256, 256), 0)
    query = lax.broadcasted_iota(jnp.int32, (256, 256), 1) & 127
    return ((place - query + 128) & 255) - 128


def near_bias(local_bias):
    heads, buckets = local_bias.shape
    pairs = heads // 2
    offset = near_offset()
    table = jnp.repeat(local_bias.T.reshape(buckets, pairs, 1, 2), 128, axis=3)
    chosen = choose_bias(bucket_of(offset)[None], table)
    return jnp.where((offset == -128)[None], never, chosen)


def far_features(global_bias, slot_segments, slot_live, first_slot, blocks):
    heads, buckets = global_bias.shape
    pairs = heads // 2
    slots = slot_segments.shape[0]
    shape = (1, blocks, slots, 128)
    lane = lax.broadcasted_iota(jnp.int32, shape, 3)
    query_slot = first_slot + lax.broadcasted_iota(jnp.int32, shape, 1) * 8 + (lane & 7)
    bucket = bucket_of(lax.broadcasted_iota(jnp.int32, shape, 2) - query_slot)
    per_lane = jnp.repeat(global_bias.T.reshape(buckets, pairs, 2), 8, axis=2)
    table = jnp.tile(per_lane, (1, 1, 8)).reshape(buckets, pairs, 1, 1, 128)
    chosen = choose_bias(bucket, table)
    high = lax.reduce_precision(chosen, 8, 7)
    middle = lax.reduce_precision(chosen - high, 8, 7)
    lowest = chosen - high - middle
    part = lane // 16
    allowed = (slot_segments[None, None, :, None] == lane - 48) & slot_live[None, None, :, None]
    barred = jnp.where((lane >= 48) & (lane < 51) & ~allowed, never, 0.0)
    picked = jnp.where(part == 0, high, jnp.where(part == 1, middle, jnp.where(part == 2, lowest, barred)))
    return picked.astype(bf16)


def near_features(segments_ext, valid_ext):
    lane = lax.broadcasted_iota(jnp.int32, (segments_ext.shape[0], 128), 1)
    allowed = (segments_ext[:, None] == lane - 48) & (valid_ext[:, None] > 0)
    return jnp.where((lane >= 48) & (lane < 51) & ~allowed, never, 0.0).astype(bf16)


def query_features(own_segments):
    blocks = own_segments.shape[0] // 128
    shape = (blocks, 2, 128, 128)
    lane = lax.broadcasted_iota(jnp.int32, shape, 3)
    head = lax.broadcasted_iota(jnp.int32, shape, 1)
    token = lax.broadcasted_iota(jnp.int32, shape, 2)
    on_slot = (lane < 48) & ((lane & 15) == head * 8 + token // 16)
    on_segment = lane - 48 == own_segments.reshape(blocks, 1, 128, 1)
    return (on_slot | on_segment).astype(bf16).reshape(blocks, 256, 128)


def bucket_totals(near_sums, far_sums, first_slot, buckets):
    pairs, slots, _ = far_sums.shape
    ids = jnp.arange(buckets, dtype=jnp.int32)
    offset = near_offset()[:, :128]
    near_table = (bucket_of(offset)[:, :, None] == ids).astype(f32)
    near = jnp.einsum(
        "pmai,mib->pab", near_sums.reshape(pairs, 256, 2, 128), near_table, precision=highest
    ).reshape(pairs * 2, buckets)
    blocks = far_sums.shape[2] // 16
    own_slot = first_slot + jnp.arange(blocks * 8, dtype=jnp.int32).reshape(blocks, 8)
    far_offset = jnp.arange(slots, dtype=jnp.int32)[:, None, None] - own_slot[None]
    far_table = (bucket_of(far_offset)[..., None] == ids).astype(f32)
    far = jnp.einsum(
        "pgnat,gntb->pab", far_sums.reshape(pairs, slots, blocks, 2, 8), far_table, precision=highest
    ).reshape(pairs * 2, buckets)
    return near, far


def neighbour_rows(rows, width):
    count = lax.axis_size("seq")
    ends = count - 1
    before = lax.ppermute(rows[-width:], "seq", [(i, (i + 1) % count) for i in range(ends)])
    after = lax.ppermute(rows[:width], "seq", [((i + 1) % count, i) for i in range(ends)])
    return before, after


def return_rows(before, after):
    count = lax.axis_size("seq")
    ends = count - 1
    to_tail = lax.ppermute(before, "seq", [((i + 1) % count, i) for i in range(ends)])
    to_head = lax.ppermute(after, "seq", [(i, (i + 1) % count) for i in range(ends)])
    return to_head, to_tail


def gather_rows(array):
    return lax.all_gather(array, both, axis=0, tiled=True)


def scatter_rows(array):
    return lax.psum_scatter(
        array.astype(bf16), both, scatter_dimension=0, tiled=True
    ).astype(f32)


def on_device(
    hidden_state,
    segment_ids,
    valid_mask,
    cotangent,
    norm_gain,
    pool_gain,
    feed_gain,
    query_weight,
    key_weight,
    value_weight,
    output_weight,
    local_bias,
    global_bias,
    gate_weight,
    up_weight,
    down_weight,
):
    inner = query_weight.shape[1]
    hidden = gate_weight.shape[1]
    w_qkv = gather_rows(jnp.concatenate([query_weight, key_weight, value_weight], axis=1))
    w_rest = gather_rows(jnp.concatenate([output_weight, gate_weight, up_weight], axis=1))
    w_down = gather_rows(down_weight)
    w_query, w_key, w_value = w_qkv[:, :inner], w_qkv[:, inner : 2 * inner], w_qkv[:, 2 * inner :]
    model_width = hidden_state.shape[2]
    w_output = w_rest[:, :model_width]
    w_gate = w_rest[:, model_width : model_width + hidden]
    w_up = w_rest[:, model_width + hidden :]
    tok_rows = hidden_state.shape[1]
    bucket_count = local_bias.shape[1]
    block_count = tok_rows // 128
    own_slots = tok_rows // 16
    row_start = lax.axis_index("seq") * tok_rows
    first_slot = row_start // 16

    gains = jnp.stack([norm_gain, pool_gain, feed_gain]).astype(f32)
    gains = lax.all_gather(lax.all_gather(gains, "batch", axis=1, tiled=True), "seq", axis=1, tiled=True)
    gain_one, gain_pool, gain_two = gains[0], gains[1], gains[2]
    marks = lax.all_gather(jnp.concatenate([segment_ids, valid_mask], axis=0), "seq", axis=1, tiled=True)
    all_segments, all_valid = marks[0], marks[1]
    slot_count = all_segments.shape[0] // 16
    own_segments = segment_ids[0]
    valid_float = valid_mask[0].astype(f32)
    slot_segments = all_segments.reshape(slot_count, 16)[:, 0]
    slot_live = jnp.sum(all_valid.reshape(slot_count, 16), axis=1) > 0
    segments_ext = lax.dynamic_slice_in_dim(
        jnp.pad(all_segments, 128, constant_values=-1), row_start, tok_rows + 256
    )
    valid_ext = lax.dynamic_slice_in_dim(jnp.pad(all_valid, 128), row_start, tok_rows + 256)
    bias_near = near_bias(local_bias)
    feat_far = far_features(global_bias, slot_segments, slot_live, first_slot, block_count)
    feat_near = near_features(segments_ext, valid_ext)
    feat_query = query_features(own_segments)

    source = hidden_state[0].astype(f32)
    normed_full, norm_pull = jax.vjp(scaled, source, gain_one)
    normed = normed_full.astype(bf16)
    pooled_raw = jnp.sum(
        (normed.astype(f32) * valid_float[:, None]).reshape(own_slots, 16, model_width), axis=1
    )
    pooled_full, pool_pull = jax.vjp(scaled, pooled_raw, gain_pool)
    pooled = lax.all_gather(pooled_full.astype(bf16), "seq", axis=0, tiled=True)
    before, after = neighbour_rows(normed, 128)
    normed_ext = jnp.concatenate([before, normed, after], axis=0)

    queries = forward_product(normed, w_query).astype(bf16)
    keys = forward_product(normed_ext, w_key).astype(bf16)
    values = forward_product(normed_ext, w_value).astype(bf16)
    gkeys = forward_product(pooled, w_key).astype(bf16)
    gvalues = forward_product(pooled, w_value).astype(bf16)
    mixture, logs = attention_forward(
        queries, keys, values, gkeys, gvalues, bias_near, feat_near, feat_far, feat_query
    )

    middle = source + forward_product(mixture, w_output)
    normed_two_full, feed_pull = jax.vjp(scaled, middle, gain_two)
    normed_two = normed_two_full.astype(bf16)
    gate_pre = forward_product(normed_two, w_gate)
    lift_pre = forward_product(normed_two, w_up)
    product_full, act_pull = jax.vjp(activate, gate_pre, lift_pre)
    product = product_full.astype(bf16)
    layer_output = (middle + forward_product(product, w_down)).astype(bf16)
    upstream = cotangent[0]
    down_delta = scatter_rows(weight_sum(product, upstream))
    product_grad = back_product(upstream, w_down)
    gate_grad, lift_grad = act_pull(product_grad)
    gate_low = gate_grad.astype(bf16)
    lift_low = lift_grad.astype(bf16)
    normed_two_grad = back_product(gate_low, w_gate) + back_product(lift_low, w_up)
    middle_norm_grad, feed_delta = feed_pull(normed_two_grad)
    middle_grad = upstream.astype(f32) + middle_norm_grad
    attn_low = middle_grad.astype(bf16)
    rest_delta = scatter_rows(
        jnp.concatenate(
            [
                weight_sum(mixture, attn_low).astype(bf16),
                weight_sum(normed_two, gate_low).astype(bf16),
                weight_sum(normed_two, lift_low).astype(bf16),
            ],
            axis=1,
        )
    )
    mixture_grad = back_product(attn_low, w_output).astype(bf16)

    query_low, key_low, value_low, gkey_low, gvalue_low, near_sums, far_sums = attention_backward(
        queries, mixture_grad, keys, values, gkeys, gvalues, bias_near, feat_near, feat_far, feat_query, logs
    )
    qkv_delta = scatter_rows(
        jnp.concatenate(
            [
                weight_sum(normed, query_low).astype(bf16),
                (weight_sum(normed_ext, key_low) + weight_sum(pooled, gkey_low)).astype(bf16),
                (weight_sum(normed_ext, value_low) + weight_sum(pooled, gvalue_low)).astype(bf16),
            ],
            axis=1,
        )
    )
    pooled_grad = back_product(gkey_low, w_key) + back_product(gvalue_low, w_value)
    pooled_grad = jnp.sum(
        lax.all_to_all(
            pooled_grad.astype(bf16).reshape(-1, own_slots, model_width), "seq", 0, 0, tiled=True
        ).astype(f32),
        axis=0,
    )
    pooled_raw_grad, pool_delta = pool_pull(pooled_grad)
    key_part = back_product(key_low, w_key) + back_product(value_low, w_value)
    to_head, to_tail = return_rows(key_part[:128].astype(bf16), key_part[-128:].astype(bf16))
    edges = jnp.concatenate(
        [to_head.astype(f32), jnp.zeros((tok_rows - 256, model_width), f32), to_tail.astype(f32)]
    )
    normed_grad = back_product(query_low, w_query) + key_part[128:-128] + edges
    spread_grad = jnp.broadcast_to(
        pooled_raw_grad[:, None, :], (own_slots, 16, model_width)
    ).reshape(tok_rows, model_width)
    normed_grad = normed_grad + spread_grad * valid_float[:, None]
    source_grad, norm_delta = norm_pull(normed_grad)
    input_delta = middle_grad + source_grad
    local_delta, global_delta = bucket_totals(near_sums, far_sums, first_slot, bucket_count)
    small = jnp.concatenate(
        [norm_delta, pool_delta, feed_delta, local_delta.reshape(-1), global_delta.reshape(-1)]
    ).reshape(1, -1)
    small = jnp.sum(lax.all_gather(small, "batch", axis=0, tiled=True), axis=0, keepdims=True)
    small = jnp.sum(lax.all_gather(small, "seq", axis=0, tiled=True), axis=0)
    own_part = norm_gain.shape[0]
    place = (lax.axis_index("seq") * lax.axis_size("batch") + lax.axis_index("batch")) * own_part
    gain_deltas = [
        lax.dynamic_slice_in_dim(small[i * model_width : (i + 1) * model_width], place, own_part)
        for i in range(3)
    ]
    bias_size = local_bias.size
    local_total = small[3 * model_width : 3 * model_width + bias_size].reshape(local_bias.shape)
    global_total = small[3 * model_width + bias_size :].reshape(local_bias.shape)
    return (
        layer_output[None],
        input_delta[None],
        gain_deltas[0],
        gain_deltas[1],
        gain_deltas[2],
        qkv_delta[:, :inner],
        qkv_delta[:, inner : 2 * inner],
        qkv_delta[:, 2 * inner :],
        rest_delta[:, :model_width],
        local_total,
        global_total,
        rest_delta[:, model_width : model_width + hidden],
        rest_delta[:, model_width + hidden :],
        down_delta,
    )


def solution(mesh):
    row = P(both)
    matrix = P(both, None)
    return jax.shard_map(
        on_device,
        mesh=mesh,
        in_specs=(
            P("batch", "seq", None),
            P("batch", "seq"),
            P("batch", "seq"),
            P("batch", "seq", None),
            row,
            row,
            row,
            matrix,
            matrix,
            matrix,
            matrix,
            P(),
            P(),
            matrix,
            matrix,
            matrix,
        ),
        out_specs=(
            P("batch", "seq", None),
            P("batch", "seq", None),
            row,
            row,
            row,
            matrix,
            matrix,
            matrix,
            matrix,
            P(),
            P(),
            matrix,
            matrix,
            matrix,
        ),
        check_vma=False,
    )
```

```python
import jax
import jax.numpy as jnp
from jax import lax
from jax.experimental import pallas as pl
from jax.experimental.pallas import tpu as pltpu
from jax.sharding import Mesh
from jax.sharding import PartitionSpec as P

epsilon = 1e-06
boundaries = (12, 16, 23, 32, 46, 64, 91)
never = -1e30
seq = ("y", "x")
batch = ("z", "core")
everyone = seq + batch
bf16 = jnp.bfloat16
f32 = jnp.float32
i32 = jnp.int32
highest = lax.Precision.HIGHEST


def bucket_of(offset):
    distance = jnp.abs(offset)
    far_part = 8 + sum(((distance >= boundary).astype(i32) for boundary in boundaries))
    return 16 * (offset > 0).astype(i32) + jnp.where(distance < 8, distance, far_part)


def dot_nt(left, right):
    return lax.dot_general(left, right, (((1,), (1,)), ((), ())), preferred_element_type=f32)


def dot_nn(left, right):
    return lax.dot_general(left, right, (((1,), (0,)), ((), ())), preferred_element_type=f32)


def inverse_rms(values):
    return lax.rsqrt(jnp.mean(values * values, axis=-1, keepdims=True) + epsilon)


def norm_gradient(values, inverse, gain, grad):
    weighted = grad * gain
    mean = jnp.mean(weighted * values, axis=-1, keepdims=True)
    return inverse * weighted - (inverse * inverse * inverse * mean) * values


def stack_heads(rows):
    lane = lax.broadcasted_iota(i32, rows.shape, 1)
    zero = jnp.zeros_like(rows)
    return jnp.concatenate(
        [jnp.where(lane < 64, rows, zero), jnp.where(lane < 64, zero, rows)], axis=0
    )


def unstack_heads(wide):
    row = lax.broadcasted_iota(i32, (128, 128), 0)
    return jnp.where(row < 64, wide[:, :128], wide[:, 128:]).T


def upper_band():
    key = lax.broadcasted_iota(i32, (128, 256), 0)
    query = lax.broadcasted_iota(i32, (128, 256), 1) & 127
    return key > query


def spread_band(upper, own, merged):
    zero = jnp.zeros_like(merged)
    return jnp.concatenate(
        [jnp.where(upper, merged, zero), own, jnp.where(upper, zero, merged)], axis=0
    ).astype(bf16)


def window_of(block):
    return pl.ds(pl.multiple_of(block * 128, 128), 384)


def rows_of(block):
    return pl.ds(pl.multiple_of(block * 128, 128), 128)


def slot_lanes():
    row = lax.broadcasted_iota(i32, (256, 128), 0)
    lane = lax.broadcasted_iota(i32, (256, 128), 1)
    hit = (lane < 48) & ((lane & 15) == (row // 128) * 8 + (row % 128) // 16)
    return hit.astype(f32).astype(bf16)


def block_scores(block, upper, on_slot, query_two, key_ref, gkey_ref, bias_ref, klocal_ref, kglobal_ref, qfeat_ref):
    slots = gkey_ref.shape[0]
    window = window_of(block)
    segment_lanes = qfeat_ref[rows_of(block), :]
    features = jnp.concatenate([segment_lanes, segment_lanes], axis=0) + on_slot
    query_wide = jnp.concatenate([query_two, features], axis=1)
    key_wide = jnp.concatenate([key_ref[window, :], klocal_ref[window, :]], axis=1)
    local = dot_nt(key_wide, query_wide)
    own = local[128:256] + bias_ref[0, 0:128]
    merged = jnp.where(upper, local[0:128], local[256:384]) + bias_ref[0, 128:256]
    far_rows = pl.ds(pl.multiple_of(block * slots, 128), slots)
    gkey_wide = jnp.concatenate([gkey_ref[...], kglobal_ref[far_rows, :]], axis=1)
    return own, merged, dot_nt(gkey_wide, query_wide)


def attend_forward(
    source_ref, raw_ref, gain_ref, wq_ref, wk_ref, wv_ref, offsets_ref, klocal_ref, kglobal_ref, qfeat_ref,
    bias_ref, out_ref, log_ref, query_ref, key_ref, value_ref, gkey_ref, gvalue_ref, normed_ref, pooled_ref, gains_ref,
    value_turned, gvalue_turned,
):
    rows = query_ref.shape[0]
    slots = gkey_ref.shape[0]

    @pl.when(pl.program_id(0) == 0)
    def start():
        turned = gain_ref[...].astype(f32).T
        gains_ref[...] = turned[0:8]
        gain_one, gain_pool = turned[0:1], turned[1:2]

        def norm_rows(index, carry):
            part = pl.ds(pl.multiple_of(index * 128, 128), 128)
            values = source_ref[part, :].astype(f32)
            normed_ref[part, :] = (values * inverse_rms(values) * gain_one).astype(bf16)
            return carry

        lax.fori_loop(0, (rows + 256) // 128, norm_rows, 0)

        def pool_rows(index, carry):
            part = pl.ds(pl.multiple_of(index * 128, 128), 128)
            values = raw_ref[part, :].astype(f32) * gain_one
            pooled_ref[part, :] = (values * inverse_rms(values) * gain_pool).astype(bf16)
            return carry

        lax.fori_loop(0, slots // 128, pool_rows, 0)

    lane = lax.broadcasted_iota(i32, (256, 128), 1)
    spread = []
    for head in range(2):
        mine = jnp.where(lane == 2 * pl.program_id(0) + head, offsets_ref[...], 0.0)
        spread.append(jnp.broadcast_to(jnp.sum(mine, axis=1, keepdims=True), (256, 128)))
    lane_of = lax.broadcasted_iota(i32, (256, 256), 1)
    bias_ref[0] = align_offsets(jnp.concatenate(spread, axis=1), lane_of & 127, 7, -1)

    query_ref[...] = dot_nn(normed_ref[128 : 128 + rows, :], wq_ref[...]).astype(bf16)
    w_two = jnp.concatenate([wk_ref[...], wv_ref[...]], axis=1)
    two = dot_nn(normed_ref[...], w_two).astype(bf16)
    key_ref[...] = two[:, :128]
    value_ref[...] = two[:, 128:]
    value_turned[...] = two[:, 128:].T
    two = dot_nn(pooled_ref[...], w_two).astype(bf16)
    gkey_ref[...] = two[:, :128]
    gvalue_ref[...] = two[:, 128:]
    gvalue_turned[...] = two[:, 128:].T
    upper = upper_band()
    on_slot = slot_lanes()

    def step(block, carry):
        window = window_of(block)
        query_two = stack_heads(query_ref[rows_of(block), :])
        own, merged, far = block_scores(
            block, upper, on_slot, query_two, key_ref, gkey_ref, bias_ref, klocal_ref, kglobal_ref, qfeat_ref
        )
        peak = jnp.maximum(
            jnp.maximum(
                jnp.max(own, axis=0, keepdims=True), jnp.max(merged, axis=0, keepdims=True)
            ),
            jnp.max(far, axis=0, keepdims=True),
        )
        own, merged, far = jnp.exp(own - peak), jnp.exp(merged - peak), jnp.exp(far - peak)
        total = (
            jnp.sum(own, axis=0, keepdims=True)
            + jnp.sum(merged, axis=0, keepdims=True)
            + jnp.sum(far, axis=0, keepdims=True)
        )
        near_low = spread_band(upper, own, merged)
        wide = dot_nn(value_turned[:, window], near_low) + dot_nn(
            gvalue_turned[...], far.astype(bf16)
        )
        out_ref[rows_of(block), :] = unstack_heads(wide * (1.0 / total)).astype(bf16)
        log_ref[0, pl.ds(block, 1), :] = peak + jnp.log(total)
        return carry

    lax.fori_loop(0, rows // 128, step, 0, unroll=4)


def align_offsets(sums, step_of_lane, bits, sign):
    for bit in range(bits):
        shift = sign * (1 << bit)
        moved = jnp.concatenate([sums[shift:], sums[:shift]], axis=0)
        sums = jnp.where((step_of_lane >> bit) & 1 == 1, moved, sums)
    return sums


def two_totals(left, right):
    lane = lax.broadcasted_iota(i32, (left.shape[0], 128), 1)
    first = jnp.sum(left, axis=1, keepdims=True)
    second = jnp.sum(right, axis=1, keepdims=True)
    return jnp.where(lane == 0, first, jnp.where(lane == 1, second, 0.0))


def attend_backward(
    query_ref, grad_ref, key_ref, value_ref, gkey_ref, gvalue_ref, normed_ref, pooled_ref, wq_ref, wk_ref, wv_ref,
    log_ref, bias_ref, klocal_ref, kglobal_ref, qfeat_ref,
    dwq_ref, dwk_ref, dwv_ref, dnormed_ref, dpooled_ref, near_ref, far_ref,
    key_turned, gkey_turned, dquery, key_sum, value_sum, gkey_sum, gvalue_sum, near_sum, far_sum, normed_turned, pooled_turned,
):
    rows = query_ref.shape[0]
    slots = gkey_ref.shape[0]

    @pl.when(pl.program_id(0) == 0)
    def start():
        normed_turned[...] = normed_ref[...].T
        pooled_turned[...] = pooled_ref[...].T
        dnormed_ref[...] = jnp.zeros_like(dnormed_ref)
        dpooled_ref[...] = jnp.zeros_like(dpooled_ref)

    key_turned[...] = key_ref[...].T
    gkey_turned[...] = gkey_ref[...].T
    for total_ref in (key_sum, value_sum, gkey_sum, gvalue_sum, near_sum, far_sum):
        total_ref[...] = jnp.zeros_like(total_ref)
    upper = upper_band()
    on_slot = slot_lanes()
    lane = lax.broadcasted_iota(i32, (256, 128), 0)
    column = lax.broadcasted_iota(i32, (256, 128), 1)
    slot_column = (lane // 128) * 64 + (lane % 128) // 16

    def step(block, carry):
        window = window_of(block)
        query_two = stack_heads(query_ref[rows_of(block), :])
        grad_two = stack_heads(grad_ref[rows_of(block), :])
        own, merged, far = block_scores(
            block, upper, on_slot, query_two, key_ref, gkey_ref, bias_ref, klocal_ref, kglobal_ref, qfeat_ref
        )
        logs = log_ref[0, pl.ds(block, 1), :]
        own, merged, far = jnp.exp(own - logs), jnp.exp(merged - logs), jnp.exp(far - logs)
        value_sum[window, :] += dot_nn(spread_band(upper, own, merged), grad_two)
        gvalue_sum[...] += dot_nn(far.astype(bf16), grad_two)
        near_dot = dot_nt(value_ref[window, :], grad_two)
        own_dot = near_dot[128:256]
        merged_dot = jnp.where(upper, near_dot[0:128], near_dot[256:384])
        far_dot = dot_nt(gvalue_ref[...], grad_two)
        centre = (
            jnp.sum(own * own_dot, axis=0, keepdims=True)
            + jnp.sum(merged * merged_dot, axis=0, keepdims=True)
            + jnp.sum(far * far_dot, axis=0, keepdims=True)
        )
        own = own * (own_dot - centre)
        merged = merged * (merged_dot - centre)
        far = (far * (far_dot - centre)).astype(bf16)
        near_sum[0:128, :] += own
        near_sum[128:256, :] += merged
        choose = (column == slot_column + block * 8).astype(bf16)
        far_sum[...] += dot_nn(far, choose)
        near_low = spread_band(upper, own, merged)
        key_sum[window, :] += dot_nn(near_low, query_two)
        gkey_sum[...] += dot_nn(far, query_two)
        wide = dot_nn(key_turned[:, window], near_low) + dot_nn(gkey_turned[...], far)
        dquery[rows_of(block), :] = unstack_heads(wide).astype(bf16)
        return carry

    lax.fori_loop(0, rows // 128, step, 0, unroll=4)

    lane_of = lax.broadcasted_iota(i32, (256, 256), 1)
    near = align_offsets(near_sum[...], lane_of & 127, 7, 1)
    near_ref[0] = two_totals(near[:, :128], near[:, 128:])
    lane_of = lax.broadcasted_iota(i32, (slots + 64, 128), 1)
    far = jnp.concatenate([far_sum[...], jnp.zeros((64, 128), f32)], axis=0)
    far = align_offsets(far, lane_of & 63, 6, 1)
    first = lane_of < 64
    far_ref[0] = two_totals(jnp.where(first, far, 0.0), jnp.where(first, 0.0, far))

    grad_low = dquery[...]
    dwq_ref[...] = dot_nn(normed_turned[:, 128 : 128 + rows], grad_low).astype(bf16)
    dnormed_ref[128 : 128 + rows, :] += dot_nt(grad_low, wq_ref[...])
    two = jnp.concatenate([key_sum[...], value_sum[...]], axis=1).astype(bf16)
    gtwo = jnp.concatenate([gkey_sum[...], gvalue_sum[...]], axis=1).astype(bf16)
    w_two = jnp.concatenate([wk_ref[...], wv_ref[...]], axis=1)
    dw_two = (dot_nn(normed_turned[...], two) + dot_nn(pooled_turned[...], gtwo)).astype(bf16)
    dwk_ref[...] = dw_two[:, :128]
    dwv_ref[...] = dw_two[:, 128:]
    dnormed_ref[...] += dot_nt(two, w_two)
    dpooled_ref[...] += dot_nt(gtwo, w_two)


def columns(rows, first):
    return pl.BlockSpec((rows, 128), lambda pair: (0, pair + first))


def of_pair(first, *shape):
    zeros = (0,) * len(shape)
    return pl.BlockSpec((1,) + shape, lambda pair: (pair + first,) + zeros)


def fixed(*shape):
    zeros = (0,) * len(shape)
    return pl.BlockSpec(shape, lambda pair: zeros, pipeline_mode=pl.Buffered(1))


def fixed_out(*shape):
    zeros = (0,) * len(shape)
    return pl.BlockSpec(shape, lambda pair: zeros)


def attention_forward(source_ext, raw_pool, weights, bias, klocal, kglobal, qfeat):
    width = source_ext.shape[1]
    rows = source_ext.shape[0] - 256
    slots = raw_pool.shape[0]
    blocks = rows // 128
    pairs = width // 128
    return pl.pallas_call(
        attend_forward,
        grid=(pairs,),
        in_specs=[
            fixed(rows + 256, width),
            fixed(slots, width),
            pl.BlockSpec((width, 128), lambda pair: (0, 4 * pairs), pipeline_mode=pl.Buffered(1)),
            columns(width, 0),
            columns(width, pairs),
            columns(width, 2 * pairs),
            fixed(256, 128),
            fixed(rows + 256, 128),
            columns(blocks * slots, 0),
            fixed(rows, 128),
        ],
        out_specs=[
            of_pair(0, 256, 256),
            columns(rows, 0),
            of_pair(0, blocks, 256),
            columns(rows, 0),
            columns(rows + 256, 0),
            columns(rows + 256, 0),
            columns(slots, 0),
            columns(slots, 0),
            fixed_out(rows + 256, width),
            fixed_out(slots, width),
            fixed_out(8, width),
        ],
        out_shape=[
            jax.ShapeDtypeStruct((pairs, 256, 256), f32),
            jax.ShapeDtypeStruct((rows, width), bf16),
            jax.ShapeDtypeStruct((pairs, blocks, 256), f32),
            jax.ShapeDtypeStruct((rows, width), bf16),
            jax.ShapeDtypeStruct((rows + 256, width), bf16),
            jax.ShapeDtypeStruct((rows + 256, width), bf16),
            jax.ShapeDtypeStruct((slots, width), bf16),
            jax.ShapeDtypeStruct((slots, width), bf16),
            jax.ShapeDtypeStruct((rows + 256, width), bf16),
            jax.ShapeDtypeStruct((slots, width), bf16),
            jax.ShapeDtypeStruct((8, width), f32),
        ],
        scratch_shapes=[pltpu.VMEM((128, rows + 256), bf16), pltpu.VMEM((128, slots), bf16)],
        compiler_params=pltpu.CompilerParams(vmem_limit_bytes=48 << 20),
        cost_estimate=pl.CostEstimate(
            flops=30 * rows * (384 + slots) * width, bytes_accessed=24 << 20, transcendentals=0
        ),
        name="attend_forward",
    )(source_ext, raw_pool, weights, weights, weights, weights, bias, klocal, kglobal, qfeat)


def attention_backward(
    first, count, queries, grads, keys, values, gkeys, gvalues, normed, pooled, weights, logs, bias, klocal, kglobal, qfeat
):
    rows, width = queries.shape
    slots = gkeys.shape[0]
    blocks = rows // 128
    pairs = width // 128
    return pl.pallas_call(
        attend_backward,
        grid=(count,),
        in_specs=[
            columns(rows, first),
            columns(rows, first),
            columns(rows + 256, first),
            columns(rows + 256, first),
            columns(slots, first),
            columns(slots, first),
            fixed(rows + 256, width),
            fixed(slots, width),
            columns(width, first),
            columns(width, pairs + first),
            columns(width, 2 * pairs + first),
            of_pair(first, blocks, 256),
            of_pair(first, 256, 256),
            fixed(rows + 256, 128),
            columns(blocks * slots, first),
            fixed(rows, 128),
        ],
        out_specs=[
            columns(width, 0),
            columns(width, 0),
            columns(width, 0),
            fixed_out(rows + 256, width),
            fixed_out(slots, width),
            of_pair(0, 256, 128),
            of_pair(0, slots + 64, 128),
        ],
        out_shape=[
            jax.ShapeDtypeStruct((width, count * 128), bf16),
            jax.ShapeDtypeStruct((width, count * 128), bf16),
            jax.ShapeDtypeStruct((width, count * 128), bf16),
            jax.ShapeDtypeStruct((rows + 256, width), f32),
            jax.ShapeDtypeStruct((slots, width), f32),
            jax.ShapeDtypeStruct((count, 256, 128), f32),
            jax.ShapeDtypeStruct((count, slots + 64, 128), f32),
        ],
        scratch_shapes=[
            pltpu.VMEM((128, rows + 256), bf16),
            pltpu.VMEM((128, slots), bf16),
            pltpu.VMEM((rows, 128), bf16),
            pltpu.VMEM((rows + 256, 128), f32),
            pltpu.VMEM((rows + 256, 128), f32),
            pltpu.VMEM((slots, 128), f32),
            pltpu.VMEM((slots, 128), f32),
            pltpu.VMEM((256, 256), f32),
            pltpu.VMEM((slots, 128), f32),
            pltpu.VMEM((width, rows + 256), bf16),
            pltpu.VMEM((width, slots), bf16),
        ],
        compiler_params=pltpu.CompilerParams(vmem_limit_bytes=48 << 20),
        cost_estimate=pl.CostEstimate(
            flops=60 * rows * (384 + slots) * 128 * count, bytes_accessed=count << 22, transcendentals=0
        ),
        name="attend_backward",
    )(
        queries, grads, keys, values, gkeys, gvalues, normed, pooled, weights, weights, weights, logs, bias, klocal,
        kglobal, qfeat,
    )


def feed_forward(
    source_ref, mixture_ref, wo_ref, gains_ref, cot_ref, wg_ref, wu_ref, wd_ref,
    out_ref, middle_grad_ref, dmixture_ref, dwo_ref, dgain_ref, dwg_ref, dwu_ref, dwd_ref,
    middle, normed, turned, out_sum, grad_sum, product, gate_low, lift_low,
):
    rows = source_ref.shape[0]
    part_rows = 256
    parts = rows // part_rows
    gain = gains_ref[2:3, :]

    @pl.when(pl.program_id(0) == 0)
    def start():
        def norm_rows(index, carry):
            part = pl.ds(pl.multiple_of(index * 128, 128), 128)
            values = source_ref[part, :].astype(f32) + dot_nn(mixture_ref[part, :], wo_ref[...])
            middle[part, :] = values
            low = (values * inverse_rms(values) * gain).astype(bf16)
            normed[part, :] = low
            turned[:, part] = low.T
            return carry

        lax.fori_loop(0, rows // 128, norm_rows, 0)
        out_sum[...] = jnp.zeros_like(out_sum)
        grad_sum[...] = jnp.zeros_like(grad_sum)

    root = 0.7978845608028654
    for index in range(parts):
        part = slice(index * part_rows, (index + 1) * part_rows)
        low = normed[part, :]
        gate_pre = dot_nn(low, wg_ref[...])
        lift_pre = dot_nn(low, wu_ref[...])
        grad = dot_nt(cot_ref[part, :], wd_ref[...])
        square = gate_pre * gate_pre
        bent = jnp.tanh(gate_pre * (root + (root * 0.044715) * square))
        half = 0.5 + 0.5 * bent
        gelu = gate_pre * half
        slope = half + gelu * (1.0 - bent) * (root + (3 * root * 0.044715) * square)
        product[part, :] = (gelu * lift_pre).astype(bf16)
        lift_low[part, :] = (grad * gelu).astype(bf16)
        gate_low[part, :] = (grad * lift_pre * slope).astype(bf16)
        out_sum[part, :] += dot_nn(product[part, :], wd_ref[...])
        grad_sum[part, :] += dot_nt(gate_low[part, :], wg_ref[...]) + dot_nt(
            lift_low[part, :], wu_ref[...]
        )
    dwg_ref[...] = dot_nn(turned[...], gate_low[...]).astype(bf16)
    dwu_ref[...] = dot_nn(turned[...], lift_low[...]).astype(bf16)
    dwd_ref[...] = dot_nn(product[...].T, cot_ref[...]).astype(bf16)

    @pl.when(pl.program_id(0) == pl.num_programs(0) - 1)
    def finish():
        dgain_ref[...] = jnp.zeros_like(dgain_ref)

        def back_rows(index, carry):
            part = pl.ds(pl.multiple_of(index * 128, 128), 128)
            values = middle[part, :]
            out_ref[part, :] = (values + out_sum[part, :]).astype(bf16)
            inverse = inverse_rms(values)
            grad = grad_sum[part, :]
            dgain_ref[0:1, :] += jnp.sum(grad * values * inverse, axis=0, keepdims=True)
            total = cot_ref[part, :].astype(f32) + norm_gradient(values, inverse, gain, grad)
            middle_grad_ref[part, :] = total
            low = total.astype(bf16)
            normed[part, :] = low
            dmixture_ref[part, :] = dot_nt(low, wo_ref[...]).astype(bf16)
            turned[:, part] = mixture_ref[part, :].T
            return carry

        lax.fori_loop(0, rows // 128, back_rows, 0)
        dwo_ref[...] = dot_nn(turned[...], normed[...]).astype(bf16)


def feed_forward_both(source, mixture, weights, gains, cotangent, w_gate_up, w_down):
    rows, width = source.shape
    hidden = w_down.shape[0]
    tile = 256
    tiles = hidden // tile
    return pl.pallas_call(
        feed_forward,
        grid=(tiles,),
        in_specs=[
            fixed(rows, width),
            fixed(rows, width),
            pl.BlockSpec((width, width), lambda step: (0, 3), pipeline_mode=pl.Buffered(1)),
            fixed(8, width),
            fixed(rows, width),
            pl.BlockSpec((width, tile), lambda step: (0, step)),
            pl.BlockSpec((width, tile), lambda step: (0, step + tiles)),
            pl.BlockSpec((tile, width), lambda step: (step, 0)),
        ],
        out_specs=[
            fixed_out(rows, width),
            fixed_out(rows, width),
            fixed_out(rows, width),
            fixed_out(width, width),
            fixed_out(8, width),
            pl.BlockSpec((width, tile), lambda step: (0, step)),
            pl.BlockSpec((width, tile), lambda step: (0, step)),
            pl.BlockSpec((tile, width), lambda step: (step, 0)),
        ],
        out_shape=[
            jax.ShapeDtypeStruct((rows, width), bf16),
            jax.ShapeDtypeStruct((rows, width), f32),
            jax.ShapeDtypeStruct((rows, width), bf16),
            jax.ShapeDtypeStruct((width, width), bf16),
            jax.ShapeDtypeStruct((8, width), f32),
            jax.ShapeDtypeStruct((width, hidden), bf16),
            jax.ShapeDtypeStruct((width, hidden), bf16),
            jax.ShapeDtypeStruct((hidden, width), bf16),
        ],
        scratch_shapes=[
            pltpu.VMEM((rows, width), f32),
            pltpu.VMEM((rows, width), bf16),
            pltpu.VMEM((width, rows), bf16),
            pltpu.VMEM((rows, width), f32),
            pltpu.VMEM((rows, width), f32),
            pltpu.VMEM((rows, tile), bf16),
            pltpu.VMEM((rows, tile), bf16),
            pltpu.VMEM((rows, tile), bf16),
        ],
        compiler_params=pltpu.CompilerParams(vmem_limit_bytes=56 << 20),
        cost_estimate=pl.CostEstimate(
            flops=20 * rows * width * hidden, bytes_accessed=40 << 20, transcendentals=0
        ),
        name="feed_forward",
    )(source, mixture, weights, gains, cotangent, w_gate_up, w_gate_up, w_down)


def near_offsets(local_bias):
    heads, buckets = local_bias.shape
    offset = (jnp.arange(256, dtype=i32) + 128) % 256 - 128
    table = (bucket_of(offset)[:, None] == jnp.arange(buckets, dtype=i32)).astype(f32)
    chosen = jnp.einsum("ob,hb->oh", table, local_bias, precision=highest)
    chosen = jnp.where((offset == -128)[:, None], never, chosen)
    return jnp.pad(chosen, ((0, 0), (0, 128 - heads)))


def far_features(global_bias, slot_segments, slot_live, first_slot, blocks):
    heads, buckets = global_bias.shape
    pairs = heads // 2
    slots = slot_segments.shape[0]
    wide = 8 * buckets + 8
    shape = (blocks * slots, wide)
    row = lax.broadcasted_iota(i32, shape, 0)
    column = lax.broadcasted_iota(i32, shape, 1)
    slot = row % slots
    query_slot = first_slot + (row // slots) * 8 + column // buckets
    code = jnp.tile(jnp.where(slot_live, slot_segments, 3), blocks)[:, None]
    picks = jnp.where(
        column < 8 * buckets,
        bucket_of(slot - query_slot) == column % buckets,
        code == column - 8 * buckets,
    ).astype(bf16)
    high = lax.reduce_precision(global_bias, 8, 7)
    middle = lax.reduce_precision(global_bias - high, 8, 7)
    lowest = lax.reduce_precision(global_bias - high - middle, 8, 7)
    parts = jnp.stack([high, middle, lowest]).reshape(3, pairs, 2, buckets)
    parts = parts.transpose(3, 1, 0, 2)
    same = jnp.eye(8, dtype=f32)[:, None, None, None, None, :]
    table = (parts[None, :, :, :, :, None] * same).reshape(8 * buckets, pairs, 48)
    table = jnp.pad(table, ((0, 8), (0, 0), (0, 80)))
    shape = (wide, 1, 128)
    lane = lax.broadcasted_iota(i32, shape, 2) - 48
    code_row = lax.broadcasted_iota(i32, shape, 0) - 8 * buckets
    barred = (code_row >= 0) & (lane >= 0) & (lane < 3) & (lane != code_row)
    table = jnp.where(barred, never, table).astype(bf16).reshape(wide, pairs * 128)
    return jnp.dot(picks, table, preferred_element_type=f32).astype(bf16)


def near_features(segments_ext, valid_ext):
    lane = lax.broadcasted_iota(i32, (segments_ext.shape[0], 128), 1)
    allowed = (segments_ext[:, None] == lane - 48) & (valid_ext[:, None] > 0)
    return jnp.where((lane >= 48) & (lane < 51) & ~allowed, never, 0.0).astype(bf16)


def query_features(own_segments):
    lane = lax.broadcasted_iota(i32, (own_segments.shape[0], 128), 1)
    return (own_segments[:, None] == lane - 48).astype(bf16)


def bucket_totals(near_sums, far_sums, first_slot, buckets):
    heads = near_sums.shape[0] * 2
    ids = jnp.arange(buckets, dtype=i32)
    span = near_sums.shape[1]
    offset = (jnp.arange(span, dtype=i32) + 128) % span - 128
    table = (bucket_of(offset)[:, None] == ids).astype(f32)
    near = jnp.einsum("poa,ob->pab", near_sums[:, :, :2], table, precision=highest)
    span = far_sums.shape[1]
    place = jnp.arange(span, dtype=i32)
    offset = jnp.where(place < span - 64, place, place - span) - first_slot
    table = (bucket_of(offset)[:, None] == ids).astype(f32)
    far = jnp.einsum("poa,ob->pab", far_sums[:, :, :2], table, precision=highest)
    return near.reshape(heads, buckets), far.reshape(heads, buckets)


def pick(values, index, dim):
    return lax.dynamic_index_in_dim(values, index, dim, keepdims=False)


def ring(size, hop):
    return [(i, (i + hop) % size) for i in range(size)]


def split_stage(values, axis, dim):
    size, me = lax.axis_size(axis), lax.axis_index(axis)
    keep = pick(values, me, dim)
    return keep, [pick(values, (me + hop) % size, dim) for hop in range(1, size)]


def send_all(axis, pieces):
    size = lax.axis_size(axis)
    return [lax.ppermute(piece, axis, ring(size, hop + 1)) for hop, piece in enumerate(pieces)]


def join_stage(keep, pieces):
    total = keep.astype(f32)
    for piece in pieces:
        total = total + piece.astype(f32)
    return total


def place_stage(values, pieces, axis, dim):
    size, me = lax.axis_size(axis), lax.axis_index(axis)
    shape = values.shape[:dim] + (size,) + values.shape[dim:]
    out = lax.dynamic_update_index_in_dim(jnp.zeros(shape, values.dtype), values, me, dim)
    for hop, piece in enumerate(pieces):
        out = lax.dynamic_update_index_in_dim(out, piece, (me - hop - 1) % size, dim)
    return out


def half_of(width):
    return (width // 256) * 128


def sum_rows(grads):
    y, x, z, core = (lax.axis_size(axis) for axis in everyone)
    width = grads.shape[1]
    half = half_of(width)
    values = grads.reshape(y, x, z, core, -1, width)
    sends = yield split_stage(values, "core", 3)
    held = yield sends[0], send_all("core", sends[1])
    values = join_stage(*held).astype(bf16)
    left, right = values[..., :half], values[..., half:]
    for left_axis, right_axis in (("x", "y"), ("y", "x")):
        dim = 1 if left_axis == "x" else 0
        sends = yield split_stage(left, left_axis, dim), split_stage(right, right_axis, 0)
        (keep_left, send_left), (keep_right, send_right) = sends
        held = yield (
            (keep_left, send_all(left_axis, send_left)),
            (keep_right, send_all(right_axis, send_right)),
        )
        left, right = (join_stage(*part).astype(bf16) for part in held)
    sends = yield split_stage(jnp.concatenate([left, right], axis=-1), "z", 0)
    held = yield sends[0], send_all("z", sends[1])
    return join_stage(*held)


def all_rows(shard):
    width = shard.shape[1]
    half = half_of(width)
    others = lax.axis_size("z") - 1
    shard = yield shard
    held = yield shard, send_all("z", [shard] * others)
    values = place_stage(*held, "z", 0)
    left, right = values[..., :half], values[..., half:]
    for left_axis, right_axis in (("x", "y"), ("y", "x")):
        dim = 1 if right_axis == "x" else 0
        left, right = yield left, right
        held = yield (
            (left, send_all(left_axis, [left] * (lax.axis_size(left_axis) - 1))),
            (right, send_all(right_axis, [right] * (lax.axis_size(right_axis) - 1))),
        )
        left, right = place_stage(*held[0], left_axis, 0), place_stage(*held[1], right_axis, dim)
    values = yield jnp.concatenate([left, right], axis=-1)
    held = yield values, send_all("core", [values])
    return place_stage(*held, "core", 3).reshape(-1, width)


class Chain:
    def __init__(self, steps):
        self.steps = steps
        self.value = next(steps)
        self.done = False

    def advance(self):
        try:
            self.value = self.steps.send(self.value)
        except StopIteration as end:
            self.value, self.done = end.value, True


def phase(chains, operand, work):
    chains = [chain for chain in chains if not chain.done]
    values, operand = lax.optimization_barrier(([chain.value for chain in chains], operand))
    for chain, value in zip(chains, values):
        chain.value = value
        chain.advance()
    result = work(operand)
    values, result = lax.optimization_barrier(([chain.value for chain in chains], result))
    for chain, value in zip(chains, values):
        chain.value = value
        chain.advance()
    return result


def neighbour_rows(to_after, to_before):
    count = lax.axis_size(seq)
    ends = count - 1
    before = lax.ppermute(to_after, seq, [(i, i + 1) for i in range(ends)])
    after = lax.ppermute(to_before, seq, [(i + 1, i) for i in range(ends)])
    return before, after


def on_device(
    hidden_state,
    segment_ids,
    valid_mask,
    cotangent,
    norm_gain,
    pool_gain,
    feed_gain,
    query_weight,
    key_weight,
    value_weight,
    output_weight,
    local_bias,
    global_bias,
    gate_weight,
    up_weight,
    down_weight,
):
    model_width = hidden_state.shape[2]
    hidden = gate_weight.shape[1]
    tok_rows = hidden_state.shape[1]
    own_part = norm_gain.shape[0]
    buckets = local_bias.shape[1]
    pairs = local_bias.shape[0] // 2
    blocks = tok_rows // 128
    own_slots = tok_rows // 16
    seq_count = lax.axis_size(seq)
    slot_count = own_slots * seq_count
    row_start = lax.axis_index(seq) * tok_rows
    first_slot = row_start // 16
    source = hidden_state[0]
    upstream = cotangent[0]
    own_segments = segment_ids[0]
    valid_float = valid_mask[0].astype(f32)

    gain_columns = jnp.pad(jnp.stack([norm_gain, pool_gain, feed_gain], axis=1), ((0, 0), (0, 125)))
    first = Chain(
        all_rows(
            jnp.concatenate(
                [query_weight, key_weight, value_weight, output_weight, gain_columns], axis=1
            )
        )
    )
    second = Chain(all_rows(down_weight))
    values = source.astype(f32)
    inverse = inverse_rms(values)

    def share(operands):
        values, gate_weight, up_weight = operands
        w_gate_up = lax.all_gather(
            jnp.concatenate([gate_weight, up_weight], axis=1), everyone, axis=0, tiled=True
        )
        before, after = neighbour_rows(source[-128:], source[:128])
        own_raw = jnp.sum(
            (values * (inverse * valid_float[:, None])).reshape(own_slots, 16, model_width), axis=1
        )
        marks = jnp.stack([own_segments, valid_mask[0]]).astype(bf16).reshape(-1)
        mark_rows = -(-marks.size // model_width)
        pad_rows = -(-mark_rows // 16) * 16
        marks = jnp.pad(marks, (0, pad_rows * model_width - marks.size))
        shared = lax.all_gather(
            jnp.concatenate([own_raw.astype(bf16), marks.reshape(pad_rows, model_width)], axis=0),
            seq, axis=0, tiled=False,
        )
        return own_raw, shared, before, after, w_gate_up

    own_raw, shared, before, after, w_gate_up = share((values, gate_weight, up_weight))
    shared = phase([first], shared, lambda shared: shared)

    def near_parts(operands):
        shared, local_bias = operands
        raw_pool = shared[:, :own_slots].reshape(slot_count, model_width)
        all_marks = shared[:, own_slots:].reshape(seq_count, -1)[:, : 2 * tok_rows].astype(i32)
        all_marks = all_marks.reshape(seq_count, 2, tok_rows)
        all_segments, all_valid = all_marks[:, 0].reshape(-1), all_marks[:, 1].reshape(-1)
        slot_segments = all_segments.reshape(slot_count, 16)[:, 0]
        slot_live = jnp.sum(all_valid.reshape(slot_count, 16), axis=1) > 0
        segments_ext = lax.dynamic_slice_in_dim(
            jnp.pad(all_segments, 128, constant_values=-1), row_start, tok_rows + 256
        )
        valid_ext = lax.dynamic_slice_in_dim(jnp.pad(all_valid, 128), row_start, tok_rows + 256)
        feat_near = near_features(segments_ext, valid_ext)
        source_ext = jnp.concatenate([before, source, after], axis=0)
        return raw_pool, slot_segments, slot_live, feat_near, near_offsets(local_bias), source_ext

    raw_pool, slot_segments, slot_live, feat_near, bias_near, source_ext = phase(
        [first, second], (shared, local_bias), near_parts
    )
    feat_query = query_features(own_segments)
    feat_far = phase(
        [first, second],
        (global_bias, slot_segments, slot_live),
        lambda operands: far_features(*operands, first_slot, blocks),
    )
    phase([first], (), lambda nothing: nothing)
    weights = first.value

    bias, mixture, logs, queries, keys, vals, gkeys, gvals, normed, pooled, gains = phase(
        [second],
        (source_ext, raw_pool, weights, bias_near, feat_near, feat_far, feat_query),
        lambda operands: attention_forward(*operands),
    )
    phase([second], (), lambda nothing: nothing)
    w_down = second.value
    layer_output, middle_grad, mixture_grad, d_output, d_feed, d_gate, d_up, d_down = feed_forward_both(
        source, mixture, weights, gains, upstream, w_gate_up, w_down
    )
    chains = [
        Chain(sum_rows(jnp.concatenate([d_gate, d_up, d_output], axis=1))),
        Chain(sum_rows(d_down)),
    ]
    calls = 3 if pairs % 3 == 0 else 1
    count = pairs // calls
    near_sums, far_sums = [], []
    normed_grad, pooled_grad = 0.0, 0.0
    for call in range(calls):
        dwq, dwk, dwv, dnormed, dpooled, near, far = phase(
            chains,
            mixture_grad,
            lambda grad: attention_backward(
                call * count, count, queries, grad, keys, vals, gkeys, gvals, normed, pooled, weights, logs,
                bias, feat_near, feat_far, feat_query,
            ),
        )
        chains.append(Chain(sum_rows(jnp.concatenate([dwq, dwk, dwv], axis=1))))
        near_sums.append(near)
        far_sums.append(far)
        normed_grad = normed_grad + dnormed
        pooled_grad = pooled_grad + dpooled

    def return_grads(operands):
        normed_grad, pooled_grad = operands
        spread = lax.all_to_all(
            pooled_grad.astype(bf16).reshape(seq_count, own_slots, model_width), seq, 0, 0, tiled=True
        )
        to_head, to_tail = neighbour_rows(
            normed_grad[-128:].astype(bf16), normed_grad[:128].astype(bf16)
        )
        return normed_grad, spread, to_head, to_tail

    normed_grad, spread, to_head, to_tail = phase(chains, (normed_grad, pooled_grad), return_grads)
    pooled_grad = jnp.sum(spread.astype(f32), axis=0)
    edges = jnp.concatenate(
        [to_head.astype(f32), jnp.zeros((tok_rows - 256, model_width), f32), to_tail.astype(f32)]
    )
    gain_one, gain_pool = gains[0:1], gains[1:2]

    def finish(operands):
        normed_grad, pooled_grad, edges = operands
        pooled_raw = own_raw * gain_one
        pool_inverse = inverse_rms(pooled_raw)
        pool_delta = jnp.sum(pooled_grad * pooled_raw * pool_inverse, axis=0)
        pooled_raw_grad = norm_gradient(pooled_raw, pool_inverse, gain_pool, pooled_grad)
        spread_grad = jnp.broadcast_to(
            pooled_raw_grad[:, None, :], (own_slots, 16, model_width)
        ).reshape(tok_rows, model_width)
        normed_grad = normed_grad[128:-128] + edges + spread_grad * valid_float[:, None]
        norm_delta = jnp.sum(normed_grad * values * inverse, axis=0)
        input_delta = middle_grad + norm_gradient(values, inverse, gain_one, normed_grad)
        local_delta, global_delta = bucket_totals(
            jnp.concatenate(near_sums), jnp.concatenate(far_sums), first_slot, buckets
        )
        small = jnp.concatenate(
            [norm_delta, pool_delta, d_feed[0], local_delta.reshape(-1), global_delta.reshape(-1)]
        ).reshape(1, -1)
        return input_delta, small

    input_delta, small = phase(chains, (normed_grad, pooled_grad, edges), finish)
    small = phase(
        chains,
        small,
        lambda small: jnp.sum(lax.all_gather(small, batch, axis=0, tiled=True), axis=0, keepdims=True),
    )
    small = phase(
        chains,
        small,
        lambda small: jnp.sum(lax.all_gather(small, seq, axis=0, tiled=True), axis=0),
    )
    rest_delta, down_delta = chains[0].value, chains[1].value
    size = count * 128
    query_deltas = [chain.value[:, :size] for chain in chains[2:]]
    key_deltas = [chain.value[:, size : 2 * size] for chain in chains[2:]]
    value_deltas = [chain.value[:, 2 * size :] for chain in chains[2:]]
    place = lax.axis_index(everyone) * own_part
    gain_deltas = [
        lax.dynamic_slice_in_dim(small[i * model_width : (i + 1) * model_width], place, own_part)
        for i in range(3)
    ]
    bias_size = local_bias.size
    local_total = small[3 * model_width : 3 * model_width + bias_size].reshape(local_bias.shape)
    global_total = small[3 * model_width + bias_size :].reshape(local_bias.shape)
    return (
        layer_output[None],
        input_delta[None],
        gain_deltas[0],
        gain_deltas[1],
        gain_deltas[2],
        jnp.concatenate(query_deltas, axis=1),
        jnp.concatenate(key_deltas, axis=1),
        jnp.concatenate(value_deltas, axis=1),
        rest_delta[:, 2 * hidden :],
        local_total,
        global_total,
        rest_delta[:, :hidden],
        rest_delta[:, hidden : 2 * hidden],
        down_delta,
    )


def solution(mesh):
    seq_size, batch_size = mesh.shape["seq"], mesh.shape["batch"]
    chips = Mesh(mesh.devices.reshape(2, seq_size // 2, batch_size // 2, 2), everyone)
    tokens = P(batch, seq, None)
    marks = P(batch, seq)
    row = P(everyone)
    matrix = P(everyone, None)
    whole = P()
    return jax.shard_map(
        on_device,
        mesh=chips,
        in_specs=(tokens, marks, marks, tokens, row, row, row)
        + (matrix,) * 4
        + (whole,) * 2
        + (matrix,) * 3,
        out_specs=(tokens, tokens, row, row, row)
        + (matrix,) * 4
        + (whole,) * 2
        + (matrix,) * 3,
        check_vma=False,
    )
```

```python
import functools

import jax
import jax.numpy as jnp
from jax import lax
from jax.experimental import pallas as pl
from jax.experimental.pallas import tpu as pltpu
from jax.sharding import Mesh
from jax.sharding import PartitionSpec as P

epsilon = 1e-06
boundaries = (12, 16, 23, 32, 46, 64, 91)
never = -1e30
seq = ("y", "x")
batch = ("z", "core")
everyone = seq + batch
bf16 = jnp.bfloat16
f32 = jnp.float32
i32 = jnp.int32
highest = lax.Precision.HIGHEST
calls = 3


def bucket_of(offset):
    distance = jnp.abs(offset)
    far_part = 8 + sum(((distance >= boundary).astype(i32) for boundary in boundaries))
    return 16 * (offset > 0).astype(i32) + jnp.where(distance < 8, distance, far_part)


def dot_nt(left, right):
    return lax.dot_general(left, right, (((1,), (1,)), ((), ())), preferred_element_type=f32)


def dot_nn(left, right):
    return lax.dot_general(left, right, (((1,), (0,)), ((), ())), preferred_element_type=f32)


def inverse_rms(values):
    return lax.rsqrt(jnp.mean(values * values, axis=-1, keepdims=True) + epsilon)


def norm_gradient(values, inverse, gain, grad):
    weighted = grad * gain
    mean = jnp.mean(weighted * values, axis=-1, keepdims=True)
    return inverse * weighted - (inverse * inverse * inverse * mean) * values


def store_halves(keep_ref, send_ref, index, value, core, part):
    rows, width = value.shape
    value = value.reshape(rows // (2 * part), 2, part, width)
    first, second = value[:, 0].reshape(rows // 2, width), value[:, 1].reshape(rows // 2, width)
    keep_ref[index] = jnp.where(core == 0, first, second).astype(bf16)
    send_ref[index] = jnp.where(core == 0, second, first).astype(bf16)


def stack_heads(rows):
    lane = lax.broadcasted_iota(i32, rows.shape, 1)
    zero = jnp.zeros_like(rows)
    return jnp.concatenate(
        [jnp.where(lane < 64, rows, zero), jnp.where(lane < 64, zero, rows)], axis=0
    )


def unstack_heads(wide):
    row = lax.broadcasted_iota(i32, (128, 128), 0)
    return jnp.where(row < 64, wide[:, :128], wide[:, 128:]).T


def upper_band():
    key = lax.broadcasted_iota(i32, (128, 256), 0)
    query = lax.broadcasted_iota(i32, (128, 256), 1) & 127
    return key > query


def spread_band(upper, own, merged):
    zero = jnp.zeros_like(merged)
    return jnp.concatenate(
        [jnp.where(upper, merged, zero), own, jnp.where(upper, zero, merged)], axis=0
    ).astype(bf16)


def window_of(block):
    return pl.ds(pl.multiple_of(block * 128, 128), 384)


def rows_of(block):
    return pl.ds(pl.multiple_of(block * 128, 128), 128)


def slot_lanes():
    row = lax.broadcasted_iota(i32, (256, 128), 0)
    lane = lax.broadcasted_iota(i32, (256, 128), 1)
    hit = (lane < 48) & ((lane & 15) == (row // 128) * 8 + (row % 128) // 16)
    return hit.astype(f32).astype(bf16)


def block_scores(block, upper, on_slot, query_two, key_ref, gkey_ref, bias_ref, klocal_ref, kglobal_ref, qfeat_ref):
    slots = gkey_ref.shape[0]
    window = window_of(block)
    segment_lanes = qfeat_ref[rows_of(block), :]
    features = jnp.concatenate([segment_lanes, segment_lanes], axis=0) + on_slot
    query_wide = jnp.concatenate([query_two, features], axis=1)
    key_wide = jnp.concatenate([key_ref[window, :], klocal_ref[window, :]], axis=1)
    local = dot_nt(key_wide, query_wide)
    own = local[128:256] + bias_ref[0, 0:128]
    merged = jnp.where(upper, local[0:128], local[256:384]) + bias_ref[0, 128:256]
    far_rows = pl.ds(pl.multiple_of(block * slots, 128), slots)
    gkey_wide = jnp.concatenate([gkey_ref[...], kglobal_ref[far_rows, :]], axis=1)
    return own, merged, dot_nt(gkey_wide, query_wide)


def attend_forward(
    source_ref, raw_ref, gain_ref, wq_ref, wk_ref, wv_ref, offsets_ref, klocal_ref, kglobal_ref, qfeat_ref,
    bias_ref, out_ref, log_ref, query_ref, key_ref, value_ref, gkey_ref, gvalue_ref, normed_ref, gains_ref,
    normed_turned, pooled_turned, pooled_ref, value_turned, gvalue_turned,
):
    rows = query_ref.shape[0]
    slots = gkey_ref.shape[0]

    @pl.when(pl.program_id(0) == 0)
    def start():
        turned = gain_ref[...].astype(f32).T
        gains_ref[...] = turned[0:8]
        gain_one, gain_pool = turned[0:1], turned[1:2]

        def norm_rows(index, carry):
            part = pl.ds(pl.multiple_of(index * 128, 128), 128)
            values = source_ref[part, :].astype(f32)
            low = (values * inverse_rms(values) * gain_one).astype(bf16)
            normed_ref[part, :] = low
            normed_turned[:, part] = low.T
            return carry

        lax.fori_loop(0, (rows + 256) // 128, norm_rows, 0)

        def pool_rows(index, carry):
            part = pl.ds(pl.multiple_of(index * 128, 128), 128)
            values = raw_ref[part, :].astype(f32) * gain_one
            low = (values * inverse_rms(values) * gain_pool).astype(bf16)
            pooled_ref[part, :] = low
            pooled_turned[:, part] = low.T
            return carry

        lax.fori_loop(0, slots // 128, pool_rows, 0)

    lane = lax.broadcasted_iota(i32, (256, 128), 1)
    spread = []
    for head in range(2):
        mine = jnp.where(lane == 2 * pl.program_id(0) + head, offsets_ref[...], 0.0)
        spread.append(jnp.broadcast_to(jnp.sum(mine, axis=1, keepdims=True), (256, 128)))
    lane_of = lax.broadcasted_iota(i32, (256, 256), 1)
    bias_ref[0] = align_offsets(jnp.concatenate(spread, axis=1), lane_of & 127, 7, -1)

    query_ref[...] = dot_nn(normed_ref[128 : 128 + rows, :], wq_ref[...]).astype(bf16)
    w_two = jnp.concatenate([wk_ref[...], wv_ref[...]], axis=1)
    two = dot_nn(normed_ref[...], w_two).astype(bf16)
    key_ref[...] = two[:, :128]
    value_ref[...] = two[:, 128:]
    value_turned[...] = two[:, 128:].T
    two = dot_nn(pooled_ref[...], w_two).astype(bf16)
    gkey_ref[...] = two[:, :128]
    gvalue_ref[...] = two[:, 128:]
    gvalue_turned[...] = two[:, 128:].T
    upper = upper_band()
    on_slot = slot_lanes()

    def step(block, carry):
        window = window_of(block)
        query_two = stack_heads(query_ref[rows_of(block), :])
        own, merged, far = block_scores(
            block, upper, on_slot, query_two, key_ref, gkey_ref, bias_ref, klocal_ref, kglobal_ref, qfeat_ref
        )
        peak = jnp.maximum(
            jnp.maximum(
                jnp.max(own, axis=0, keepdims=True), jnp.max(merged, axis=0, keepdims=True)
            ),
            jnp.max(far, axis=0, keepdims=True),
        )
        own, merged, far = jnp.exp(own - peak), jnp.exp(merged - peak), jnp.exp(far - peak)
        total = (
            jnp.sum(own, axis=0, keepdims=True)
            + jnp.sum(merged, axis=0, keepdims=True)
            + jnp.sum(far, axis=0, keepdims=True)
        )
        near_low = spread_band(upper, own, merged)
        wide = dot_nn(value_turned[:, window], near_low) + dot_nn(
            gvalue_turned[...], far.astype(bf16)
        )
        out_ref[rows_of(block), :] = unstack_heads(wide * (1.0 / total)).astype(bf16)
        log_ref[0, pl.ds(block, 1), :] = peak + jnp.log(total)
        return carry

    lax.fori_loop(0, rows // 128, step, 0, unroll=4)


def align_offsets(sums, step_of_lane, bits, sign):
    for bit in range(bits):
        shift = sign * (1 << bit)
        moved = jnp.concatenate([sums[shift:], sums[:shift]], axis=0)
        sums = jnp.where((step_of_lane >> bit) & 1 == 1, moved, sums)
    return sums


def two_totals(left, right):
    lane = lax.broadcasted_iota(i32, (left.shape[0], 128), 1)
    first = jnp.sum(left, axis=1, keepdims=True)
    second = jnp.sum(right, axis=1, keepdims=True)
    return jnp.where(lane == 0, first, jnp.where(lane == 1, second, 0.0))


def add_buckets(table_ref, sums, offset, head):
    hit = (bucket_of(offset) == lax.broadcasted_iota(i32, sums.shape, 1)).astype(f32)
    totals = lax.dot_general(
        sums, hit, (((0,), (0,)), ((), ())), precision=highest, preferred_element_type=f32
    )
    row = lax.broadcasted_iota(i32, table_ref.shape, 0)
    table_ref[...] += jnp.where(
        row == head, totals[0:1], jnp.where(row == head + 1, totals[1:2], 0.0)
    )


def attend_backward(
    last, part, own_part, first_pair, query_ref, grad_ref, key_ref, value_ref, gkey_ref, gvalue_ref, normed_ref, normed_turned, pooled_turned, wq_ref, wk_ref, wv_ref,
    log_ref, bias_ref, klocal_ref, kglobal_ref, qfeat_ref, raw_ref, gains_ref, place_ref, old_small_ref, old_table_ref,
    keep_ref, send_ref, dnormed_ref, draw_ref, small_ref, table_ref,
    dnormed_sum, dpooled_sum, key_turned, gkey_turned, dquery, key_sum, value_sum, gkey_sum, gvalue_sum, near_sum, far_sum,
):
    rows = query_ref.shape[0]
    slots = gkey_ref.shape[0]

    @pl.when(pl.program_id(0) == 0)
    def start():
        dnormed_sum[...] = jnp.zeros_like(dnormed_sum)
        dpooled_sum[...] = jnp.zeros_like(dpooled_sum)
        table_ref[...] = old_table_ref[...]

    key_turned[...] = key_ref[...].T
    gkey_turned[...] = gkey_ref[...].T
    for total_ref in (key_sum, value_sum, gkey_sum, gvalue_sum, near_sum, far_sum):
        total_ref[...] = jnp.zeros_like(total_ref)
    upper = upper_band()
    on_slot = slot_lanes()
    lane = lax.broadcasted_iota(i32, (256, 128), 0)
    column = lax.broadcasted_iota(i32, (256, 128), 1)
    slot_column = (lane // 128) * 64 + (lane % 128) // 16

    def step(block, carry):
        window = window_of(block)
        query_two = stack_heads(query_ref[rows_of(block), :])
        grad_two = stack_heads(grad_ref[rows_of(block), :])
        own, merged, far = block_scores(
            block, upper, on_slot, query_two, key_ref, gkey_ref, bias_ref, klocal_ref, kglobal_ref, qfeat_ref
        )
        logs = log_ref[0, pl.ds(block, 1), :]
        own, merged, far = jnp.exp(own - logs), jnp.exp(merged - logs), jnp.exp(far - logs)
        value_sum[window, :] += dot_nn(spread_band(upper, own, merged), grad_two)
        gvalue_sum[...] += dot_nn(far.astype(bf16), grad_two)
        near_dot = dot_nt(value_ref[window, :], grad_two)
        own_dot = near_dot[128:256]
        merged_dot = jnp.where(upper, near_dot[0:128], near_dot[256:384])
        far_dot = dot_nt(gvalue_ref[...], grad_two)
        centre = (
            jnp.sum(own * own_dot, axis=0, keepdims=True)
            + jnp.sum(merged * merged_dot, axis=0, keepdims=True)
            + jnp.sum(far * far_dot, axis=0, keepdims=True)
        )
        own = own * (own_dot - centre)
        merged = merged * (merged_dot - centre)
        far = (far * (far_dot - centre)).astype(bf16)
        near_sum[0:128, :] += own
        near_sum[128:256, :] += merged
        choose = (column == slot_column + block * 8).astype(bf16)
        far_sum[...] += dot_nn(far, choose)
        near_low = spread_band(upper, own, merged)
        key_sum[window, :] += dot_nn(near_low, query_two)
        gkey_sum[...] += dot_nn(far, query_two)
        wide = dot_nn(key_turned[:, window], near_low) + dot_nn(gkey_turned[...], far)
        dquery[rows_of(block), :] = unstack_heads(wide).astype(bf16)
        return carry

    lax.fori_loop(0, rows // 128, step, 0, unroll=4)

    core, first_slot = place_ref[0], place_ref[1]
    head = 2 * (first_pair + pl.program_id(0))
    lane_of = lax.broadcasted_iota(i32, (256, 256), 1)
    near = align_offsets(near_sum[...], lane_of & 127, 7, 1)
    near = two_totals(near[:, :128], near[:, 128:])
    place = lax.broadcasted_iota(i32, (256, 128), 0)
    add_buckets(table_ref, near, ((place + 128) & 255) - 128, head)
    lane_of = lax.broadcasted_iota(i32, (slots + 64, 128), 1)
    far = jnp.concatenate([far_sum[...], jnp.zeros((64, 128), f32)], axis=0)
    far = align_offsets(far, lane_of & 63, 6, 1)
    far = two_totals(jnp.where(lane_of < 64, far, 0.0), jnp.where(lane_of < 64, 0.0, far))
    place = lax.broadcasted_iota(i32, (slots + 64, 128), 0)
    heads = normed_ref.shape[1] // 64
    add_buckets(table_ref, far, jnp.where(place < slots, place, place - slots - 64) - first_slot, heads + head)

    width = normed_ref.shape[1]
    grad_low = dquery[...]
    dwq = dot_nn(normed_turned[:, 128 : 128 + rows], grad_low)
    planes = 4 if last else 3
    lead = pl.program_id(0) * planes
    store_halves(keep_ref, send_ref, lead, dwq, core, part)
    dnormed_sum[128 : 128 + rows, :] += dot_nt(grad_low, wq_ref[...])
    two = jnp.concatenate([key_sum[...], value_sum[...]], axis=1).astype(bf16)
    gtwo = jnp.concatenate([gkey_sum[...], gvalue_sum[...]], axis=1).astype(bf16)
    w_two = jnp.concatenate([wk_ref[...], wv_ref[...]], axis=1)
    dw_two = dot_nn(normed_turned[...], two) + dot_nn(pooled_turned[...], gtwo)
    store_halves(keep_ref, send_ref, lead + 1, dw_two[:, :128], core, part)
    store_halves(keep_ref, send_ref, lead + 2, dw_two[:, 128:], core, part)
    dnormed_sum[...] += dot_nt(two, w_two)
    dpooled_sum[...] += dot_nt(gtwo, w_two)

    @pl.when(pl.program_id(0) == pl.num_programs(0) - 1)
    def finish():
        gain_one, gain_pool = gains_ref[0:1, :], gains_ref[1:2, :]
        small_ref[...] = old_small_ref[...]

        def norm_rows(index, carry):
            part = pl.ds(pl.multiple_of(index * 128, 128), 128)
            grad = dnormed_sum[part, :]
            dnormed_ref[part, :] = grad.astype(bf16)
            return carry + jnp.sum(grad * normed_ref[part, :].astype(f32), axis=0, keepdims=True)

        norm_part = lax.fori_loop(0, (rows + 256) // 128, norm_rows, jnp.zeros((1, width), f32))
        norm_part = norm_part / gain_one

        def pool_rows(index, carry):
            norm_part, pool_part = carry
            part = pl.ds(pl.multiple_of(index * 128, 128), 128)
            raw = raw_ref[part, :].astype(f32)
            values = raw * gain_one
            inverse = inverse_rms(values)
            grad = dpooled_sum[part, :]
            back = norm_gradient(values, inverse, gain_pool, grad)
            draw_ref[part, :] = back.astype(bf16)
            return (
                norm_part + jnp.sum(back * raw, axis=0, keepdims=True),
                pool_part + jnp.sum(grad * values * inverse, axis=0, keepdims=True),
            )

        norm_part, pool_part = lax.fori_loop(
            0, slots // 128, pool_rows, (norm_part, jnp.zeros((1, width), f32))
        )
        small_ref[0:1, :] += norm_part
        small_ref[1:2, :] += pool_part
        if not last:
            return
        rows_of_small = jnp.concatenate([small_ref[...], jnp.zeros((120, width), f32)], axis=0)
        tables = jnp.zeros((width, 128), f32)
        row = lax.broadcasted_iota(i32, (width, 32), 0)
        column = lax.broadcasted_iota(i32, (width, 32), 1)
        for block in range(-(-2 * heads // own_part)):
            chosen = (column == row % own_part + block * own_part).astype(f32)
            shifted = table_ref[...]
            if block:
                shifted = jnp.concatenate(
                    [shifted[:, 128 - 32 * block :], shifted[:, : 128 - 32 * block]], axis=1
                )
            tables = tables + jnp.dot(
                chosen, shifted, precision=highest, preferred_element_type=f32
            )
        store_halves(keep_ref, send_ref, 3, rows_of_small.T, core, part)
        store_halves(keep_ref, send_ref, keep_ref.shape[0] - 1, tables, core, part)


def columns(rows, first):
    return pl.BlockSpec((rows, 128), lambda pair: (0, pair + first))


def of_pair(first, *shape):
    zeros = (0,) * len(shape)
    return pl.BlockSpec((1,) + shape, lambda pair: (pair + first,) + zeros)


def fixed(*shape):
    zeros = (0,) * len(shape)
    return pl.BlockSpec(shape, lambda pair: zeros, pipeline_mode=pl.Buffered(1))


def fixed_out(*shape):
    zeros = (0,) * len(shape)
    return pl.BlockSpec(shape, lambda pair: zeros)


def attention_forward(source_ext, raw_pool, weights, bias, klocal, kglobal, qfeat):
    width = source_ext.shape[1]
    rows = source_ext.shape[0] - 256
    slots = raw_pool.shape[0]
    blocks = rows // 128
    pairs = width // 128
    return pl.pallas_call(
        attend_forward,
        grid=(pairs,),
        in_specs=[
            fixed(rows + 256, width),
            fixed(slots, width),
            pl.BlockSpec((width, 128), lambda pair: (0, 4 * pairs), pipeline_mode=pl.Buffered(1)),
            columns(width, 0),
            columns(width, pairs),
            columns(width, 2 * pairs),
            fixed(256, 128),
            fixed(rows + 256, 128),
            columns(blocks * slots, 0),
            fixed(rows, 128),
        ],
        out_specs=[
            of_pair(0, 256, 256),
            columns(rows, 0),
            of_pair(0, blocks, 256),
            columns(rows, 0),
            columns(rows + 256, 0),
            columns(rows + 256, 0),
            columns(slots, 0),
            columns(slots, 0),
            fixed_out(rows + 256, width),
            fixed_out(8, width),
            fixed_out(width, rows + 256),
            fixed_out(width, slots),
        ],
        out_shape=[
            jax.ShapeDtypeStruct((pairs, 256, 256), f32),
            jax.ShapeDtypeStruct((rows, width), bf16),
            jax.ShapeDtypeStruct((pairs, blocks, 256), f32),
            jax.ShapeDtypeStruct((rows, width), bf16),
            jax.ShapeDtypeStruct((rows + 256, width), bf16),
            jax.ShapeDtypeStruct((rows + 256, width), bf16),
            jax.ShapeDtypeStruct((slots, width), bf16),
            jax.ShapeDtypeStruct((slots, width), bf16),
            jax.ShapeDtypeStruct((rows + 256, width), bf16),
            jax.ShapeDtypeStruct((8, width), f32),
            jax.ShapeDtypeStruct((width, rows + 256), bf16),
            jax.ShapeDtypeStruct((width, slots), bf16),
        ],
        scratch_shapes=[pltpu.VMEM((slots, width), bf16), pltpu.VMEM((128, rows + 256), bf16), pltpu.VMEM((128, slots), bf16)],
        compiler_params=pltpu.CompilerParams(vmem_limit_bytes=48 << 20),
        cost_estimate=pl.CostEstimate(
            flops=30 * rows * (384 + slots) * width, bytes_accessed=24 << 20, transcendentals=0
        ),
        name="attend_forward",
    )(source_ext, raw_pool, weights, weights, weights, weights, bias, klocal, kglobal, qfeat)


def attention_backward(
    first, count, part, queries, grads, keys, values, gkeys, gvalues, normed, turned, pooled, weights, logs, bias, klocal,
    kglobal, qfeat, raw_pool, gains, place, old_small, old_table,
):
    rows, width = queries.shape
    slots = gkeys.shape[0]
    blocks = rows // 128
    pairs = width // 128
    lead = count * (4 if first + count == pairs else 3)
    return pl.pallas_call(
        functools.partial(attend_backward, first + count == pairs, width // 32, part, first),
        grid=(count,),
        in_specs=[
            columns(rows, first),
            columns(rows, first),
            columns(rows + 256, first),
            columns(rows + 256, first),
            columns(slots, first),
            columns(slots, first),
            fixed(rows + 256, width),
            fixed(width, rows + 256),
            fixed(width, slots),
            columns(width, first),
            columns(width, pairs + first),
            columns(width, 2 * pairs + first),
            of_pair(first, blocks, 256),
            of_pair(first, 256, 256),
            fixed(rows + 256, 128),
            columns(blocks * slots, first),
            fixed(rows, 128),
            fixed(slots, width),
            fixed(8, width),
            pl.BlockSpec(memory_space=pltpu.SMEM),
            fixed(8, width),
            fixed(32, 128),
        ],
        out_specs=[
            fixed_out(lead, width // 2, 128),
            fixed_out(lead, width // 2, 128),
            fixed_out(rows + 256, width),
            fixed_out(slots, width),
            fixed_out(8, width),
            fixed_out(32, 128),
        ],
        out_shape=[
            jax.ShapeDtypeStruct((lead, width // 2, 128), bf16),
            jax.ShapeDtypeStruct((lead, width // 2, 128), bf16),
            jax.ShapeDtypeStruct((rows + 256, width), bf16),
            jax.ShapeDtypeStruct((slots, width), bf16),
            jax.ShapeDtypeStruct((8, width), f32),
            jax.ShapeDtypeStruct((32, 128), f32),
        ],
        scratch_shapes=[
            pltpu.VMEM((rows + 256, width), f32),
            pltpu.VMEM((slots, width), f32),
            pltpu.VMEM((128, rows + 256), bf16),
            pltpu.VMEM((128, slots), bf16),
            pltpu.VMEM((rows, 128), bf16),
            pltpu.VMEM((rows + 256, 128), f32),
            pltpu.VMEM((rows + 256, 128), f32),
            pltpu.VMEM((slots, 128), f32),
            pltpu.VMEM((slots, 128), f32),
            pltpu.VMEM((256, 256), f32),
            pltpu.VMEM((slots, 128), f32),
        ],
        compiler_params=pltpu.CompilerParams(vmem_limit_bytes=48 << 20),
        cost_estimate=pl.CostEstimate(
            flops=60 * rows * (384 + slots) * 128 * count, bytes_accessed=count << 22, transcendentals=0
        ),
        name="attend_backward",
    )(
        queries, grads, keys, values, gkeys, gvalues, normed, turned, pooled, weights, weights, weights, logs, bias, klocal,
        kglobal, qfeat, raw_pool, gains, place, old_small, old_table,
    )


def interleave(held, other, core):
    held, other = held.astype(f32), other.astype(f32)
    both = jnp.stack([jnp.where(core == 0, held, other), jnp.where(core == 0, other, held)], axis=1)
    return both.reshape(-1, both.shape[-1])


def fold_rows(tall):
    rows, width = tall.shape[1:]
    return jnp.concatenate(
        [
            jnp.concatenate(
                [tall[:, r : r + 8, c : c + 256] for r in range(0, rows, 8)], axis=2
            )
            for c in range(0, width, 256)
        ],
        axis=1,
    )


unfold_rows = fold_rows


def pack(
    source_ref, keep_ref, marks_ref, wq_ref, wk_ref, wv_ref, wo_ref, gains_ref, gate_ref, up_ref, down_ref,
    first_ref, second_ref, shared_ref,
):
    width = source_ref.shape[1]
    for index, weight_ref in enumerate((wq_ref, wk_ref, wv_ref, wo_ref)):
        first_ref[:, index * width : (index + 1) * width] = weight_ref[...]
    first_ref[:, 4 * width :] = gains_ref[...]
    if second_ref.shape[1] > 128:
        hidden = gate_ref.shape[1]
        second_ref[:, :hidden] = gate_ref[...]
        second_ref[:, hidden : 2 * hidden] = up_ref[...]
        second_ref[:, 2 * hidden :] = fold_rows(down_ref[...].astype(f32)[None])[0].astype(bf16)
    slots = source_ref.shape[0] // 16
    for slot in range(0, slots, 16):
        rows = slice(slot * 16, slot * 16 + 256)
        values = source_ref[rows, :].astype(f32)
        values = values * (inverse_rms(values) * keep_ref[rows, :])
        shared_ref[slot : slot + 16, :] = jnp.sum(values.reshape(16, 16, width), axis=1).astype(bf16)
    marks = marks_ref[...].astype(f32)
    rest = jnp.zeros((marks.shape[0], width - 128), f32)
    shared_ref[slots:, :] = jnp.concatenate([marks, rest], axis=1).astype(bf16)


def pack_all(source, keep, marks, wq, wk, wv, wo, gains, gate, up, down, aligned):
    rows, width = source.shape
    part, hidden = gate.shape
    return pl.pallas_call(
        pack,
        out_shape=[
            jax.ShapeDtypeStruct((part, 4 * width + 128), bf16),
            jax.ShapeDtypeStruct((part, 3 * hidden if aligned else 128), bf16),
            jax.ShapeDtypeStruct((rows // 16 + marks.shape[0], width), bf16),
        ],
        compiler_params=pltpu.CompilerParams(vmem_limit_bytes=60 << 20),
        name="pack",
    )(source, keep, marks, wq, wk, wv, wo, gains, gate, up, down)


def feed_forward(
    source_ref, mixture_ref, wo_ref, gains_ref, cot_ref, gate_held, gate_other, up_held, up_other, down_held, down_other,
    place_ref,
    out_ref, middle_grad_ref, dmixture_ref, dgain_ref, keep_out, send_out, keep_wide, send_wide, keep_down, send_down,
    middle, normed, turned, out_sum, grad_sum, product, gate_low, lift_low, wg_ref, wu_ref, wd_ref,
):
    rows, width = source_ref.shape
    part_rows = 256
    parts = rows // part_rows
    gain = gains_ref[2:3, :]
    core = place_ref[0]
    wg_ref[...] = interleave(gate_held[...], gate_other[...], core).astype(bf16)
    wu_ref[...] = interleave(up_held[...], up_other[...], core).astype(bf16)
    wd_ref[...] = interleave(
        unfold_rows(down_held[...].astype(f32)), unfold_rows(down_other[...].astype(f32)), core
    ).astype(bf16)

    @pl.when(pl.program_id(0) == 0)
    def start():
        def norm_rows(index, carry):
            part = pl.ds(pl.multiple_of(index * 128, 128), 128)
            values = source_ref[part, :].astype(f32) + dot_nn(mixture_ref[part, :], wo_ref[...])
            middle[part, :] = values
            low = (values * inverse_rms(values) * gain).astype(bf16)
            normed[part, :] = low
            turned[:, part] = low.T
            return carry

        lax.fori_loop(0, rows // 128, norm_rows, 0)
        out_sum[...] = jnp.zeros_like(out_sum)
        grad_sum[...] = jnp.zeros_like(grad_sum)

    root = 0.7978845608028654
    for index in range(parts):
        part = slice(index * part_rows, (index + 1) * part_rows)
        low = normed[part, :]
        gate_pre = dot_nn(low, wg_ref[...])
        lift_pre = dot_nn(low, wu_ref[...])
        grad = dot_nt(cot_ref[part, :], wd_ref[...])
        square = gate_pre * gate_pre
        bent = jnp.tanh(gate_pre * (root + (root * 0.044715) * square))
        half = 0.5 + 0.5 * bent
        gelu = gate_pre * half
        slope = half + gelu * (1.0 - bent) * (root + (3 * root * 0.044715) * square)
        product[part, :] = (gelu * lift_pre).astype(bf16)
        lift_low[part, :] = (grad * gelu).astype(bf16)
        gate_low[part, :] = (grad * lift_pre * slope).astype(bf16)
        out_sum[part, :] += dot_nn(product[part, :], wd_ref[...])
        grad_sum[part, :] += dot_nt(gate_low[part, :], wg_ref[...]) + dot_nt(
            lift_low[part, :], wu_ref[...]
        )
    wide_part, down_part = width // 32, down_held.shape[1] * down_held.shape[2] // width
    store_halves(keep_wide, send_wide, 0, dot_nn(turned[...], gate_low[...]), core, wide_part)
    store_halves(keep_wide, send_wide, 1, dot_nn(turned[...], lift_low[...]), core, wide_part)
    value = dot_nn(product[...].T, cot_ref[...]).reshape(-1, 2, down_part, width)
    first, second = value[:, 0], value[:, 1]
    for half_ref, chosen in (
        (keep_down, jnp.where(core == 0, first, second)),
        (send_down, jnp.where(core == 0, second, first)),
    ):
        folded = fold_rows(chosen)
        folded = folded.reshape(-1, folded.shape[2]).astype(bf16)
        half_ref[0], half_ref[1] = folded[:, : folded.shape[1] // 2], folded[:, folded.shape[1] // 2 :]

    @pl.when(pl.program_id(0) == pl.num_programs(0) - 1)
    def finish():
        dgain_ref[...] = jnp.zeros_like(dgain_ref)

        def back_rows(index, carry):
            part = pl.ds(pl.multiple_of(index * 128, 128), 128)
            values = middle[part, :]
            out_ref[part, :] = (values + out_sum[part, :]).astype(bf16)
            inverse = inverse_rms(values)
            grad = grad_sum[part, :]
            dgain_ref[2:3, :] += jnp.sum(grad * values * inverse, axis=0, keepdims=True)
            total = cot_ref[part, :].astype(f32) + norm_gradient(values, inverse, gain, grad)
            middle_grad_ref[part, :] = total
            low = total.astype(bf16)
            normed[part, :] = low
            dmixture_ref[part, :] = dot_nt(low, wo_ref[...]).astype(bf16)
            turned[:, part] = mixture_ref[part, :].T
            return carry

        lax.fori_loop(0, rows // 128, back_rows, 0)
        for side in range(2):
            half = slice(side * width // 2, (side + 1) * width // 2)
            store_halves(keep_out, send_out, side, dot_nn(turned[...], normed[:, half]), core, width // 32)


def feed_forward_both(source, mixture, weights, gains, cotangent, held, other, place):
    rows, width = source.shape
    groups, part, total = held.shape
    hidden = total // 3
    tile = 512
    tiles = hidden // tile
    step_groups = groups // tiles
    gate_spec = pl.BlockSpec((groups, part, tile), lambda step: (0, 0, step))
    up_spec = pl.BlockSpec((groups, part, tile), lambda step: (0, 0, step + tiles))
    down_spec = pl.BlockSpec((step_groups, part, hidden), lambda step: (step, 0, 2))
    wide_spec = pl.BlockSpec((2, width // 2, tile), lambda step: (0, 0, step))
    fold_spec = pl.BlockSpec((2, step_groups * part, hidden // 2), lambda step: (0, step, 0))
    out_spec = fixed_out(2, width // 2, width // 2)
    return pl.pallas_call(
        feed_forward,
        grid=(tiles,),
        in_specs=[
            fixed(rows, width),
            fixed(rows, width),
            pl.BlockSpec((width, width), lambda step: (0, 3), pipeline_mode=pl.Buffered(1)),
            fixed(8, width),
            fixed(rows, width),
            gate_spec,
            gate_spec,
            up_spec,
            up_spec,
            down_spec,
            down_spec,
            pl.BlockSpec(memory_space=pltpu.SMEM),
        ],
        out_specs=[
            fixed_out(rows, width),
            fixed_out(rows, width),
            fixed_out(rows, width),
            fixed_out(8, width),
            out_spec,
            out_spec,
            wide_spec,
            wide_spec,
            fold_spec,
            fold_spec,
        ],
        out_shape=[
            jax.ShapeDtypeStruct((rows, width), bf16),
            jax.ShapeDtypeStruct((rows, width), f32),
            jax.ShapeDtypeStruct((rows, width), bf16),
            jax.ShapeDtypeStruct((8, width), f32),
            jax.ShapeDtypeStruct((2, width // 2, width // 2), bf16),
            jax.ShapeDtypeStruct((2, width // 2, width // 2), bf16),
            jax.ShapeDtypeStruct((2, width // 2, hidden), bf16),
            jax.ShapeDtypeStruct((2, width // 2, hidden), bf16),
            jax.ShapeDtypeStruct((2, width // 2, hidden // 2), bf16),
            jax.ShapeDtypeStruct((2, width // 2, hidden // 2), bf16),
        ],
        scratch_shapes=[
            pltpu.VMEM((rows, width), f32),
            pltpu.VMEM((rows, width), bf16),
            pltpu.VMEM((width, rows), bf16),
            pltpu.VMEM((rows, width), f32),
            pltpu.VMEM((rows, width), f32),
            pltpu.VMEM((rows, tile), bf16),
            pltpu.VMEM((rows, tile), bf16),
            pltpu.VMEM((rows, tile), bf16),
            pltpu.VMEM((width, tile), bf16),
            pltpu.VMEM((width, tile), bf16),
            pltpu.VMEM((tile, width), bf16),
        ],
        compiler_params=pltpu.CompilerParams(vmem_limit_bytes=60 << 20),
        cost_estimate=pl.CostEstimate(
            flops=20 * rows * width * hidden, bytes_accessed=40 << 20, transcendentals=0
        ),
        name="feed_forward",
    )(source, mixture, weights, gains, cotangent, held, other, held, other, held, other, place)


def near_offsets(local_bias):
    heads, buckets = local_bias.shape
    offset = (jnp.arange(256, dtype=i32) + 128) % 256 - 128
    table = (bucket_of(offset)[:, None] == jnp.arange(buckets, dtype=i32)).astype(f32)
    chosen = jnp.einsum("ob,hb->oh", table, local_bias, precision=highest)
    chosen = jnp.where((offset == -128)[:, None], never, chosen)
    return jnp.pad(chosen, ((0, 0), (0, 128 - heads)))


def far_features(global_bias, slot_segments, slot_live, first_slot, blocks):
    heads, buckets = global_bias.shape
    pairs = heads // 2
    slots = slot_segments.shape[0]
    wide = 8 * buckets + 8
    shape = (blocks * slots, wide)
    row = lax.broadcasted_iota(i32, shape, 0)
    column = lax.broadcasted_iota(i32, shape, 1)
    slot = row % slots
    query_slot = first_slot + (row // slots) * 8 + column // buckets
    code = jnp.tile(jnp.where(slot_live, slot_segments, 3), blocks)[:, None]
    picks = jnp.where(
        column < 8 * buckets,
        bucket_of(slot - query_slot) == column % buckets,
        code == column - 8 * buckets,
    ).astype(bf16)
    high = lax.reduce_precision(global_bias, 8, 7)
    middle = lax.reduce_precision(global_bias - high, 8, 7)
    lowest = lax.reduce_precision(global_bias - high - middle, 8, 7)
    parts = jnp.stack([high, middle, lowest]).reshape(3, pairs, 2, buckets)
    parts = parts.transpose(3, 1, 0, 2)
    same = jnp.eye(8, dtype=f32)[:, None, None, None, None, :]
    table = (parts[None, :, :, :, :, None] * same).reshape(8 * buckets, pairs, 48)
    table = jnp.pad(table, ((0, 8), (0, 0), (0, 80)))
    shape = (wide, 1, 128)
    lane = lax.broadcasted_iota(i32, shape, 2) - 48
    code_row = lax.broadcasted_iota(i32, shape, 0) - 8 * buckets
    barred = (code_row >= 0) & (lane >= 0) & (lane < 3) & (lane != code_row)
    table = jnp.where(barred, never, table).astype(bf16).reshape(wide, pairs * 128)
    return jnp.dot(picks, table, preferred_element_type=f32).astype(bf16)


def near_features(segments_ext, valid_ext):
    lane = lax.broadcasted_iota(i32, (segments_ext.shape[0], 128), 1)
    allowed = (segments_ext[:, None] == lane - 48) & (valid_ext[:, None] > 0)
    return jnp.where((lane >= 48) & (lane < 51) & ~allowed, never, 0.0).astype(bf16)


def query_features(own_segments):
    lane = lax.broadcasted_iota(i32, (own_segments.shape[0], 128), 1)
    return (own_segments[:, None] == lane - 48).astype(bf16)


def pick(values, index, dim):
    return lax.dynamic_index_in_dim(values, index, dim, keepdims=False)


def ring(size, hop):
    return [(i, (i + hop) % size) for i in range(size)]


def add_up(parts):
    if len(parts) == 1:
        return parts[0]
    return sum((part.astype(f32) for part in parts[1:]), parts[0].astype(f32))


def split_stage(side, labels, axis, join):
    size, me = lax.axis_size(axis), lax.axis_index(axis)
    dim = labels.index(axis) - len(labels) - 2 + side[0][0].ndim
    chosen = []
    for hop in range(size):
        pieces = [
            add_up([pick(part, (me + hop) % size, dim) for part in piece]).astype(bf16) for piece in side
        ]
        chosen.append(pieces[0] if len(pieces) == 1 else jnp.concatenate(pieces, axis=join))
    return chosen[1:], chosen[0]


def send_all(axis, pieces):
    size = lax.axis_size(axis)
    return [lax.ppermute(piece, axis, ring(size, hop + 1)) for hop, piece in enumerate(pieces)]


def place_stage(values, pieces, axis, dim):
    size, me = lax.axis_size(axis), lax.axis_index(axis)
    shape = values.shape[:dim] + (size,) + values.shape[dim:]
    out = lax.dynamic_update_index_in_dim(jnp.zeros(shape, values.dtype), values, me, dim)
    for hop, piece in enumerate(pieces):
        out = lax.dynamic_update_index_in_dim(out, piece, (me - hop - 1) % size, dim)
    return out


def half_of(width):
    return (width // 256) * 128


def scatter_steps(sides, labels, stages, join):
    labels = [list(labels) for _ in sides]
    for axes in stages:
        if len(axes) < len(sides):
            sides, labels = [[piece for side in sides for piece in side]], labels[:1]
        split = [split_stage(side, names, axis, join) for side, names, axis in zip(sides, labels, axes)]
        sends = yield [send for send, _ in split]
        gots = yield [send_all(axis, send) for axis, send in zip(axes, sends)]
        sides = [[[keep] + got] for (_, keep), got in zip(split, gots)]
        for names, axis in zip(labels, axes):
            names.remove(axis)
    return add_up(sides[0][0])


across = (("x", "y"), ("y", "x"))


stages = (("x", "y"), ("y", "x"), ("z",))
labels = ("y", "x", "z")


def core_steps(pairs, part):
    y, x, z, _ = (lax.axis_size(axis) for axis in everyone)
    keeps, sends = zip(*pairs)
    if part != keeps[0].shape[1] // 16:
        keeps, sends = zip(*(regroup(keep, send, part) for keep, send in pairs))
    sends = yield sends
    gots = yield [lax.ppermute(send, "core", ring(2, 1)) for send in sends]
    sides = [[], []]
    for keep, got in zip(keeps, gots):
        lead, _, width = keep.shape
        held, new = (values.reshape(lead, y, x, z, part, width) for values in (keep, got))
        sides[0].append([held[: lead // 2], new[: lead // 2]])
        sides[1].append([held[lead // 2 :], new[lead // 2 :]])
    return sides


def sum_rows(pairs, part, join):
    sides = yield from core_steps(pairs, part)
    return (yield from scatter_steps(sides, labels, stages, join))


def regroup(keep, send, part):
    lead, half, width = keep.shape
    both = jnp.stack([keep.reshape(lead, 16, -1, width), send.reshape(lead, 16, -1, width)], axis=2)
    both = both.reshape(lead, half // part, 2, part, width)
    me = lax.axis_index("core")
    return tuple(pick(both, index, 2).reshape(keep.shape) for index in (me, 1 - me))


def all_rows(shard, last):
    width = shard.shape[1]
    half = half_of(width)
    others = lax.axis_size("z") - 1
    shard = yield shard
    pieces = yield send_all("z", [shard] * others)
    values = place_stage(shard, pieces, "z", 0)
    left, right = values[..., :half], values[..., half:]
    for left_axis, right_axis in across:
        dim = 1 if right_axis == "x" else 0
        left, right = yield left, right
        got = yield (
            send_all(left_axis, [left] * (lax.axis_size(left_axis) - 1)),
            send_all(right_axis, [right] * (lax.axis_size(right_axis) - 1)),
        )
        left = place_stage(left, got[0], left_axis, 0)
        right = place_stage(right, got[1], right_axis, dim)
    values = yield jnp.concatenate([left, right], axis=-1)
    got = yield send_all("core", [values])
    if not last:
        return values.reshape(-1, *values.shape[-2:]), got[0].reshape(-1, *values.shape[-2:])
    return place_stage(values, got, "core", 3).reshape(-1, width)


class Chain:
    def __init__(self, steps):
        self.steps = steps
        self.value = next(steps)
        self.done = False

    def advance(self):
        try:
            self.value = self.steps.send(self.value)
        except StopIteration as end:
            self.value, self.done = end.value, True


def phase(operand, work, launch=(), collect=None):
    collect = launch if collect is None else collect
    values, operand = lax.optimization_barrier(([chain.value for chain in launch], operand))
    for chain, value in zip(launch, values):
        chain.value = value
        chain.advance()
    result = work(operand)
    values, result = lax.optimization_barrier(([chain.value for chain in collect], result))
    for chain, value in zip(collect, values):
        chain.value = value
        chain.advance()
    return result


def neighbour_rows(to_after, to_before):
    count = lax.axis_size(seq)
    ends = count - 1
    before = lax.ppermute(to_after, seq, [(i, i + 1) for i in range(ends)])
    after = lax.ppermute(to_before, seq, [(i + 1, i) for i in range(ends)])
    return before, after


def on_device(
    hidden_state,
    segment_ids,
    valid_mask,
    cotangent,
    norm_gain,
    pool_gain,
    feed_gain,
    query_weight,
    key_weight,
    value_weight,
    output_weight,
    local_bias,
    global_bias,
    gate_weight,
    up_weight,
    down_weight,
):
    model_width = hidden_state.shape[2]
    hidden = gate_weight.shape[1]
    tok_rows = hidden_state.shape[1]
    own_part = norm_gain.shape[0]
    buckets = local_bias.shape[1]
    pairs = local_bias.shape[0] // 2
    blocks = tok_rows // 128
    own_slots = tok_rows // 16
    seq_count = lax.axis_size(seq)
    slot_count = own_slots * seq_count
    row_start = lax.axis_index(seq) * tok_rows
    first_slot = row_start // 16
    source = hidden_state[0]
    upstream = cotangent[0]
    own_segments = segment_ids[0]
    valid_float = valid_mask[0].astype(f32)

    aligned = own_part * 32 == model_width
    gain_columns = jnp.pad(jnp.stack([norm_gain, pool_gain, feed_gain], axis=1), ((0, 0), (0, 125)))
    marks = jnp.concatenate([segment_ids.reshape(-1, 128), valid_mask.reshape(-1, 128)])
    packed, packed_second, shared = pack_all(
        source, valid_float[:, None], marks, query_weight, key_weight, value_weight, output_weight, gain_columns,
        gate_weight, up_weight, down_weight, aligned,
    )
    first = Chain(all_rows(packed, True))
    later = [Chain(all_rows(packed_second, False))] if aligned else []
    place = jnp.stack([lax.axis_index("core"), first_slot]).astype(i32)

    def share(shared):
        before, after = neighbour_rows(source[-128:], source[:128])
        copies = jnp.broadcast_to(shared, (seq_count,) + shared.shape)
        return lax.all_to_all(copies, seq, 0, 0, tiled=True), before, after

    shared, before, after = phase(shared, share, [first])

    def near_parts(operands):
        shared, before, after, local_bias = operands
        raw_pool = shared[:, :own_slots].reshape(slot_count, model_width)
        all_marks = shared[:, own_slots:, :128].astype(i32).reshape(seq_count, 2, tok_rows)
        all_segments, all_valid = all_marks[:, 0].reshape(-1), all_marks[:, 1].reshape(-1)
        slot_segments = all_segments.reshape(slot_count, 16)[:, 0]
        slot_live = jnp.sum(all_valid.reshape(slot_count, 16), axis=1) > 0
        segments_ext = lax.dynamic_slice_in_dim(
            jnp.pad(all_segments, 128, constant_values=-1), row_start, tok_rows + 256
        )
        valid_ext = lax.dynamic_slice_in_dim(jnp.pad(all_valid, 128), row_start, tok_rows + 256)
        feat_near = near_features(segments_ext, valid_ext)
        source_ext = jnp.concatenate([before, source, after], axis=0)
        return raw_pool, slot_segments, slot_live, feat_near, near_offsets(local_bias), source_ext

    raw_pool, slot_segments, slot_live, feat_near, bias_near, source_ext = phase(
        (shared, before, after, local_bias), near_parts, [first] + later, [first]
    )
    feat_query = query_features(own_segments)
    feat_far = phase(
        (global_bias, slot_segments, slot_live),
        lambda operands: far_features(*operands, first_slot, blocks),
        [first],
        [first] + later,
    )
    phase((), lambda nothing: nothing, [first] + later)
    weights = first.value

    bias, mixture, logs, queries, keys, vals, gkeys, gvals, normed, gains, turned, pooled = phase(
        (source_ext, raw_pool, weights, bias_near, feat_near, feat_far, feat_query),
        lambda operands: attention_forward(*operands),
        later,
    )
    phase((), lambda nothing: nothing, later)
    if aligned:
        held, other = later[0].value
        kernel_place = place
    else:
        wide = lax.all_gather(jnp.concatenate([gate_weight, up_weight], axis=1), everyone, axis=0, tiled=True)
        tall = lax.all_gather(down_weight, everyone, axis=0, tiled=True)
        tall = fold_rows(tall.reshape(32, -1, model_width))
        both = jnp.concatenate([wide.reshape(32, -1, 2 * hidden), tall], axis=2)
        both = both.reshape(16, 2, -1, 3 * hidden)
        held, other = both[:, 0], both[:, 1]
        kernel_place = place * jnp.array([0, 1], i32)
    layer_output, middle_grad, mixture_grad, small, out_keep, out_send, wide_keep, wide_send, down_keep, down_send = (
        feed_forward_both(source, mixture, weights, gains, upstream, held, other, kernel_place)
    )
    rest = []
    if aligned:
        pieces = [(wide_keep, wide_send), (down_keep, down_send), (out_keep, out_send)]
        rest = [Chain(sum_rows(pieces, own_part, -1))]
    table = jnp.zeros((32, 128), f32)
    count = pairs // calls
    dnormed, draw, waiting, started = [], [], [], []
    for call in range(calls):
        keep, send, dnormed_part, draw_part, small, table = phase(
            (mixture_grad, small, table),
            lambda operands: attention_backward(
                call * count, count, own_part, queries, operands[0], keys, vals, gkeys, gvals, normed, turned, pooled, weights,
                logs, bias, feat_near, feat_far, feat_query, raw_pool, gains, kernel_place, *operands[1:],
            ),
            rest + started,
        )
        waiting.append((keep, send))
        if call > 0:
            started.append(Chain(core_steps(waiting, own_part)))
            waiting = []
        dnormed.append(dnormed_part)
        draw.append(draw_part)

    def return_grads(operands):
        dnormed, draw = operands
        me = lax.axis_index(seq)
        head, tail = (add_up([part[where] for part in dnormed]).astype(bf16) for where in (slice(128), slice(-128, None)))
        target = lax.broadcasted_iota(i32, (seq_count, 1, 1), 0)
        edges = jnp.where(target == me - 1, head[None], jnp.where(target == me + 1, tail[None], 0))
        pools = add_up(draw).astype(bf16).reshape(seq_count, own_slots, model_width)
        return lax.all_to_all(jnp.concatenate([pools, edges], axis=1), seq, 0, 0, tiled=True)

    def finish(operands):
        me = lax.axis_index(seq)
        spread = operands[:, :own_slots]
        to_head, to_tail = (
            jnp.where(
                (near >= 0) & (near < seq_count),
                pick(operands[:, own_slots:], jnp.clip(near, 0, seq_count - 1), 0),
                0,
            )
            for near in (me - 1, me + 1)
        )
        values = source.astype(f32)
        inverse = inverse_rms(values)
        edges = jnp.concatenate(
            [to_head.astype(f32), jnp.zeros((tok_rows - 256, model_width), f32), to_tail.astype(f32)]
        )
        pooled_raw_grad = jnp.sum(spread.astype(f32), axis=0)
        spread_grad = jnp.broadcast_to(
            pooled_raw_grad[:, None, :], (own_slots, 16, model_width)
        ).reshape(tok_rows, model_width)
        normed_grad = add_up([part[128:-128] for part in dnormed])
        normed_grad = normed_grad + edges + spread_grad * valid_float[:, None]
        return middle_grad + norm_gradient(values, inverse, gains[0:1], normed_grad)

    def return_and_start(operands):
        for chain in rest:
            chain.advance()
        return return_grads(operands)

    held = []
    phase((dnormed, draw), lambda operands: held.append(return_and_start(operands)), started[1:])
    operands = held[0]
    sides = [sum((chain.value[side] for chain in started), []) for side in range(2)]
    last = Chain(scatter_steps(sides, labels, stages, 0))
    operands = phase(operands, lambda operands: operands, [last])
    input_delta = phase(operands, finish, [last], rest + [last])
    phase((), lambda nothing: nothing, [last])
    total = last.value
    half = total.shape[0] // 2
    sides = [total[:half], total[half:]]
    extra = jnp.concatenate([side[half - 1] for side in sides], axis=-1)
    blocks_of_table = -(-4 * pairs // own_part)
    tables = extra[:, 128 : 128 + buckets * blocks_of_table].reshape(own_part, blocks_of_table, buckets)
    tables = tables.transpose(1, 0, 2).reshape((2,) + local_bias.shape)
    query_delta, key_delta, value_delta = (
        jnp.concatenate(
            [sides[pair % count][3 * (pair // count) + index] for pair in range(pairs)],
            axis=-1,
        )
        for index in range(3)
    )
    if aligned:
        total = rest[0].value[0]
        side, fold, half = total.shape[1] // 2, hidden // 2, model_width // 2
        left, right = total[:, :side], total[:, side:]
        gate_delta, up_delta = left[:, :hidden], right[:, :hidden]
        tall = jnp.concatenate([left[:, hidden : hidden + fold], right[:, hidden : hidden + fold]], axis=1)
        down_delta = unfold_rows(tall[None])[0]
        output_delta = jnp.concatenate([left[:, hidden + fold :], right[:, hidden + fold :]], axis=1)
    else:

        def whole_rows(keep, send):
            width = keep.shape[-1]
            both = jnp.stack([keep.reshape(16, -1, width), send.reshape(16, -1, width)], axis=1)
            return both.reshape(32, -1, width)

        def join(halves):
            return jnp.concatenate([halves[0], halves[1]], axis=-1)

        def scatter(grads):
            grads = grads.reshape(-1, grads.shape[-1])
            return lax.psum_scatter(grads, everyone, scatter_dimension=0, tiled=True).astype(f32)

        gate_delta = scatter(whole_rows(wide_keep[0], wide_send[0]))
        up_delta = scatter(whole_rows(wide_keep[1], wide_send[1]))
        output_delta = scatter(whole_rows(join(out_keep), join(out_send)))
        down_delta = scatter(unfold_rows(whole_rows(join(down_keep), join(down_send))))
    return (
        layer_output[None],
        input_delta[None],
        extra[:, 0],
        extra[:, 1],
        extra[:, 2],
        query_delta,
        key_delta,
        value_delta,
        output_delta,
        tables[0],
        tables[1],
        gate_delta,
        up_delta,
        down_delta,
    )


def solution(mesh):
    seq_size, batch_size = mesh.shape["seq"], mesh.shape["batch"]
    chips = Mesh(mesh.devices.reshape(2, seq_size // 2, batch_size // 2, 2), everyone)
    tokens = P(batch, seq, None)
    marks = P(batch, seq)
    row = P(everyone)
    matrix = P(everyone, None)
    whole = P()
    return jax.shard_map(
        on_device,
        mesh=chips,
        in_specs=(tokens, marks, marks, tokens, row, row, row)
        + (matrix,) * 4
        + (whole,) * 2
        + (matrix,) * 3,
        out_specs=(tokens, tokens, row, row, row)
        + (matrix,) * 4
        + (whole,) * 2
        + (matrix,) * 3,
        check_vma=False,
    )
```

```python
import functools

import jax
import jax.numpy as jnp
from jax import lax
from jax.experimental import pallas as pl
from jax.experimental.pallas import tpu as pltpu
from jax.sharding import Mesh
from jax.sharding import PartitionSpec as P

epsilon = 1e-06
boundaries = (12, 16, 23, 32, 46, 64, 91)
never = -1e30
seq = ("y", "x")
batch = ("z", "core")
everyone = seq + batch
bf16 = jnp.bfloat16
f32 = jnp.float32
i32 = jnp.int32
highest = lax.Precision.HIGHEST
calls = 3


def bucket_of(offset):
    distance = jnp.abs(offset)
    far_part = 8 + sum(((distance >= boundary).astype(i32) for boundary in boundaries))
    return 16 * (offset > 0).astype(i32) + jnp.where(distance < 8, distance, far_part)


def dot_nt(left, right):
    return lax.dot_general(left, right, (((1,), (1,)), ((), ())), preferred_element_type=f32)


def dot_nn(left, right):
    return lax.dot_general(left, right, (((1,), (0,)), ((), ())), preferred_element_type=f32)


def inverse_rms(values):
    return lax.rsqrt(jnp.mean(values * values, axis=-1, keepdims=True) + epsilon)


def norm_gradient(values, inverse, gain, grad):
    weighted = grad * gain
    mean = jnp.mean(weighted * values, axis=-1, keepdims=True)
    return inverse * weighted - (inverse * inverse * inverse * mean) * values


def store_halves(keep_ref, send_ref, index, value, core, part):
    rows, width = value.shape
    value = value.reshape(rows // (2 * part), 2, part, width)
    first, second = value[:, 0].reshape(rows // 2, width), value[:, 1].reshape(rows // 2, width)
    keep_ref[index] = jnp.where(core == 0, first, second).astype(bf16)
    send_ref[index] = jnp.where(core == 0, second, first).astype(bf16)


def stack_heads(rows):
    lane = lax.broadcasted_iota(i32, rows.shape, 1)
    zero = jnp.zeros_like(rows)
    return jnp.concatenate(
        [jnp.where(lane < 64, rows, zero), jnp.where(lane < 64, zero, rows)], axis=0
    )


def unstack_heads(wide):
    row = lax.broadcasted_iota(i32, (128, 128), 0)
    return jnp.where(row < 64, wide[:, :128], wide[:, 128:]).T


def upper_band():
    key = lax.broadcasted_iota(i32, (128, 256), 0)
    query = lax.broadcasted_iota(i32, (128, 256), 1) & 127
    return key > query


def spread_band(upper, own, merged):
    zero = jnp.zeros_like(merged)
    return jnp.concatenate(
        [jnp.where(upper, merged, zero), own, jnp.where(upper, zero, merged)], axis=0
    ).astype(bf16)


def window_of(block):
    return pl.ds(pl.multiple_of(block * 128, 128), 384)


def rows_of(block):
    return pl.ds(pl.multiple_of(block * 128, 128), 128)


def slot_lanes():
    row = lax.broadcasted_iota(i32, (256, 128), 0)
    lane = lax.broadcasted_iota(i32, (256, 128), 1)
    hit = (lane < 48) & ((lane & 15) == (row // 128) * 8 + (row % 128) // 16)
    return hit.astype(f32).astype(bf16)


def block_scores(block, upper, on_slot, query_two, key_ref, gkey_ref, bias_ref, klocal_ref, kglobal_ref, qfeat_ref):
    slots = gkey_ref.shape[0]
    window = window_of(block)
    segment_lanes = qfeat_ref[rows_of(block), :]
    features = jnp.concatenate([segment_lanes, segment_lanes], axis=0) + on_slot
    query_wide = jnp.concatenate([query_two, features], axis=1)
    key_wide = jnp.concatenate([key_ref[window, :], klocal_ref[window, :]], axis=1)
    local = dot_nt(key_wide, query_wide)
    own = local[128:256] + bias_ref[0, 0:128]
    merged = jnp.where(upper, local[0:128], local[256:384]) + bias_ref[0, 128:256]
    far_rows = pl.ds(pl.multiple_of(block * slots, 128), slots)
    gkey_wide = jnp.concatenate([gkey_ref[...], kglobal_ref[far_rows, :]], axis=1)
    return own, merged, dot_nt(gkey_wide, query_wide)


def attend_forward(
    source_ref, raw_ref, gain_ref, wq_ref, wk_ref, wv_ref, offsets_ref, klocal_ref, kglobal_ref, qfeat_ref,
    bias_ref, out_ref, log_ref, query_ref, key_ref, value_ref, gkey_ref, gvalue_ref, normed_ref, gains_ref,
    normed_turned, pooled_turned, pooled_ref, value_turned, gvalue_turned,
):
    rows = query_ref.shape[0]
    slots = gkey_ref.shape[0]

    @pl.when(pl.program_id(0) == 0)
    def start():
        turned = gain_ref[...].astype(f32).T
        gains_ref[...] = turned[0:8]
        gain_one, gain_pool = turned[0:1], turned[1:2]

        def norm_rows(index, carry):
            part = pl.ds(pl.multiple_of(index * 128, 128), 128)
            values = source_ref[part, :].astype(f32)
            low = (values * inverse_rms(values) * gain_one).astype(bf16)
            normed_ref[part, :] = low
            normed_turned[:, part] = low.T
            return carry

        lax.fori_loop(0, (rows + 256) // 128, norm_rows, 0)

        def pool_rows(index, carry):
            part = pl.ds(pl.multiple_of(index * 128, 128), 128)
            values = raw_ref[part, :].astype(f32) * gain_one
            low = (values * inverse_rms(values) * gain_pool).astype(bf16)
            pooled_ref[part, :] = low
            pooled_turned[:, part] = low.T
            return carry

        lax.fori_loop(0, slots // 128, pool_rows, 0)

    lane = lax.broadcasted_iota(i32, (256, 128), 1)
    spread = []
    for head in range(2):
        mine = jnp.where(lane == 2 * pl.program_id(0) + head, offsets_ref[...], 0.0)
        spread.append(jnp.broadcast_to(jnp.sum(mine, axis=1, keepdims=True), (256, 128)))
    lane_of = lax.broadcasted_iota(i32, (256, 256), 1)
    bias_ref[0] = align_offsets(jnp.concatenate(spread, axis=1), lane_of & 127, 7, -1)

    query_ref[...] = dot_nn(normed_ref[128 : 128 + rows, :], wq_ref[...]).astype(bf16)
    w_two = jnp.concatenate([wk_ref[...], wv_ref[...]], axis=1)
    two = dot_nn(normed_ref[...], w_two).astype(bf16)
    key_ref[...] = two[:, :128]
    value_ref[...] = two[:, 128:]
    value_turned[...] = two[:, 128:].T
    two = dot_nn(pooled_ref[...], w_two).astype(bf16)
    gkey_ref[...] = two[:, :128]
    gvalue_ref[...] = two[:, 128:]
    gvalue_turned[...] = two[:, 128:].T
    upper = upper_band()
    on_slot = slot_lanes()

    def step(block, carry):
        window = window_of(block)
        query_two = stack_heads(query_ref[rows_of(block), :])
        own, merged, far = block_scores(
            block, upper, on_slot, query_two, key_ref, gkey_ref, bias_ref, klocal_ref, kglobal_ref, qfeat_ref
        )
        peak = jnp.maximum(
            jnp.maximum(
                jnp.max(own, axis=0, keepdims=True), jnp.max(merged, axis=0, keepdims=True)
            ),
            jnp.max(far, axis=0, keepdims=True),
        )
        own, merged, far = jnp.exp(own - peak), jnp.exp(merged - peak), jnp.exp(far - peak)
        total = (
            jnp.sum(own, axis=0, keepdims=True)
            + jnp.sum(merged, axis=0, keepdims=True)
            + jnp.sum(far, axis=0, keepdims=True)
        )
        near_low = spread_band(upper, own, merged)
        wide = dot_nn(value_turned[:, window], near_low) + dot_nn(
            gvalue_turned[...], far.astype(bf16)
        )
        out_ref[rows_of(block), :] = unstack_heads(wide * (1.0 / total)).astype(bf16)
        log_ref[0, pl.ds(block, 1), :] = peak + jnp.log(total)
        return carry

    lax.fori_loop(0, rows // 128, step, 0, unroll=8)


def align_offsets(sums, step_of_lane, bits, sign):
    for bit in range(bits):
        shift = sign * (1 << bit)
        moved = jnp.concatenate([sums[shift:], sums[:shift]], axis=0)
        sums = jnp.where((step_of_lane >> bit) & 1 == 1, moved, sums)
    return sums


def two_totals(left, right):
    lane = lax.broadcasted_iota(i32, (left.shape[0], 128), 1)
    first = jnp.sum(left, axis=1, keepdims=True)
    second = jnp.sum(right, axis=1, keepdims=True)
    return jnp.where(lane == 0, first, jnp.where(lane == 1, second, 0.0))


def add_buckets(table_ref, sums, offset, head):
    hit = (bucket_of(offset) == lax.broadcasted_iota(i32, sums.shape, 1)).astype(f32)
    totals = lax.dot_general(
        sums, hit, (((0,), (0,)), ((), ())), precision=highest, preferred_element_type=f32
    )
    row = lax.broadcasted_iota(i32, table_ref.shape, 0)
    table_ref[...] += jnp.where(
        row == head, totals[0:1], jnp.where(row == head + 1, totals[1:2], 0.0)
    )


def attend_backward(
    last, part, own_part, first_pair, query_ref, grad_ref, key_ref, value_ref, gkey_ref, gvalue_ref, normed_ref, normed_turned, pooled_turned, wq_ref, wk_ref, wv_ref,
    log_ref, bias_ref, klocal_ref, kglobal_ref, qfeat_ref, raw_ref, gains_ref, place_ref, old_small_ref, old_table_ref, old_dnormed_ref, old_draw_ref,
    keep_ref, send_ref, dnormed_ref, draw_ref, small_ref, table_ref,
    dnormed_sum, dpooled_sum, draw_sum, key_turned, gkey_turned, dquery, key_sum, value_sum, gkey_sum, gvalue_sum, near_sum, far_sum,
):
    rows = query_ref.shape[0]
    slots = gkey_ref.shape[0]

    @pl.when(pl.program_id(0) == 0)
    def start():
        dnormed_sum[...] = jnp.zeros_like(dnormed_sum)
        dpooled_sum[...] = jnp.zeros_like(dpooled_sum)
        table_ref[...] = old_table_ref[...]

    key_turned[...] = key_ref[...].T
    gkey_turned[...] = gkey_ref[...].T
    for total_ref in (key_sum, value_sum, gkey_sum, gvalue_sum, near_sum, far_sum):
        total_ref[...] = jnp.zeros_like(total_ref)
    upper = upper_band()
    on_slot = slot_lanes()
    lane = lax.broadcasted_iota(i32, (256, 128), 0)
    column = lax.broadcasted_iota(i32, (256, 128), 1)
    slot_column = (lane // 128) * 64 + (lane % 128) // 16

    def step(block, carry):
        window = window_of(block)
        query_two = stack_heads(query_ref[rows_of(block), :])
        grad_two = stack_heads(grad_ref[rows_of(block), :])
        own, merged, far = block_scores(
            block, upper, on_slot, query_two, key_ref, gkey_ref, bias_ref, klocal_ref, kglobal_ref, qfeat_ref
        )
        logs = log_ref[0, pl.ds(block, 1), :]
        own, merged, far = jnp.exp(own - logs), jnp.exp(merged - logs), jnp.exp(far - logs)
        value_sum[window, :] += dot_nn(spread_band(upper, own, merged), grad_two)
        gvalue_sum[...] += dot_nn(far.astype(bf16), grad_two)
        near_dot = dot_nt(value_ref[window, :], grad_two)
        own_dot = near_dot[128:256]
        merged_dot = jnp.where(upper, near_dot[0:128], near_dot[256:384])
        far_dot = dot_nt(gvalue_ref[...], grad_two)
        centre = (
            jnp.sum(own * own_dot, axis=0, keepdims=True)
            + jnp.sum(merged * merged_dot, axis=0, keepdims=True)
            + jnp.sum(far * far_dot, axis=0, keepdims=True)
        )
        own = own * (own_dot - centre)
        merged = merged * (merged_dot - centre)
        far = (far * (far_dot - centre)).astype(bf16)
        near_sum[0:128, :] += own
        near_sum[128:256, :] += merged
        choose = (column == slot_column + block * 8).astype(bf16)
        far_sum[...] += dot_nn(far, choose)
        near_low = spread_band(upper, own, merged)
        key_sum[window, :] += dot_nn(near_low, query_two)
        gkey_sum[...] += dot_nn(far, query_two)
        wide = dot_nn(key_turned[:, window], near_low) + dot_nn(gkey_turned[...], far)
        dquery[rows_of(block), :] = unstack_heads(wide).astype(bf16)
        return carry

    lax.fori_loop(0, rows // 128, step, 0, unroll=8)

    core, first_slot = place_ref[0], place_ref[1]
    head = 2 * (first_pair + pl.program_id(0))
    lane_of = lax.broadcasted_iota(i32, (256, 256), 1)
    near = align_offsets(near_sum[...], lane_of & 127, 7, 1)
    near = two_totals(near[:, :128], near[:, 128:])
    place = lax.broadcasted_iota(i32, (256, 128), 0)
    add_buckets(table_ref, near, ((place + 128) & 255) - 128, head)
    lane_of = lax.broadcasted_iota(i32, (slots + 64, 128), 1)
    far = jnp.concatenate([far_sum[...], jnp.zeros((64, 128), f32)], axis=0)
    far = align_offsets(far, lane_of & 63, 6, 1)
    far = two_totals(jnp.where(lane_of < 64, far, 0.0), jnp.where(lane_of < 64, 0.0, far))
    place = lax.broadcasted_iota(i32, (slots + 64, 128), 0)
    heads = normed_ref.shape[1] // 64
    add_buckets(table_ref, far, jnp.where(place < slots, place, place - slots - 64) - first_slot, heads + head)

    width = normed_ref.shape[1]
    grad_low = dquery[...]
    dwq = dot_nn(normed_turned[:, 128 : 128 + rows], grad_low)
    planes = 4 if last else 3
    lead = pl.program_id(0) * planes
    store_halves(keep_ref, send_ref, lead, dwq, core, part)
    dnormed_sum[128 : 128 + rows, :] += dot_nt(grad_low, wq_ref[...])
    two = jnp.concatenate([key_sum[...], value_sum[...]], axis=1).astype(bf16)
    gtwo = jnp.concatenate([gkey_sum[...], gvalue_sum[...]], axis=1).astype(bf16)
    w_two = jnp.concatenate([wk_ref[...], wv_ref[...]], axis=1)
    dw_two = dot_nn(normed_turned[...], two) + dot_nn(pooled_turned[...], gtwo)
    store_halves(keep_ref, send_ref, lead + 1, dw_two[:, :128], core, part)
    store_halves(keep_ref, send_ref, lead + 2, dw_two[:, 128:], core, part)
    dnormed_sum[...] += dot_nt(two, w_two)
    dpooled_sum[...] += dot_nt(gtwo, w_two)

    @pl.when(pl.program_id(0) == pl.num_programs(0) - 1)
    def finish():
        gain_one, gain_pool = gains_ref[0:1, :], gains_ref[1:2, :]
        small_ref[...] = old_small_ref[...]

        def norm_rows(index, carry):
            part = pl.ds(pl.multiple_of(index * 128, 128), 128)
            grad = dnormed_sum[part, :]
            total = grad if first_pair == 0 else grad + old_dnormed_ref[part, :].astype(f32)
            dnormed_ref[part, :] = total.astype(bf16)
            return carry + jnp.sum(grad * normed_ref[part, :].astype(f32), axis=0, keepdims=True)

        norm_part = lax.fori_loop(0, (rows + 256) // 128, norm_rows, jnp.zeros((1, width), f32))
        norm_part = norm_part / gain_one

        def pool_rows(index, carry):
            norm_part, pool_part = carry
            part = pl.ds(pl.multiple_of(index * 128, 128), 128)
            raw = raw_ref[part, :].astype(f32)
            values = raw * gain_one
            inverse = inverse_rms(values)
            grad = dpooled_sum[part, :]
            back = norm_gradient(values, inverse, gain_pool, grad)
            total = back if first_pair == 0 else back + old_draw_ref[part, :].astype(f32)
            draw_sum[part, :] = total.astype(bf16)
            return (
                norm_part + jnp.sum(back * raw, axis=0, keepdims=True),
                pool_part + jnp.sum(grad * values * inverse, axis=0, keepdims=True),
            )

        norm_part, pool_part = lax.fori_loop(
            0, slots // 128, pool_rows, (norm_part, jnp.zeros((1, width), f32))
        )
        small_ref[0:1, :] += norm_part
        small_ref[1:2, :] += pool_part
        if not last:
            draw_ref[...] = draw_sum[...]
            return
        own_slots = rows // 16
        me = lax.axis_index("y") * lax.axis_size("x") + lax.axis_index("x")
        for hop in range(draw_ref.shape[0]):
            target = lax.rem(me + hop, draw_ref.shape[0])
            draw_ref[hop, :own_slots, :] = draw_sum[
                pl.ds(pl.multiple_of(target * own_slots, own_slots), own_slots), :
            ]
            before = target == me - 1

            @pl.when(before)
            def head():
                draw_ref[hop, own_slots:, :] = dnormed_ref[:128, :]

            @pl.when(jnp.logical_not(before))
            def tail():
                draw_ref[hop, own_slots:, :] = dnormed_ref[rows + 128 :, :]

        rows_of_small = jnp.concatenate([small_ref[...], jnp.zeros((120, width), f32)], axis=0)
        tables = jnp.zeros((width, 128), f32)
        row = lax.broadcasted_iota(i32, (width, 32), 0)
        column = lax.broadcasted_iota(i32, (width, 32), 1)
        for block in range(-(-2 * heads // own_part)):
            chosen = (column == row % own_part + block * own_part).astype(f32)
            shifted = table_ref[...]
            if block:
                shifted = jnp.concatenate(
                    [shifted[:, 128 - 32 * block :], shifted[:, : 128 - 32 * block]], axis=1
                )
            tables = tables + jnp.dot(
                chosen, shifted, precision=highest, preferred_element_type=f32
            )
        store_halves(keep_ref, send_ref, 3, rows_of_small.T, core, part)
        store_halves(keep_ref, send_ref, keep_ref.shape[0] - 1, tables, core, part)


def columns(rows, first):
    return pl.BlockSpec((rows, 128), lambda pair: (0, pair + first))


def of_pair(first, *shape):
    zeros = (0,) * len(shape)
    return pl.BlockSpec((1,) + shape, lambda pair: (pair + first,) + zeros)


def fixed(*shape):
    zeros = (0,) * len(shape)
    return pl.BlockSpec(shape, lambda pair: zeros, pipeline_mode=pl.Buffered(1))


def fixed_out(*shape):
    zeros = (0,) * len(shape)
    return pl.BlockSpec(shape, lambda pair: zeros)


def attention_forward(source_ext, raw_pool, weights, bias, klocal, kglobal, qfeat):
    width = source_ext.shape[1]
    rows = source_ext.shape[0] - 256
    slots = raw_pool.shape[0]
    blocks = rows // 128
    pairs = width // 128
    return pl.pallas_call(
        attend_forward,
        grid=(pairs,),
        in_specs=[
            fixed(rows + 256, width),
            fixed(slots, width),
            pl.BlockSpec((width, 128), lambda pair: (0, 4 * pairs), pipeline_mode=pl.Buffered(1)),
            columns(width, 0),
            columns(width, pairs),
            columns(width, 2 * pairs),
            fixed(256, 128),
            fixed(rows + 256, 128),
            columns(blocks * slots, 0),
            fixed(rows, 128),
        ],
        out_specs=[
            of_pair(0, 256, 256),
            columns(rows, 0),
            of_pair(0, blocks, 256),
            columns(rows, 0),
            columns(rows + 256, 0),
            columns(rows + 256, 0),
            columns(slots, 0),
            columns(slots, 0),
            fixed_out(rows + 256, width),
            fixed_out(8, width),
            fixed_out(width, rows + 256),
            fixed_out(width, slots),
        ],
        out_shape=[
            jax.ShapeDtypeStruct((pairs, 256, 256), f32),
            jax.ShapeDtypeStruct((rows, width), bf16),
            jax.ShapeDtypeStruct((pairs, blocks, 256), f32),
            jax.ShapeDtypeStruct((rows, width), bf16),
            jax.ShapeDtypeStruct((rows + 256, width), bf16),
            jax.ShapeDtypeStruct((rows + 256, width), bf16),
            jax.ShapeDtypeStruct((slots, width), bf16),
            jax.ShapeDtypeStruct((slots, width), bf16),
            jax.ShapeDtypeStruct((rows + 256, width), bf16),
            jax.ShapeDtypeStruct((8, width), f32),
            jax.ShapeDtypeStruct((width, rows + 256), bf16),
            jax.ShapeDtypeStruct((width, slots), bf16),
        ],
        scratch_shapes=[pltpu.VMEM((slots, width), bf16), pltpu.VMEM((128, rows + 256), bf16), pltpu.VMEM((128, slots), bf16)],
        compiler_params=pltpu.CompilerParams(vmem_limit_bytes=48 << 20),
        cost_estimate=pl.CostEstimate(
            flops=30 * rows * (384 + slots) * width, bytes_accessed=24 << 20, transcendentals=0
        ),
        name="attend_forward",
    )(source_ext, raw_pool, weights, weights, weights, weights, bias, klocal, kglobal, qfeat)


def attention_backward(
    first, count, part, queries, grads, keys, values, gkeys, gvalues, normed, turned, pooled, weights, logs, bias, klocal,
    kglobal, qfeat, raw_pool, gains, place, old_small, old_table, old_dnormed, old_draw,
):
    rows, width = queries.shape
    slots = gkeys.shape[0]
    blocks = rows // 128
    pairs = width // 128
    lead = count * (4 if first + count == pairs else 3)
    own_slots = rows // 16
    draw_shape = (slots // own_slots, own_slots + 128, width) if first + count == pairs else (slots, width)
    return pl.pallas_call(
        functools.partial(attend_backward, first + count == pairs, width // 32, part, first),
        grid=(count,),
        in_specs=[
            columns(rows, first),
            columns(rows, first),
            columns(rows + 256, first),
            columns(rows + 256, first),
            columns(slots, first),
            columns(slots, first),
            fixed(rows + 256, width),
            fixed(width, rows + 256),
            fixed(width, slots),
            columns(width, first),
            columns(width, pairs + first),
            columns(width, 2 * pairs + first),
            of_pair(first, blocks, 256),
            of_pair(first, 256, 256),
            fixed(rows + 256, 128),
            columns(blocks * slots, first),
            fixed(rows, 128),
            fixed(slots, width),
            fixed(8, width),
            pl.BlockSpec(memory_space=pltpu.SMEM),
            fixed(8, width),
            fixed(32, 128),
            fixed(rows + 256, width) if first else fixed(8, width),
            fixed(slots, width) if first else fixed(8, width),
        ],
        out_specs=[
            fixed_out(lead, width // 2, 128),
            fixed_out(lead, width // 2, 128),
            fixed_out(rows + 256, width),
            fixed_out(*draw_shape),
            fixed_out(8, width),
            fixed_out(32, 128),
        ],
        out_shape=[
            jax.ShapeDtypeStruct((lead, width // 2, 128), bf16),
            jax.ShapeDtypeStruct((lead, width // 2, 128), bf16),
            jax.ShapeDtypeStruct((rows + 256, width), bf16),
            jax.ShapeDtypeStruct(draw_shape, bf16),
            jax.ShapeDtypeStruct((8, width), f32),
            jax.ShapeDtypeStruct((32, 128), f32),
        ],
        scratch_shapes=[
            pltpu.VMEM((rows + 256, width), f32),
            pltpu.VMEM((slots, width), f32),
            pltpu.VMEM((slots, width), bf16),
            pltpu.VMEM((128, rows + 256), bf16),
            pltpu.VMEM((128, slots), bf16),
            pltpu.VMEM((rows, 128), bf16),
            pltpu.VMEM((rows + 256, 128), f32),
            pltpu.VMEM((rows + 256, 128), f32),
            pltpu.VMEM((slots, 128), f32),
            pltpu.VMEM((slots, 128), f32),
            pltpu.VMEM((256, 256), f32),
            pltpu.VMEM((slots, 128), f32),
        ],
        compiler_params=pltpu.CompilerParams(vmem_limit_bytes=48 << 20),
        cost_estimate=pl.CostEstimate(
            flops=60 * rows * (384 + slots) * 128 * count, bytes_accessed=count << 22, transcendentals=0
        ),
        name="attend_backward",
    )(
        queries, grads, keys, values, gkeys, gvalues, normed, turned, pooled, weights, weights, weights, logs, bias, klocal,
        kglobal, qfeat, raw_pool, gains, place, old_small, old_table, old_dnormed, old_draw,
    )


def interleave(held, other, core):
    held, other = held.astype(f32), other.astype(f32)
    both = jnp.stack([jnp.where(core == 0, held, other), jnp.where(core == 0, other, held)], axis=1)
    return both.reshape(-1, both.shape[-1])


def fold_rows(tall):
    rows, width = tall.shape[1:]
    return jnp.concatenate(
        [
            jnp.concatenate(
                [tall[:, r : r + 8, c : c + 256] for r in range(0, rows, 8)], axis=2
            )
            for c in range(0, width, 256)
        ],
        axis=1,
    )


unfold_rows = fold_rows


def pack_weights(wq_ref, wk_ref, wv_ref, wo_ref, gains_ref, gate_ref, up_ref, down_ref, first_ref, second_ref):
    width = wq_ref.shape[1]
    for index, weight_ref in enumerate((wq_ref, wk_ref, wv_ref, wo_ref)):
        first_ref[:, index * width : (index + 1) * width] = weight_ref[...]
    first_ref[:, 4 * width :] = gains_ref[...]
    if second_ref.shape[1] > 128:
        hidden = gate_ref.shape[1]
        second_ref[:, :hidden] = gate_ref[...]
        second_ref[:, hidden : 2 * hidden] = up_ref[...]
        second_ref[:, 2 * hidden :] = fold_rows(down_ref[...].astype(f32)[None])[0].astype(bf16)


def pack_tokens(source_ref, keep_ref, marks_ref, shared_ref):
    width = source_ref.shape[1]
    slots = source_ref.shape[0] // 16
    for slot in range(0, slots, 16):
        rows = slice(slot * 16, slot * 16 + 256)
        values = source_ref[rows, :].astype(f32)
        values = values * (inverse_rms(values) * keep_ref[rows, :])
        shared_ref[0, slot : slot + 16, :] = jnp.sum(values.reshape(16, 16, width), axis=1).astype(bf16)
    marks = marks_ref[...].astype(f32)
    rest = jnp.zeros((marks.shape[0], width - 128), f32)
    count = slots + marks.shape[0]
    shared_ref[0, slots:count, :] = jnp.concatenate([marks, rest], axis=1).astype(bf16)
    for target in range(1, shared_ref.shape[0]):
        shared_ref[target, :count, :] = shared_ref[0, :count, :]
    for target in range(shared_ref.shape[0]):
        before = target == lax.axis_index("y") * lax.axis_size("x") + lax.axis_index("x") - 1

        @pl.when(before)
        def head():
            shared_ref[target, count:, :] = source_ref[:128, :]

        @pl.when(jnp.logical_not(before))
        def tail():
            shared_ref[target, count:, :] = source_ref[source_ref.shape[0] - 128 :, :]


def pack_all(wq, wk, wv, wo, gains, gate, up, down, aligned):
    part, width = wq.shape
    return pl.pallas_call(
        pack_weights,
        out_shape=[
            jax.ShapeDtypeStruct((part, 4 * width + 128), bf16),
            jax.ShapeDtypeStruct((part, 3 * gate.shape[1] if aligned else 128), bf16),
        ],
        compiler_params=pltpu.CompilerParams(vmem_limit_bytes=60 << 20),
        name="pack_weights",
    )(wq, wk, wv, wo, gains, gate, up, down)


def pack_shared(source, keep, marks, count):
    rows, width = source.shape
    return pl.pallas_call(
        pack_tokens,
        out_shape=jax.ShapeDtypeStruct((count, rows // 16 + marks.shape[0] + 128, width), bf16),
        compiler_params=pltpu.CompilerParams(vmem_limit_bytes=60 << 20),
        name="pack_tokens",
    )(source, keep, marks)


def feed_forward(
    source_ref, mixture_ref, wo_ref, gains_ref, cot_ref, gate_held, gate_other, up_held, up_other, down_held, down_other,
    place_ref,
    out_ref, middle_grad_ref, dmixture_ref, dgain_ref, keep_out, send_out, keep_wide, send_wide, keep_down, send_down,
    middle, normed, turned, out_sum, grad_sum, product, gate_low, lift_low, wg_ref, wu_ref, wd_ref,
):
    rows, width = source_ref.shape
    part_rows = 256
    parts = rows // part_rows
    gain = gains_ref[2:3, :]
    core = place_ref[0]
    wg_ref[...] = interleave(gate_held[...], gate_other[...], core).astype(bf16)
    wu_ref[...] = interleave(up_held[...], up_other[...], core).astype(bf16)
    wd_ref[...] = interleave(
        unfold_rows(down_held[...].astype(f32)), unfold_rows(down_other[...].astype(f32)), core
    ).astype(bf16)

    @pl.when(pl.program_id(0) == 0)
    def start():
        def norm_rows(index, carry):
            part = pl.ds(pl.multiple_of(index * 256, 256), 256)
            values = source_ref[part, :].astype(f32) + dot_nn(mixture_ref[part, :], wo_ref[...])
            middle[part, :] = values
            low = (values * inverse_rms(values) * gain).astype(bf16)
            normed[part, :] = low
            turned[:, part] = low.T
            return carry

        lax.fori_loop(0, rows // 256, norm_rows, 0, unroll=True)
        out_sum[...] = jnp.zeros_like(out_sum)
        grad_sum[...] = jnp.zeros_like(grad_sum)

    root = 0.7978845608028654
    for index in range(parts):
        part = slice(index * part_rows, (index + 1) * part_rows)
        low = normed[part, :]
        gate_pre = dot_nn(low, wg_ref[...])
        lift_pre = dot_nn(low, wu_ref[...])
        grad = dot_nt(cot_ref[part, :], wd_ref[...])
        square = gate_pre * gate_pre
        bent = jnp.tanh(gate_pre * (root + (root * 0.044715) * square))
        half = 0.5 + 0.5 * bent
        gelu = gate_pre * half
        slope = half + gelu * (1.0 - bent) * (root + (3 * root * 0.044715) * square)
        product[part, :] = (gelu * lift_pre).astype(bf16)
        lift_low[part, :] = (grad * gelu).astype(bf16)
        gate_low[part, :] = (grad * lift_pre * slope).astype(bf16)
        out_sum[part, :] += dot_nn(product[part, :], wd_ref[...])
        grad_sum[part, :] += dot_nt(gate_low[part, :], wg_ref[...]) + dot_nt(
            lift_low[part, :], wu_ref[...]
        )
    wide_part, down_part = width // 32, down_held.shape[1] * down_held.shape[2] // width
    store_halves(keep_wide, send_wide, 0, dot_nn(turned[...], gate_low[...]), core, wide_part)
    store_halves(keep_wide, send_wide, 1, dot_nn(turned[...], lift_low[...]), core, wide_part)
    value = dot_nn(product[...].T, cot_ref[...]).reshape(-1, 2, down_part, width)
    first, second = value[:, 0], value[:, 1]
    for half_ref, chosen in (
        (keep_down, jnp.where(core == 0, first, second)),
        (send_down, jnp.where(core == 0, second, first)),
    ):
        folded = fold_rows(chosen)
        folded = folded.reshape(-1, folded.shape[2]).astype(bf16)
        half_ref[0], half_ref[1] = folded[:, : folded.shape[1] // 2], folded[:, folded.shape[1] // 2 :]

    @pl.when(pl.program_id(0) == pl.num_programs(0) - 1)
    def finish():
        dgain_ref[...] = jnp.zeros_like(dgain_ref)

        def back_rows(index, carry):
            part = pl.ds(pl.multiple_of(index * 256, 256), 256)
            values = middle[part, :]
            out_ref[part, :] = (values + out_sum[part, :]).astype(bf16)
            inverse = inverse_rms(values)
            grad = grad_sum[part, :]
            dgain_ref[2:3, :] += jnp.sum(grad * values * inverse, axis=0, keepdims=True)
            total = cot_ref[part, :].astype(f32) + norm_gradient(values, inverse, gain, grad)
            middle_grad_ref[part, :] = total
            low = total.astype(bf16)
            normed[part, :] = low
            dmixture_ref[part, :] = dot_nt(low, wo_ref[...]).astype(bf16)
            turned[:, part] = mixture_ref[part, :].T
            return carry

        lax.fori_loop(0, rows // 256, back_rows, 0, unroll=True)
        for side in range(2):
            half = slice(side * width // 2, (side + 1) * width // 2)
            store_halves(keep_out, send_out, side, dot_nn(turned[...], normed[:, half]), core, width // 32)


def feed_forward_both(source, mixture, weights, gains, cotangent, held, other, place):
    rows, width = source.shape
    groups, part, total = held.shape
    hidden = total // 3
    tile = 512
    tiles = hidden // tile
    step_groups = groups // tiles
    gate_spec = pl.BlockSpec((groups, part, tile), lambda step: (0, 0, step))
    up_spec = pl.BlockSpec((groups, part, tile), lambda step: (0, 0, step + tiles))
    down_spec = pl.BlockSpec((step_groups, part, hidden), lambda step: (step, 0, 2))
    wide_spec = pl.BlockSpec((2, width // 2, tile), lambda step: (0, 0, step))
    fold_spec = pl.BlockSpec((2, step_groups * part, hidden // 2), lambda step: (0, step, 0))
    out_spec = fixed_out(2, width // 2, width // 2)
    return pl.pallas_call(
        feed_forward,
        grid=(tiles,),
        in_specs=[
            fixed(rows, width),
            fixed(rows, width),
            pl.BlockSpec((width, width), lambda step: (0, 3), pipeline_mode=pl.Buffered(1)),
            fixed(8, width),
            fixed(rows, width),
            gate_spec,
            gate_spec,
            up_spec,
            up_spec,
            down_spec,
            down_spec,
            pl.BlockSpec(memory_space=pltpu.SMEM),
        ],
        out_specs=[
            fixed_out(rows, width),
            fixed_out(rows, width),
            fixed_out(rows, width),
            fixed_out(8, width),
            out_spec,
            out_spec,
            wide_spec,
            wide_spec,
            fold_spec,
            fold_spec,
        ],
        out_shape=[
            jax.ShapeDtypeStruct((rows, width), bf16),
            jax.ShapeDtypeStruct((rows, width), f32),
            jax.ShapeDtypeStruct((rows, width), bf16),
            jax.ShapeDtypeStruct((8, width), f32),
            jax.ShapeDtypeStruct((2, width // 2, width // 2), bf16),
            jax.ShapeDtypeStruct((2, width // 2, width // 2), bf16),
            jax.ShapeDtypeStruct((2, width // 2, hidden), bf16),
            jax.ShapeDtypeStruct((2, width // 2, hidden), bf16),
            jax.ShapeDtypeStruct((2, width // 2, hidden // 2), bf16),
            jax.ShapeDtypeStruct((2, width // 2, hidden // 2), bf16),
        ],
        scratch_shapes=[
            pltpu.VMEM((rows, width), f32),
            pltpu.VMEM((rows, width), bf16),
            pltpu.VMEM((width, rows), bf16),
            pltpu.VMEM((rows, width), f32),
            pltpu.VMEM((rows, width), f32),
            pltpu.VMEM((rows, tile), bf16),
            pltpu.VMEM((rows, tile), bf16),
            pltpu.VMEM((rows, tile), bf16),
            pltpu.VMEM((width, tile), bf16),
            pltpu.VMEM((width, tile), bf16),
            pltpu.VMEM((tile, width), bf16),
        ],
        compiler_params=pltpu.CompilerParams(vmem_limit_bytes=60 << 20),
        cost_estimate=pl.CostEstimate(
            flops=20 * rows * width * hidden, bytes_accessed=40 << 20, transcendentals=0
        ),
        name="feed_forward",
    )(source, mixture, weights, gains, cotangent, held, other, held, other, held, other, place)


def source_gradient(source_ref, keep_ref, middle_grad_ref, gains_ref, dnormed_ref, payload_ref, *refs):
    step, steps = pl.program_id(0), pl.num_programs(0)
    received, out_ref = refs[:-1], refs[-1]
    seq_count = len(received) + 1
    own_slots = payload_ref.shape[1] - 128
    rows, width = source_ref.shape
    slots = pl.ds(pl.multiple_of(step * (rows // 16), rows // 16), rows // 16)
    pooled = payload_ref[0, slots, :].astype(f32)
    for other_ref in received:
        pooled = pooled + other_ref[slots, :].astype(f32)
    pooled = jnp.broadcast_to(pooled[:, None, :], (rows // 16, 16, width)).reshape(rows, width)
    own = pl.ds(pl.multiple_of(128 + step * rows, 128), rows)
    grad = dnormed_ref[own, :].astype(f32) + pooled * keep_ref[...]
    me = lax.axis_index("y") * lax.axis_size("x") + lax.axis_index("x")
    before = (step == 0) & (me > 0)
    after = (step == steps - 1) & (me < seq_count - 1)
    head = received[0][own_slots:, :].astype(f32)
    tail = received[-1][own_slots:, :].astype(f32)
    edges = [jnp.where(before, head, 0.0), jnp.zeros((rows - 256, width), f32), jnp.where(after, tail, 0.0)]
    grad = grad + jnp.concatenate([edge for edge in edges if edge.shape[0]], axis=0)
    values = source_ref[...].astype(f32)
    out_ref[...] = middle_grad_ref[...] + norm_gradient(values, inverse_rms(values), gains_ref[0:1, :], grad)


def input_gradient(source, keep, middle_grad, gains, dnormed, payload, received):
    rows, width = source.shape
    tile = 256
    row_spec = pl.BlockSpec((tile, width), lambda step: (step, 0))
    return pl.pallas_call(
        source_gradient,
        grid=(rows // tile,),
        in_specs=[
            row_spec,
            pl.BlockSpec((tile, 1), lambda step: (step, 0)),
            row_spec,
            fixed(8, width),
            fixed(*dnormed.shape),
            pl.BlockSpec((1,) + payload.shape[1:], lambda step: (0, 0, 0), pipeline_mode=pl.Buffered(1)),
        ]
        + [fixed(*other.shape) for other in received],
        out_specs=row_spec,
        out_shape=jax.ShapeDtypeStruct((rows, width), f32),
        compiler_params=pltpu.CompilerParams(vmem_limit_bytes=60 << 20),
        cost_estimate=pl.CostEstimate(
            flops=20 * rows * width, bytes_accessed=14 << 20, transcendentals=0
        ),
        name="source_gradient",
    )(source, keep, middle_grad, gains, dnormed, payload, *received)


def near_offsets(local_bias):
    heads, buckets = local_bias.shape
    offset = (jnp.arange(256, dtype=i32) + 128) % 256 - 128
    table = (bucket_of(offset)[:, None] == jnp.arange(buckets, dtype=i32)).astype(f32)
    chosen = jnp.einsum("ob,hb->oh", table, local_bias, precision=highest)
    chosen = jnp.where((offset == -128)[:, None], never, chosen)
    return jnp.pad(chosen, ((0, 0), (0, 128 - heads)))


def far_features(global_bias, slot_segments, slot_live, first_slot, blocks):
    heads, buckets = global_bias.shape
    pairs = heads // 2
    slots = slot_segments.shape[0]
    wide = 8 * buckets + 8
    shape = (blocks * slots, wide)
    row = lax.broadcasted_iota(i32, shape, 0)
    column = lax.broadcasted_iota(i32, shape, 1)
    slot = row % slots
    query_slot = first_slot + (row // slots) * 8 + column // buckets
    code = jnp.tile(jnp.where(slot_live, slot_segments, 3), blocks)[:, None]
    picks = jnp.where(
        column < 8 * buckets,
        bucket_of(slot - query_slot) == column % buckets,
        code == column - 8 * buckets,
    ).astype(bf16)
    high = lax.reduce_precision(global_bias, 8, 7)
    middle = lax.reduce_precision(global_bias - high, 8, 7)
    lowest = lax.reduce_precision(global_bias - high - middle, 8, 7)
    parts = jnp.stack([high, middle, lowest]).reshape(3, pairs, 2, buckets)
    parts = parts.transpose(3, 1, 0, 2)
    same = jnp.eye(8, dtype=f32)[:, None, None, None, None, :]
    table = (parts[None, :, :, :, :, None] * same).reshape(8 * buckets, pairs, 48)
    table = jnp.pad(table, ((0, 8), (0, 0), (0, 80)))
    shape = (wide, 1, 128)
    lane = lax.broadcasted_iota(i32, shape, 2) - 48
    code_row = lax.broadcasted_iota(i32, shape, 0) - 8 * buckets
    barred = (code_row >= 0) & (lane >= 0) & (lane < 3) & (lane != code_row)
    table = jnp.where(barred, never, table).astype(bf16).reshape(wide, pairs * 128)
    return jnp.dot(picks, table, preferred_element_type=f32).astype(bf16)


def near_features(segments_ext, valid_ext):
    lane = lax.broadcasted_iota(i32, (segments_ext.shape[0], 128), 1)
    allowed = (segments_ext[:, None] == lane - 48) & (valid_ext[:, None] > 0)
    return jnp.where((lane >= 48) & (lane < 51) & ~allowed, never, 0.0).astype(bf16)


def query_features(own_segments):
    lane = lax.broadcasted_iota(i32, (own_segments.shape[0], 128), 1)
    return (own_segments[:, None] == lane - 48).astype(bf16)


def pick(values, index, dim):
    return lax.dynamic_index_in_dim(values, index, dim, keepdims=False)


def ring(size, hop):
    return [(i, (i + hop) % size) for i in range(size)]


def add_up(parts):
    if len(parts) == 1:
        return parts[0]
    return sum((part.astype(f32) for part in parts[1:]), parts[0].astype(f32))


def split_stage(side, labels, axis, join):
    size, me = lax.axis_size(axis), lax.axis_index(axis)
    dim = labels.index(axis) - len(labels) - 2 + side[0][0].ndim
    chosen = []
    for hop in range(size):
        pieces = [
            add_up([pick(part, (me + hop) % size, dim) for part in piece]).astype(bf16) for piece in side
        ]
        chosen.append(pieces[0] if len(pieces) == 1 else jnp.concatenate(pieces, axis=join))
    return chosen[1:], chosen[0]


def send_all(axis, pieces):
    size = lax.axis_size(axis)
    return [lax.ppermute(piece, axis, ring(size, hop + 1)) for hop, piece in enumerate(pieces)]


def place_stage(values, pieces, axis, dim):
    size, me = lax.axis_size(axis), lax.axis_index(axis)
    shape = values.shape[:dim] + (size,) + values.shape[dim:]
    out = lax.dynamic_update_index_in_dim(jnp.zeros(shape, values.dtype), values, me, dim)
    for hop, piece in enumerate(pieces):
        out = lax.dynamic_update_index_in_dim(out, piece, (me - hop - 1) % size, dim)
    return out


def half_of(width):
    return (width // 256) * 128


def scatter_steps(sides, labels, stages, join):
    labels = [list(labels) for _ in sides]
    for axes in stages:
        if axes == ("all z",):
            merged = [add_up(piece).astype(bf16) for side in sides for piece in side]
            merged = yield jnp.concatenate(merged, axis=join)
            dim = merged.ndim - 3
            got = yield lax.all_to_all(merged, "z", dim, dim, tiled=True)
            return jnp.sum(got.astype(f32), axis=dim)
        if len(axes) < len(sides):
            sides, labels = [[piece for side in sides for piece in side]], labels[:1]
        split = [split_stage(side, names, axis, join) for side, names, axis in zip(sides, labels, axes)]
        sends = yield [send for send, _ in split]
        gots = yield [send_all(axis, send) for axis, send in zip(axes, sends)]
        sides = [[[keep] + got] for (_, keep), got in zip(split, gots)]
        for names, axis in zip(labels, axes):
            names.remove(axis)
    return add_up(sides[0][0])


across = (("x", "y"), ("y", "x"))


stages = (("x", "y"), ("y", "x"), ("z",))
labels = ("y", "x", "z")


def core_steps(pairs, part):
    y, x, z, _ = (lax.axis_size(axis) for axis in everyone)
    keeps, sends = zip(*pairs)
    if part != keeps[0].shape[1] // 16:
        keeps, sends = zip(*(regroup(keep, send, part) for keep, send in pairs))
    sends = yield sends
    gots = yield [lax.ppermute(send, "core", ring(2, 1)) for send in sends]
    sides = [[], []]
    for keep, got in zip(keeps, gots):
        lead, _, width = keep.shape
        held, new = (values.reshape(lead, y, x, z, part, width) for values in (keep, got))
        sides[0].append([held[: lead // 2], new[: lead // 2]])
        sides[1].append([held[lead // 2 :], new[lead // 2 :]])
    return sides


def sum_rows(pairs, part, join):
    sides = yield from core_steps(pairs, part)
    return (yield from scatter_steps(sides, labels, across + (("all z",),), join))


def regroup(keep, send, part):
    lead, half, width = keep.shape
    both = jnp.stack([keep.reshape(lead, 16, -1, width), send.reshape(lead, 16, -1, width)], axis=2)
    both = both.reshape(lead, half // part, 2, part, width)
    me = lax.axis_index("core")
    return tuple(pick(both, index, 2).reshape(keep.shape) for index in (me, 1 - me))


def all_rows(shard, last):
    width = shard.shape[1]
    half = half_of(width)
    others = lax.axis_size("z") - 1
    shard = yield shard
    pieces = yield send_all("z", [shard] * others)
    values = place_stage(shard, pieces, "z", 0)
    left, right = values[..., :half], values[..., half:]
    for left_axis, right_axis in across:
        dim = 1 if right_axis == "x" else 0
        left, right = yield left, right
        got = yield (
            send_all(left_axis, [left] * (lax.axis_size(left_axis) - 1)),
            send_all(right_axis, [right] * (lax.axis_size(right_axis) - 1)),
        )
        left = place_stage(left, got[0], left_axis, 0)
        right = place_stage(right, got[1], right_axis, dim)
    values = yield jnp.concatenate([left, right], axis=-1)
    got = yield send_all("core", [values])
    if not last:
        return values.reshape(-1, *values.shape[-2:]), got[0].reshape(-1, *values.shape[-2:])
    return place_stage(values, got, "core", 3).reshape(-1, width)


class Chain:
    def __init__(self, steps):
        self.steps = steps
        self.value = next(steps)
        self.done = False

    def advance(self):
        try:
            self.value = self.steps.send(self.value)
        except StopIteration as end:
            self.value, self.done = end.value, True


def phase(operand, work, launch=(), collect=None):
    collect = launch if collect is None else collect
    values, operand = lax.optimization_barrier(([chain.value for chain in launch], operand))
    for chain, value in zip(launch, values):
        chain.value = value
        chain.advance()
    result = work(operand)
    values, result = lax.optimization_barrier(([chain.value for chain in collect], result))
    for chain, value in zip(collect, values):
        chain.value = value
        chain.advance()
    return result


def on_device(
    hidden_state,
    segment_ids,
    valid_mask,
    cotangent,
    norm_gain,
    pool_gain,
    feed_gain,
    query_weight,
    key_weight,
    value_weight,
    output_weight,
    local_bias,
    global_bias,
    gate_weight,
    up_weight,
    down_weight,
):
    model_width = hidden_state.shape[2]
    hidden = gate_weight.shape[1]
    tok_rows = hidden_state.shape[1]
    own_part = norm_gain.shape[0]
    buckets = local_bias.shape[1]
    pairs = local_bias.shape[0] // 2
    blocks = tok_rows // 128
    own_slots = tok_rows // 16
    seq_count = lax.axis_size(seq)
    slot_count = own_slots * seq_count
    row_start = lax.axis_index(seq) * tok_rows
    first_slot = row_start // 16
    source = hidden_state[0]
    upstream = cotangent[0]
    own_segments = segment_ids[0]
    valid_float = valid_mask[0].astype(f32)

    aligned = own_part * 32 == model_width
    place = jnp.stack([lax.axis_index("core"), first_slot]).astype(i32)
    gain_columns = jnp.pad(jnp.stack([norm_gain, pool_gain, feed_gain], axis=1), ((0, 0), (0, 125)))
    marks = jnp.concatenate([segment_ids.reshape(-1, 128), valid_mask.reshape(-1, 128)])
    packed, packed_second = pack_all(
        query_weight, key_weight, value_weight, output_weight, gain_columns, gate_weight, up_weight, down_weight, aligned
    )
    first = Chain(all_rows(packed, True))
    later = [Chain(all_rows(packed_second, False))] if aligned else []

    def share(operands):
        shared = pack_shared(*operands, seq_count)
        return lax.all_to_all(shared, seq, 0, 0, tiled=True)

    held = []
    phase(
        (source, valid_float[:, None], marks), lambda operands: held.append(share(operands)), [first] + later, [first]
    )

    def near_parts(operands):
        shared, local_bias = operands
        me = lax.axis_index(seq)
        edge = own_slots + marks.shape[0]
        raw_pool = shared[:, :own_slots].reshape(slot_count, model_width)
        all_marks = shared[:, own_slots:edge, :128].astype(i32).reshape(seq_count, 2, tok_rows)
        before, after = (
            jnp.where((near >= 0) & (near < seq_count), pick(shared[:, edge:], jnp.clip(near, 0, seq_count - 1), 0), 0)
            for near in (me - 1, me + 1)
        )
        all_segments, all_valid = all_marks[:, 0].reshape(-1), all_marks[:, 1].reshape(-1)
        slot_segments = all_segments.reshape(slot_count, 16)[:, 0]
        slot_live = jnp.sum(all_valid.reshape(slot_count, 16), axis=1) > 0
        segments_ext = lax.dynamic_slice_in_dim(
            jnp.pad(all_segments, 128, constant_values=-1), row_start, tok_rows + 256
        )
        valid_ext = lax.dynamic_slice_in_dim(jnp.pad(all_valid, 128), row_start, tok_rows + 256)
        feat_near = near_features(segments_ext, valid_ext)
        source_ext = jnp.concatenate([before, source, after], axis=0)
        return raw_pool, slot_segments, slot_live, feat_near, near_offsets(local_bias), source_ext

    raw_pool, slot_segments, slot_live, feat_near, bias_near, source_ext = phase(
        (held[0], local_bias), near_parts, [first], [first] + later
    )
    feat_query = query_features(own_segments)
    feat_far = phase(
        (global_bias, slot_segments, slot_live),
        lambda operands: far_features(*operands, first_slot, blocks),
        [first],
        [],
    )
    feat_far = phase(feat_far, lambda operands: operands, later, [first])
    phase((), lambda nothing: nothing, [first], [first] + later)
    weights = first.value

    bias, mixture, logs, queries, keys, vals, gkeys, gvals, normed, gains, turned, pooled = phase(
        (source_ext, raw_pool, weights, bias_near, feat_near, feat_far, feat_query),
        lambda operands: attention_forward(*operands),
        later,
    )
    phase((), lambda nothing: nothing, later)
    if aligned:
        held, other = later[0].value
        kernel_place = place
    else:
        wide = lax.all_gather(jnp.concatenate([gate_weight, up_weight], axis=1), everyone, axis=0, tiled=True)
        tall = lax.all_gather(down_weight, everyone, axis=0, tiled=True)
        tall = fold_rows(tall.reshape(32, -1, model_width))
        both = jnp.concatenate([wide.reshape(32, -1, 2 * hidden), tall], axis=2)
        both = both.reshape(16, 2, -1, 3 * hidden)
        held, other = both[:, 0], both[:, 1]
        kernel_place = place * jnp.array([0, 1], i32)
    layer_output, middle_grad, mixture_grad, small, out_keep, out_send, wide_keep, wide_send, down_keep, down_send = (
        feed_forward_both(source, mixture, weights, gains, upstream, held, other, kernel_place)
    )
    rest = []
    if aligned:
        pieces = [(wide_keep, wide_send), (down_keep, down_send), (out_keep, out_send)]
        rest = [Chain(sum_rows(pieces, own_part, -1))]
    table = jnp.zeros((32, 128), f32)
    count = pairs // calls
    waiting, started = [], []
    dnormed, draw = gains, gains
    keep_column = valid_float[:, None]
    for call in range(calls):
        keep, send, dnormed, draw, small, table = phase(
            (mixture_grad, small, table, dnormed, draw),
            lambda operands: attention_backward(
                call * count, count, own_part, queries, operands[0], keys, vals, gkeys, gvals, normed, turned, pooled, weights,
                logs, bias, feat_near, feat_far, feat_query, raw_pool, gains, kernel_place, *operands[1:],
            ),
            rest + started,
        )
        waiting.append((keep, send))
        if call > 0:
            started.append(Chain(core_steps(waiting, own_part)))
            waiting = []

    def return_rows(payload):
        return [lax.ppermute(payload[hop], seq, ring(seq_count, hop)) for hop in range(1, seq_count)]

    held = []
    phase(draw, lambda operands: held.append(return_rows(operands)), started[1:] + rest, started[1:])
    operands = held[0]
    sides = [sum((chain.value[side] for chain in started), []) for side in range(2)]
    last = Chain(scatter_steps(sides, labels, stages, 0))
    operands = phase(operands, lambda operands: operands, [last])
    input_delta = phase(
        operands,
        lambda received: input_gradient(source, keep_column, middle_grad, gains, dnormed, draw, received),
        [last],
        rest + [last],
    )
    phase((), lambda nothing: nothing, [last])
    total = last.value
    half = total.shape[0] // 2
    sides = [total[:half], total[half:]]
    extra = jnp.concatenate([side[half - 1] for side in sides], axis=-1)
    blocks_of_table = -(-4 * pairs // own_part)
    tables = extra[:, 128 : 128 + buckets * blocks_of_table].reshape(own_part, blocks_of_table, buckets)
    tables = tables.transpose(1, 0, 2).reshape((2,) + local_bias.shape)
    query_delta, key_delta, value_delta = (
        jnp.concatenate(
            [sides[pair % count][3 * (pair // count) + index] for pair in range(pairs)],
            axis=-1,
        )
        for index in range(3)
    )
    if aligned:
        total = rest[0].value[0]
        side, fold, half = total.shape[1] // 2, hidden // 2, model_width // 2
        left, right = total[:, :side], total[:, side:]
        gate_delta, up_delta = left[:, :hidden], right[:, :hidden]
        tall = jnp.concatenate([left[:, hidden : hidden + fold], right[:, hidden : hidden + fold]], axis=1)
        down_delta = unfold_rows(tall[None])[0]
        output_delta = jnp.concatenate([left[:, hidden + fold :], right[:, hidden + fold :]], axis=1)
    else:

        def whole_rows(keep, send):
            width = keep.shape[-1]
            both = jnp.stack([keep.reshape(16, -1, width), send.reshape(16, -1, width)], axis=1)
            return both.reshape(32, -1, width)

        def join(halves):
            return jnp.concatenate([halves[0], halves[1]], axis=-1)

        def scatter(grads):
            grads = grads.reshape(-1, grads.shape[-1])
            return lax.psum_scatter(grads, everyone, scatter_dimension=0, tiled=True).astype(f32)

        gate_delta = scatter(whole_rows(wide_keep[0], wide_send[0]))
        up_delta = scatter(whole_rows(wide_keep[1], wide_send[1]))
        output_delta = scatter(whole_rows(join(out_keep), join(out_send)))
        down_delta = scatter(unfold_rows(whole_rows(join(down_keep), join(down_send))))
    return (
        layer_output[None],
        input_delta[None],
        extra[:, 0],
        extra[:, 1],
        extra[:, 2],
        query_delta,
        key_delta,
        value_delta,
        output_delta,
        tables[0],
        tables[1],
        gate_delta,
        up_delta,
        down_delta,
    )


def solution(mesh):
    seq_size, batch_size = mesh.shape["seq"], mesh.shape["batch"]
    chips = Mesh(mesh.devices.reshape(2, seq_size // 2, batch_size // 2, 2), everyone)
    tokens = P(batch, seq, None)
    marks = P(batch, seq)
    row = P(everyone)
    matrix = P(everyone, None)
    whole = P()
    return jax.shard_map(
        on_device,
        mesh=chips,
        in_specs=(tokens, marks, marks, tokens, row, row, row)
        + (matrix,) * 4
        + (whole,) * 2
        + (matrix,) * 3,
        out_specs=(tokens, tokens, row, row, row)
        + (matrix,) * 4
        + (whole,) * 2
        + (matrix,) * 3,
        check_vma=False,
    )
```

```python
import functools

import jax
import jax.numpy as jnp
from jax import lax
from jax.experimental import pallas as pl
from jax.experimental.pallas import tpu as pltpu
from jax.sharding import Mesh
from jax.sharding import PartitionSpec as P

epsilon = 1e-06
boundaries = (12, 16, 23, 32, 46, 64, 91)
never = -1e30
seq = ("y", "x")
batch = ("z", "core")
everyone = seq + batch
bf16 = jnp.bfloat16
f32 = jnp.float32
i32 = jnp.int32
highest = lax.Precision.HIGHEST
calls = 3


def bucket_of(offset):
    distance = jnp.abs(offset)
    far_part = 8 + sum(((distance >= boundary).astype(i32) for boundary in boundaries))
    return 16 * (offset > 0).astype(i32) + jnp.where(distance < 8, distance, far_part)


def dot_nt(left, right):
    return lax.dot_general(left, right, (((1,), (1,)), ((), ())), preferred_element_type=f32)


def dot_nn(left, right):
    return lax.dot_general(left, right, (((1,), (0,)), ((), ())), preferred_element_type=f32)


def inverse_rms(values):
    return lax.rsqrt(jnp.mean(values * values, axis=-1, keepdims=True) + epsilon)


def norm_gradient(values, inverse, gain, grad):
    weighted = grad * gain
    mean = jnp.mean(weighted * values, axis=-1, keepdims=True)
    return inverse * weighted - (inverse * inverse * inverse * mean) * values


def store_halves(keep_ref, send_ref, index, value, core, part):
    rows, width = value.shape
    value = value.reshape(rows // (2 * part), 2, part, width)
    first, second = value[:, 0].reshape(rows // 2, width), value[:, 1].reshape(rows // 2, width)
    keep_ref[index] = jnp.where(core == 0, first, second).astype(bf16)
    send_ref[index] = jnp.where(core == 0, second, first).astype(bf16)


def stack_heads(rows):
    lane = lax.broadcasted_iota(i32, rows.shape, 1)
    zero = jnp.zeros_like(rows)
    return jnp.concatenate(
        [jnp.where(lane < 64, rows, zero), jnp.where(lane < 64, zero, rows)], axis=0
    )


def unstack_heads(wide):
    row = lax.broadcasted_iota(i32, (128, 128), 0)
    return jnp.where(row < 64, wide[:, :128], wide[:, 128:]).T


def upper_band():
    key = lax.broadcasted_iota(i32, (128, 256), 0)
    query = lax.broadcasted_iota(i32, (128, 256), 1) & 127
    return key > query


def spread_band(upper, own, merged):
    zero = jnp.zeros_like(merged)
    return jnp.concatenate(
        [jnp.where(upper, merged, zero), own, jnp.where(upper, zero, merged)], axis=0
    ).astype(bf16)


def window_of(block):
    return pl.ds(pl.multiple_of(block * 128, 128), 384)


def rows_of(block):
    return pl.ds(pl.multiple_of(block * 128, 128), 128)


def slot_lanes():
    row = lax.broadcasted_iota(i32, (256, 128), 0)
    lane = lax.broadcasted_iota(i32, (256, 128), 1)
    hit = (lane < 48) & ((lane & 15) == (row // 128) * 8 + (row % 128) // 16)
    return hit.astype(f32).astype(bf16)


def block_scores(block, upper, on_slot, query_two, key_ref, gkey_ref, bias_ref, klocal_ref, kglobal_ref, qfeat_ref):
    slots = gkey_ref.shape[0]
    window = window_of(block)
    segment_lanes = qfeat_ref[rows_of(block), :]
    features = jnp.concatenate([segment_lanes, segment_lanes], axis=0) + on_slot
    query_wide = jnp.concatenate([query_two, features], axis=1)
    key_wide = jnp.concatenate([key_ref[window, :], klocal_ref[window, :]], axis=1)
    local = dot_nt(key_wide, query_wide)
    own = local[128:256] + bias_ref[0, 0:128]
    merged = jnp.where(upper, local[0:128], local[256:384]) + bias_ref[0, 128:256]
    far_rows = pl.ds(pl.multiple_of(block * slots, 128), slots)
    gkey_wide = jnp.concatenate([gkey_ref[...], kglobal_ref[far_rows, :]], axis=1)
    return own, merged, dot_nt(gkey_wide, query_wide)


def attend_forward(
    source_ref, raw_ref, gain_ref, wq_ref, wk_ref, wv_ref, offsets_ref, klocal_ref, kglobal_ref, qfeat_ref,
    bias_ref, out_ref, log_ref, query_ref, key_ref, value_ref, gkey_ref, gvalue_ref, normed_ref, gains_ref,
    normed_turned, pooled_turned, pooled_ref, value_turned, gvalue_turned,
):
    rows = query_ref.shape[0]
    slots = gkey_ref.shape[0]

    @pl.when(pl.program_id(0) == 0)
    def start():
        turned = gain_ref[...].astype(f32).T
        gains_ref[...] = turned[0:8]
        gain_one, gain_pool = turned[0:1], turned[1:2]

        def norm_rows(index, carry):
            part = pl.ds(pl.multiple_of(index * 128, 128), 128)
            values = source_ref[part, :].astype(f32)
            low = (values * inverse_rms(values) * gain_one).astype(bf16)
            normed_ref[part, :] = low
            normed_turned[:, part] = low.T
            return carry

        lax.fori_loop(0, (rows + 256) // 128, norm_rows, 0)

        def pool_rows(index, carry):
            part = pl.ds(pl.multiple_of(index * 128, 128), 128)
            values = raw_ref[part, :].astype(f32) * gain_one
            low = (values * inverse_rms(values) * gain_pool).astype(bf16)
            pooled_ref[part, :] = low
            pooled_turned[:, part] = low.T
            return carry

        lax.fori_loop(0, slots // 128, pool_rows, 0)

    lane = lax.broadcasted_iota(i32, (256, 128), 1)
    spread = []
    for head in range(2):
        mine = jnp.where(lane == 2 * pl.program_id(0) + head, offsets_ref[...], 0.0)
        spread.append(jnp.broadcast_to(jnp.sum(mine, axis=1, keepdims=True), (256, 128)))
    lane_of = lax.broadcasted_iota(i32, (256, 256), 1)
    bias_ref[0] = align_offsets(jnp.concatenate(spread, axis=1), lane_of & 127, 7, -1)

    query_ref[...] = dot_nn(normed_ref[128 : 128 + rows, :], wq_ref[...]).astype(bf16)
    w_two = jnp.concatenate([wk_ref[...], wv_ref[...]], axis=1)
    two = dot_nn(normed_ref[...], w_two).astype(bf16)
    key_ref[...] = two[:, :128]
    value_ref[...] = two[:, 128:]
    value_turned[...] = two[:, 128:].T
    two = dot_nn(pooled_ref[...], w_two).astype(bf16)
    gkey_ref[...] = two[:, :128]
    gvalue_ref[...] = two[:, 128:]
    gvalue_turned[...] = two[:, 128:].T
    upper = upper_band()
    on_slot = slot_lanes()

    def step(block, carry):
        window = window_of(block)
        query_two = stack_heads(query_ref[rows_of(block), :])
        own, merged, far = block_scores(
            block, upper, on_slot, query_two, key_ref, gkey_ref, bias_ref, klocal_ref, kglobal_ref, qfeat_ref
        )
        peak = jnp.maximum(
            jnp.maximum(
                jnp.max(own, axis=0, keepdims=True), jnp.max(merged, axis=0, keepdims=True)
            ),
            jnp.max(far, axis=0, keepdims=True),
        )
        own, merged, far = jnp.exp(own - peak), jnp.exp(merged - peak), jnp.exp(far - peak)
        total = (
            jnp.sum(own, axis=0, keepdims=True)
            + jnp.sum(merged, axis=0, keepdims=True)
            + jnp.sum(far, axis=0, keepdims=True)
        )
        near_low = spread_band(upper, own, merged)
        wide = dot_nn(value_turned[:, window], near_low) + dot_nn(
            gvalue_turned[...], far.astype(bf16)
        )
        out_ref[rows_of(block), :] = unstack_heads(wide * (1.0 / total)).astype(bf16)
        log_ref[0, pl.ds(block, 1), :] = peak + jnp.log(total)
        return carry

    lax.fori_loop(0, rows // 128, step, 0, unroll=8)


def align_offsets(sums, step_of_lane, bits, sign):
    for bit in range(bits):
        shift = sign * (1 << bit)
        moved = jnp.concatenate([sums[shift:], sums[:shift]], axis=0)
        sums = jnp.where((step_of_lane >> bit) & 1 == 1, moved, sums)
    return sums


def two_totals(left, right):
    lane = lax.broadcasted_iota(i32, (left.shape[0], 128), 1)
    first = jnp.sum(left, axis=1, keepdims=True)
    second = jnp.sum(right, axis=1, keepdims=True)
    return jnp.where(lane == 0, first, jnp.where(lane == 1, second, 0.0))


def add_buckets(table_ref, sums, offset, head):
    hit = (bucket_of(offset) == lax.broadcasted_iota(i32, sums.shape, 1)).astype(f32)
    totals = lax.dot_general(
        sums, hit, (((0,), (0,)), ((), ())), precision=highest, preferred_element_type=f32
    )
    row = lax.broadcasted_iota(i32, table_ref.shape, 0)
    table_ref[...] += jnp.where(
        row == head, totals[0:1], jnp.where(row == head + 1, totals[1:2], 0.0)
    )


def attend_backward(
    last, part, own_part, first_pair, query_ref, grad_ref, key_ref, value_ref, gkey_ref, gvalue_ref, normed_ref, normed_turned, pooled_turned, wq_ref, wk_ref, wv_ref,
    log_ref, bias_ref, klocal_ref, kglobal_ref, qfeat_ref, raw_ref, gains_ref, place_ref, old_small_ref, old_table_ref, old_dnormed_ref, old_draw_ref,
    keep_ref, send_ref, dnormed_ref, draw_ref, small_ref, table_ref,
    dnormed_sum, dpooled_sum, draw_sum, key_turned, gkey_turned, dquery, key_sum, value_sum, gkey_sum, gvalue_sum, near_sum, far_sum,
):
    rows = query_ref.shape[0]
    slots = gkey_ref.shape[0]

    @pl.when(pl.program_id(0) == 0)
    def start():
        dnormed_sum[...] = jnp.zeros_like(dnormed_sum)
        dpooled_sum[...] = jnp.zeros_like(dpooled_sum)
        table_ref[...] = old_table_ref[...]

    key_turned[...] = key_ref[...].T
    gkey_turned[...] = gkey_ref[...].T
    for total_ref in (key_sum, value_sum, gkey_sum, gvalue_sum, near_sum, far_sum):
        total_ref[...] = jnp.zeros_like(total_ref)
    upper = upper_band()
    on_slot = slot_lanes()
    lane = lax.broadcasted_iota(i32, (256, 128), 0)
    column = lax.broadcasted_iota(i32, (256, 128), 1)
    slot_column = (lane // 128) * 64 + (lane % 128) // 16

    def step(block, carry):
        window = window_of(block)
        query_two = stack_heads(query_ref[rows_of(block), :])
        grad_two = stack_heads(grad_ref[rows_of(block), :])
        own, merged, far = block_scores(
            block, upper, on_slot, query_two, key_ref, gkey_ref, bias_ref, klocal_ref, kglobal_ref, qfeat_ref
        )
        logs = log_ref[0, pl.ds(block, 1), :]
        own, merged, far = jnp.exp(own - logs), jnp.exp(merged - logs), jnp.exp(far - logs)
        value_sum[window, :] += dot_nn(spread_band(upper, own, merged), grad_two)
        gvalue_sum[...] += dot_nn(far.astype(bf16), grad_two)
        near_dot = dot_nt(value_ref[window, :], grad_two)
        own_dot = near_dot[128:256]
        merged_dot = jnp.where(upper, near_dot[0:128], near_dot[256:384])
        far_dot = dot_nt(gvalue_ref[...], grad_two)
        centre = (
            jnp.sum(own * own_dot, axis=0, keepdims=True)
            + jnp.sum(merged * merged_dot, axis=0, keepdims=True)
            + jnp.sum(far * far_dot, axis=0, keepdims=True)
        )
        own = own * (own_dot - centre)
        merged = merged * (merged_dot - centre)
        far = (far * (far_dot - centre)).astype(bf16)
        near_sum[0:128, :] += own
        near_sum[128:256, :] += merged
        choose = (column == slot_column + block * 8).astype(bf16)
        far_sum[...] += dot_nn(far, choose)
        near_low = spread_band(upper, own, merged)
        key_sum[window, :] += dot_nn(near_low, query_two)
        gkey_sum[...] += dot_nn(far, query_two)
        wide = dot_nn(key_turned[:, window], near_low) + dot_nn(gkey_turned[...], far)
        dquery[rows_of(block), :] = unstack_heads(wide).astype(bf16)
        return carry

    lax.fori_loop(0, rows // 128, step, 0, unroll=8)

    core, first_slot = place_ref[0], place_ref[1]
    head = 2 * (first_pair + pl.program_id(0))
    lane_of = lax.broadcasted_iota(i32, (256, 256), 1)
    near = align_offsets(near_sum[...], lane_of & 127, 7, 1)
    near = two_totals(near[:, :128], near[:, 128:])
    place = lax.broadcasted_iota(i32, (256, 128), 0)
    add_buckets(table_ref, near, ((place + 128) & 255) - 128, head)
    lane_of = lax.broadcasted_iota(i32, (slots + 64, 128), 1)
    far = jnp.concatenate([far_sum[...], jnp.zeros((64, 128), f32)], axis=0)
    far = align_offsets(far, lane_of & 63, 6, 1)
    far = two_totals(jnp.where(lane_of < 64, far, 0.0), jnp.where(lane_of < 64, 0.0, far))
    place = lax.broadcasted_iota(i32, (slots + 64, 128), 0)
    heads = normed_ref.shape[1] // 64
    add_buckets(table_ref, far, jnp.where(place < slots, place, place - slots - 64) - first_slot, heads + head)

    width = normed_ref.shape[1]
    grad_low = dquery[...]
    dwq = dot_nn(normed_turned[:, 128 : 128 + rows], grad_low)
    planes = 4 if last else 3
    lead = pl.program_id(0) * planes
    store_halves(keep_ref, send_ref, lead, dwq, core, part)
    dnormed_sum[128 : 128 + rows, :] += dot_nt(grad_low, wq_ref[...])
    two = jnp.concatenate([key_sum[...], value_sum[...]], axis=1).astype(bf16)
    gtwo = jnp.concatenate([gkey_sum[...], gvalue_sum[...]], axis=1).astype(bf16)
    w_two = jnp.concatenate([wk_ref[...], wv_ref[...]], axis=1)
    dw_two = dot_nn(normed_turned[...], two) + dot_nn(pooled_turned[...], gtwo)
    store_halves(keep_ref, send_ref, lead + 1, dw_two[:, :128], core, part)
    store_halves(keep_ref, send_ref, lead + 2, dw_two[:, 128:], core, part)
    dnormed_sum[...] += dot_nt(two, w_two)
    dpooled_sum[...] += dot_nt(gtwo, w_two)

    @pl.when(pl.program_id(0) == pl.num_programs(0) - 1)
    def finish():
        gain_one, gain_pool = gains_ref[0:1, :], gains_ref[1:2, :]
        small_ref[...] = old_small_ref[...]

        def norm_rows(index, carry):
            part = pl.ds(pl.multiple_of(index * 128, 128), 128)
            grad = dnormed_sum[part, :]
            total = grad if first_pair == 0 else grad + old_dnormed_ref[part, :].astype(f32)
            dnormed_ref[part, :] = total.astype(bf16)
            return carry + jnp.sum(grad * normed_ref[part, :].astype(f32), axis=0, keepdims=True)

        norm_part = lax.fori_loop(0, (rows + 256) // 128, norm_rows, jnp.zeros((1, width), f32))
        norm_part = norm_part / gain_one

        def pool_rows(index, carry):
            norm_part, pool_part = carry
            part = pl.ds(pl.multiple_of(index * 128, 128), 128)
            raw = raw_ref[part, :].astype(f32)
            values = raw * gain_one
            inverse = inverse_rms(values)
            grad = dpooled_sum[part, :]
            back = norm_gradient(values, inverse, gain_pool, grad)
            total = back if first_pair == 0 else back + old_draw_ref[part, :].astype(f32)
            draw_sum[part, :] = total.astype(bf16)
            return (
                norm_part + jnp.sum(back * raw, axis=0, keepdims=True),
                pool_part + jnp.sum(grad * values * inverse, axis=0, keepdims=True),
            )

        norm_part, pool_part = lax.fori_loop(
            0, slots // 128, pool_rows, (norm_part, jnp.zeros((1, width), f32))
        )
        small_ref[0:1, :] += norm_part
        small_ref[1:2, :] += pool_part
        if not last:
            draw_ref[...] = draw_sum[...]
            return
        own_slots = rows // 16
        me = lax.axis_index("y") * lax.axis_size("x") + lax.axis_index("x")
        for hop in range(draw_ref.shape[0]):
            target = lax.rem(me + hop, draw_ref.shape[0])
            draw_ref[hop, :own_slots, :] = draw_sum[
                pl.ds(pl.multiple_of(target * own_slots, own_slots), own_slots), :
            ]
            before = target == me - 1

            @pl.when(before)
            def head():
                draw_ref[hop, own_slots:, :] = dnormed_ref[:128, :]

            @pl.when(jnp.logical_not(before))
            def tail():
                draw_ref[hop, own_slots:, :] = dnormed_ref[rows + 128 :, :]

        rows_of_small = jnp.concatenate([small_ref[...], jnp.zeros((120, width), f32)], axis=0)
        tables = jnp.zeros((width, 128), f32)
        row = lax.broadcasted_iota(i32, (width, 32), 0)
        column = lax.broadcasted_iota(i32, (width, 32), 1)
        for block in range(-(-2 * heads // own_part)):
            chosen = (column == row % own_part + block * own_part).astype(f32)
            shifted = table_ref[...]
            if block:
                shifted = jnp.concatenate(
                    [shifted[:, 128 - 32 * block :], shifted[:, : 128 - 32 * block]], axis=1
                )
            tables = tables + jnp.dot(
                chosen, shifted, precision=highest, preferred_element_type=f32
            )
        store_halves(keep_ref, send_ref, 3, rows_of_small.T, core, part)
        store_halves(keep_ref, send_ref, keep_ref.shape[0] - 1, tables, core, part)


def columns(rows, first):
    return pl.BlockSpec((rows, 128), lambda pair: (0, pair + first))


def of_pair(first, *shape):
    zeros = (0,) * len(shape)
    return pl.BlockSpec((1,) + shape, lambda pair: (pair + first,) + zeros)


def fixed(*shape):
    zeros = (0,) * len(shape)
    return pl.BlockSpec(shape, lambda pair: zeros, pipeline_mode=pl.Buffered(1))


def fixed_out(*shape):
    zeros = (0,) * len(shape)
    return pl.BlockSpec(shape, lambda pair: zeros)


def attention_forward(source_ext, raw_pool, weights, bias, klocal, kglobal, qfeat):
    width = source_ext.shape[1]
    rows = source_ext.shape[0] - 256
    slots = raw_pool.shape[0]
    blocks = rows // 128
    pairs = width // 128
    return pl.pallas_call(
        attend_forward,
        grid=(pairs,),
        in_specs=[
            fixed(rows + 256, width),
            fixed(slots, width),
            pl.BlockSpec((width, 128), lambda pair: (0, 4 * pairs), pipeline_mode=pl.Buffered(1)),
            columns(width, 0),
            columns(width, pairs),
            columns(width, 2 * pairs),
            fixed(256, 128),
            fixed(rows + 256, 128),
            columns(blocks * slots, 0),
            fixed(rows, 128),
        ],
        out_specs=[
            of_pair(0, 256, 256),
            columns(rows, 0),
            of_pair(0, blocks, 256),
            columns(rows, 0),
            columns(rows + 256, 0),
            columns(rows + 256, 0),
            columns(slots, 0),
            columns(slots, 0),
            fixed_out(rows + 256, width),
            fixed_out(8, width),
            fixed_out(width, rows + 256),
            fixed_out(width, slots),
        ],
        out_shape=[
            jax.ShapeDtypeStruct((pairs, 256, 256), f32),
            jax.ShapeDtypeStruct((rows, width), bf16),
            jax.ShapeDtypeStruct((pairs, blocks, 256), f32),
            jax.ShapeDtypeStruct((rows, width), bf16),
            jax.ShapeDtypeStruct((rows + 256, width), bf16),
            jax.ShapeDtypeStruct((rows + 256, width), bf16),
            jax.ShapeDtypeStruct((slots, width), bf16),
            jax.ShapeDtypeStruct((slots, width), bf16),
            jax.ShapeDtypeStruct((rows + 256, width), bf16),
            jax.ShapeDtypeStruct((8, width), f32),
            jax.ShapeDtypeStruct((width, rows + 256), bf16),
            jax.ShapeDtypeStruct((width, slots), bf16),
        ],
        scratch_shapes=[pltpu.VMEM((slots, width), bf16), pltpu.VMEM((128, rows + 256), bf16), pltpu.VMEM((128, slots), bf16)],
        compiler_params=pltpu.CompilerParams(vmem_limit_bytes=48 << 20),
        cost_estimate=pl.CostEstimate(
            flops=30 * rows * (384 + slots) * width, bytes_accessed=24 << 20, transcendentals=0
        ),
        name="attend_forward",
    )(source_ext, raw_pool, weights, weights, weights, weights, bias, klocal, kglobal, qfeat)


def attention_backward(
    first, count, part, queries, grads, keys, values, gkeys, gvalues, normed, turned, pooled, weights, logs, bias, klocal,
    kglobal, qfeat, raw_pool, gains, place, old_small, old_table, old_dnormed, old_draw,
):
    rows, width = queries.shape
    slots = gkeys.shape[0]
    blocks = rows // 128
    pairs = width // 128
    lead = count * (4 if first + count == pairs else 3)
    own_slots = rows // 16
    draw_shape = (slots // own_slots, own_slots + 128, width) if first + count == pairs else (slots, width)
    return pl.pallas_call(
        functools.partial(attend_backward, first + count == pairs, width // 32, part, first),
        grid=(count,),
        in_specs=[
            columns(rows, first),
            columns(rows, first),
            columns(rows + 256, first),
            columns(rows + 256, first),
            columns(slots, first),
            columns(slots, first),
            fixed(rows + 256, width),
            fixed(width, rows + 256),
            fixed(width, slots),
            columns(width, first),
            columns(width, pairs + first),
            columns(width, 2 * pairs + first),
            of_pair(first, blocks, 256),
            of_pair(first, 256, 256),
            fixed(rows + 256, 128),
            columns(blocks * slots, first),
            fixed(rows, 128),
            fixed(slots, width),
            fixed(8, width),
            pl.BlockSpec(memory_space=pltpu.SMEM),
            fixed(8, width),
            fixed(32, 128),
            fixed(rows + 256, width) if first else fixed(8, width),
            fixed(slots, width) if first else fixed(8, width),
        ],
        out_specs=[
            fixed_out(lead, width // 2, 128),
            fixed_out(lead, width // 2, 128),
            fixed_out(rows + 256, width),
            fixed_out(*draw_shape),
            fixed_out(8, width),
            fixed_out(32, 128),
        ],
        out_shape=[
            jax.ShapeDtypeStruct((lead, width // 2, 128), bf16),
            jax.ShapeDtypeStruct((lead, width // 2, 128), bf16),
            jax.ShapeDtypeStruct((rows + 256, width), bf16),
            jax.ShapeDtypeStruct(draw_shape, bf16),
            jax.ShapeDtypeStruct((8, width), f32),
            jax.ShapeDtypeStruct((32, 128), f32),
        ],
        scratch_shapes=[
            pltpu.VMEM((rows + 256, width), f32),
            pltpu.VMEM((slots, width), f32),
            pltpu.VMEM((slots, width), bf16),
            pltpu.VMEM((128, rows + 256), bf16),
            pltpu.VMEM((128, slots), bf16),
            pltpu.VMEM((rows, 128), bf16),
            pltpu.VMEM((rows + 256, 128), f32),
            pltpu.VMEM((rows + 256, 128), f32),
            pltpu.VMEM((slots, 128), f32),
            pltpu.VMEM((slots, 128), f32),
            pltpu.VMEM((256, 256), f32),
            pltpu.VMEM((slots, 128), f32),
        ],
        compiler_params=pltpu.CompilerParams(vmem_limit_bytes=48 << 20),
        cost_estimate=pl.CostEstimate(
            flops=60 * rows * (384 + slots) * 128 * count, bytes_accessed=count << 22, transcendentals=0
        ),
        name="attend_backward",
    )(
        queries, grads, keys, values, gkeys, gvalues, normed, turned, pooled, weights, weights, weights, logs, bias, klocal,
        kglobal, qfeat, raw_pool, gains, place, old_small, old_table, old_dnormed, old_draw,
    )


def interleave(held, other, core):
    held, other = held.astype(f32), other.astype(f32)
    both = jnp.stack([jnp.where(core == 0, held, other), jnp.where(core == 0, other, held)], axis=1)
    return both.reshape(-1, both.shape[-1])


def fold_rows(tall):
    rows, width = tall.shape[1:]
    return jnp.concatenate(
        [
            jnp.concatenate(
                [tall[:, r : r + 8, c : c + 256] for r in range(0, rows, 8)], axis=2
            )
            for c in range(0, width, 256)
        ],
        axis=1,
    )


unfold_rows = fold_rows


def pack_weights(wq_ref, wk_ref, wv_ref, wo_ref, gains_ref, gate_ref, up_ref, down_ref, first_ref, second_ref):
    width = wq_ref.shape[1]
    for index, weight_ref in enumerate((wq_ref, wk_ref, wv_ref, wo_ref)):
        first_ref[:, index * width : (index + 1) * width] = weight_ref[...]
    first_ref[:, 4 * width :] = gains_ref[...]
    if second_ref.shape[1] > 128:
        hidden = gate_ref.shape[1]
        second_ref[:, :hidden] = gate_ref[...]
        second_ref[:, hidden : 2 * hidden] = up_ref[...]
        second_ref[:, 2 * hidden :] = fold_rows(down_ref[...].astype(f32)[None])[0].astype(bf16)


def pack_tokens(source_ref, keep_ref, marks_ref, shared_ref):
    width = source_ref.shape[1]
    slots = source_ref.shape[0] // 16
    for slot in range(0, slots, 16):
        rows = slice(slot * 16, slot * 16 + 256)
        values = source_ref[rows, :].astype(f32)
        values = values * (inverse_rms(values) * keep_ref[rows, :])
        shared_ref[0, slot : slot + 16, :] = jnp.sum(values.reshape(16, 16, width), axis=1).astype(bf16)
    marks = marks_ref[...].astype(f32)
    rest = jnp.zeros((marks.shape[0], width - 128), f32)
    count = slots + marks.shape[0]
    shared_ref[0, slots:count, :] = jnp.concatenate([marks, rest], axis=1).astype(bf16)
    for target in range(1, shared_ref.shape[0]):
        shared_ref[target, :count, :] = shared_ref[0, :count, :]
    for target in range(shared_ref.shape[0]):
        before = target == lax.axis_index("y") * lax.axis_size("x") + lax.axis_index("x") - 1

        @pl.when(before)
        def head():
            shared_ref[target, count:, :] = source_ref[:128, :]

        @pl.when(jnp.logical_not(before))
        def tail():
            shared_ref[target, count:, :] = source_ref[source_ref.shape[0] - 128 :, :]


def pack_all(wq, wk, wv, wo, gains, gate, up, down, aligned):
    part, width = wq.shape
    return pl.pallas_call(
        pack_weights,
        out_shape=[
            jax.ShapeDtypeStruct((part, 4 * width + 128), bf16),
            jax.ShapeDtypeStruct((part, 3 * gate.shape[1] if aligned else 128), bf16),
        ],
        compiler_params=pltpu.CompilerParams(vmem_limit_bytes=60 << 20),
        name="pack_weights",
    )(wq, wk, wv, wo, gains, gate, up, down)


def pack_shared(source, keep, marks, count):
    rows, width = source.shape
    return pl.pallas_call(
        pack_tokens,
        out_shape=jax.ShapeDtypeStruct((count, rows // 16 + marks.shape[0] + 128, width), bf16),
        compiler_params=pltpu.CompilerParams(vmem_limit_bytes=60 << 20),
        name="pack_tokens",
    )(source, keep, marks)


def feed_forward(
    source_ref, mixture_ref, wo_ref, gains_ref, cot_ref, gate_held, gate_other, up_held, up_other, down_held, down_other,
    place_ref,
    out_ref, middle_grad_ref, dmixture_ref, dgain_ref, keep_out, send_out, keep_wide, send_wide, keep_down, send_down,
    middle, normed, turned, out_sum, grad_sum, product, gate_low, lift_low, wg_ref, wu_ref, wd_ref,
):
    rows, width = source_ref.shape
    part_rows = 256
    parts = rows // part_rows
    gain = gains_ref[2:3, :]
    core = place_ref[0]
    wg_ref[...] = interleave(gate_held[...], gate_other[...], core).astype(bf16)
    wu_ref[...] = interleave(up_held[...], up_other[...], core).astype(bf16)
    wd_ref[...] = interleave(
        unfold_rows(down_held[...].astype(f32)), unfold_rows(down_other[...].astype(f32)), core
    ).astype(bf16)

    @pl.when(pl.program_id(0) == 0)
    def start():
        def norm_rows(index, carry):
            part = pl.ds(pl.multiple_of(index * 256, 256), 256)
            values = source_ref[part, :].astype(f32) + dot_nn(mixture_ref[part, :], wo_ref[...])
            middle[part, :] = values
            low = (values * inverse_rms(values) * gain).astype(bf16)
            normed[part, :] = low
            turned[:, part] = low.T
            return carry

        lax.fori_loop(0, rows // 256, norm_rows, 0, unroll=True)
        out_sum[...] = jnp.zeros_like(out_sum)
        grad_sum[...] = jnp.zeros_like(grad_sum)

    root = 0.7978845608028654
    for index in range(parts):
        part = slice(index * part_rows, (index + 1) * part_rows)
        low = normed[part, :]
        gate_pre = dot_nn(low, wg_ref[...])
        lift_pre = dot_nn(low, wu_ref[...])
        grad = dot_nt(cot_ref[part, :], wd_ref[...])
        square = gate_pre * gate_pre
        bent = jnp.tanh(gate_pre * (root + (root * 0.044715) * square))
        half = 0.5 + 0.5 * bent
        gelu = gate_pre * half
        slope = half + gelu * (1.0 - bent) * (root + (3 * root * 0.044715) * square)
        product[part, :] = (gelu * lift_pre).astype(bf16)
        lift_low[part, :] = (grad * gelu).astype(bf16)
        gate_low[part, :] = (grad * lift_pre * slope).astype(bf16)
        out_sum[part, :] += dot_nn(product[part, :], wd_ref[...])
        grad_sum[part, :] += dot_nt(gate_low[part, :], wg_ref[...]) + dot_nt(
            lift_low[part, :], wu_ref[...]
        )
    wide_part, down_part = width // 32, down_held.shape[1] * down_held.shape[2] // width
    store_halves(keep_wide, send_wide, 0, dot_nn(turned[...], gate_low[...]), core, wide_part)
    store_halves(keep_wide, send_wide, 1, dot_nn(turned[...], lift_low[...]), core, wide_part)
    value = dot_nn(product[...].T, cot_ref[...]).reshape(-1, 2, down_part, width)
    first, second = value[:, 0], value[:, 1]
    for half_ref, chosen in (
        (keep_down, jnp.where(core == 0, first, second)),
        (send_down, jnp.where(core == 0, second, first)),
    ):
        folded = fold_rows(chosen)
        folded = folded.reshape(-1, folded.shape[2]).astype(bf16)
        half_ref[0], half_ref[1] = folded[:, : folded.shape[1] // 2], folded[:, folded.shape[1] // 2 :]

    @pl.when(pl.program_id(0) == pl.num_programs(0) - 1)
    def finish():
        dgain_ref[...] = jnp.zeros_like(dgain_ref)

        def back_rows(index, carry):
            part = pl.ds(pl.multiple_of(index * 256, 256), 256)
            values = middle[part, :]
            out_ref[part, :] = (values + out_sum[part, :]).astype(bf16)
            inverse = inverse_rms(values)
            grad = grad_sum[part, :]
            dgain_ref[2:3, :] += jnp.sum(grad * values * inverse, axis=0, keepdims=True)
            total = cot_ref[part, :].astype(f32) + norm_gradient(values, inverse, gain, grad)
            middle_grad_ref[part, :] = total
            low = total.astype(bf16)
            normed[part, :] = low
            dmixture_ref[part, :] = dot_nt(low, wo_ref[...]).astype(bf16)
            turned[:, part] = mixture_ref[part, :].T
            return carry

        lax.fori_loop(0, rows // 256, back_rows, 0, unroll=True)
        for side in range(2):
            half = slice(side * width // 2, (side + 1) * width // 2)
            store_halves(keep_out, send_out, side, dot_nn(turned[...], normed[:, half]), core, width // 32)


def feed_forward_both(source, mixture, weights, gains, cotangent, held, other, place):
    rows, width = source.shape
    groups, part, total = held.shape
    hidden = total // 3
    tile = 512
    tiles = hidden // tile
    step_groups = groups // tiles
    gate_spec = pl.BlockSpec((groups, part, tile), lambda step: (0, 0, step))
    up_spec = pl.BlockSpec((groups, part, tile), lambda step: (0, 0, step + tiles))
    down_spec = pl.BlockSpec((step_groups, part, hidden), lambda step: (step, 0, 2))
    wide_spec = pl.BlockSpec((2, width // 2, tile), lambda step: (0, 0, step))
    fold_spec = pl.BlockSpec((2, step_groups * part, hidden // 2), lambda step: (0, step, 0))
    out_spec = fixed_out(2, width // 2, width // 2)
    return pl.pallas_call(
        feed_forward,
        grid=(tiles,),
        in_specs=[
            fixed(rows, width),
            fixed(rows, width),
            pl.BlockSpec((width, width), lambda step: (0, 3), pipeline_mode=pl.Buffered(1)),
            fixed(8, width),
            fixed(rows, width),
            gate_spec,
            gate_spec,
            up_spec,
            up_spec,
            down_spec,
            down_spec,
            pl.BlockSpec(memory_space=pltpu.SMEM),
        ],
        out_specs=[
            fixed_out(rows, width),
            fixed_out(rows, width),
            fixed_out(rows, width),
            fixed_out(8, width),
            out_spec,
            out_spec,
            wide_spec,
            wide_spec,
            fold_spec,
            fold_spec,
        ],
        out_shape=[
            jax.ShapeDtypeStruct((rows, width), bf16),
            jax.ShapeDtypeStruct((rows, width), f32),
            jax.ShapeDtypeStruct((rows, width), bf16),
            jax.ShapeDtypeStruct((8, width), f32),
            jax.ShapeDtypeStruct((2, width // 2, width // 2), bf16),
            jax.ShapeDtypeStruct((2, width // 2, width // 2), bf16),
            jax.ShapeDtypeStruct((2, width // 2, hidden), bf16),
            jax.ShapeDtypeStruct((2, width // 2, hidden), bf16),
            jax.ShapeDtypeStruct((2, width // 2, hidden // 2), bf16),
            jax.ShapeDtypeStruct((2, width // 2, hidden // 2), bf16),
        ],
        scratch_shapes=[
            pltpu.VMEM((rows, width), f32),
            pltpu.VMEM((rows, width), bf16),
            pltpu.VMEM((width, rows), bf16),
            pltpu.VMEM((rows, width), f32),
            pltpu.VMEM((rows, width), f32),
            pltpu.VMEM((rows, tile), bf16),
            pltpu.VMEM((rows, tile), bf16),
            pltpu.VMEM((rows, tile), bf16),
            pltpu.VMEM((width, tile), bf16),
            pltpu.VMEM((width, tile), bf16),
            pltpu.VMEM((tile, width), bf16),
        ],
        compiler_params=pltpu.CompilerParams(vmem_limit_bytes=60 << 20),
        cost_estimate=pl.CostEstimate(
            flops=20 * rows * width * hidden, bytes_accessed=40 << 20, transcendentals=0
        ),
        name="feed_forward",
    )(source, mixture, weights, gains, cotangent, held, other, held, other, held, other, place)


def source_gradient(source_ref, keep_ref, middle_grad_ref, gains_ref, upper_ref, lower_ref, *refs):
    step, steps = pl.program_id(0), pl.num_programs(0)
    pooled_refs, edge_refs, out_ref = refs[:-5], refs[-5:-1], refs[-1]
    rows, width = source_ref.shape
    pooled = pooled_refs[0][0].astype(f32)
    for other_ref in pooled_refs[1:]:
        pooled = pooled + other_ref[...].astype(f32)
    pooled = jnp.broadcast_to(pooled[:, None, :], (rows // 16, 16, width)).reshape(rows, width)
    me = lax.axis_index("y") * lax.axis_size("x") + lax.axis_index("x")
    before = (step == 0) & (me > 0)
    after = (step == steps - 1) & (me < len(pooled_refs) - 1)
    head, tail = (
        jnp.concatenate([first[...], second[...]], axis=0).astype(f32)
        for first, second in (edge_refs[:2], edge_refs[2:])
    )
    grad = jnp.concatenate(
        [
            upper_ref[...].astype(f32) + jnp.where(before, head, 0.0),
            lower_ref[...].astype(f32) + jnp.where(after, tail, 0.0),
        ],
        axis=0,
    )
    grad = grad + pooled * keep_ref[...]
    values = source_ref[...].astype(f32)
    out_ref[...] = middle_grad_ref[...] + norm_gradient(values, inverse_rms(values), gains_ref[0:1, :], grad)


def input_gradient(source, keep, middle_grad, gains, dnormed, payload, received):
    rows, width = source.shape
    tile = 256
    own_slots = rows // 16
    row_spec = pl.BlockSpec((tile, width), lambda step: (step, 0))
    edges = [
        pl.BlockSpec((64, width), lambda step, index=index: (own_slots // 64 + index, 0), pipeline_mode=pl.Buffered(1))
        for index in range(2)
    ]
    return pl.pallas_call(
        source_gradient,
        grid=(rows // tile,),
        in_specs=[
            row_spec,
            pl.BlockSpec((tile, 1), lambda step: (step, 0)),
            row_spec,
            fixed(8, width),
            pl.BlockSpec((128, width), lambda step: (1 + 2 * step, 0)),
            pl.BlockSpec((128, width), lambda step: (2 + 2 * step, 0)),
            pl.BlockSpec((1, tile // 16, width), lambda step: (0, step, 0)),
        ]
        + [pl.BlockSpec((tile // 16, width), lambda step: (step, 0)) for _ in received]
        + edges * 2,
        out_specs=row_spec,
        out_shape=jax.ShapeDtypeStruct((rows, width), f32),
        compiler_params=pltpu.CompilerParams(vmem_limit_bytes=60 << 20),
        cost_estimate=pl.CostEstimate(
            flops=20 * rows * width, bytes_accessed=14 << 20, transcendentals=0
        ),
        name="source_gradient",
    )(
        source, keep, middle_grad, gains, dnormed, dnormed, payload, *received, received[0], received[0], received[-1],
        received[-1],
    )


def near_offsets(local_bias):
    heads, buckets = local_bias.shape
    offset = (jnp.arange(256, dtype=i32) + 128) % 256 - 128
    table = (bucket_of(offset)[:, None] == jnp.arange(buckets, dtype=i32)).astype(f32)
    chosen = jnp.einsum("ob,hb->oh", table, local_bias, precision=highest)
    chosen = jnp.where((offset == -128)[:, None], never, chosen)
    return jnp.pad(chosen, ((0, 0), (0, 128 - heads)))


def far_features(global_bias, slot_segments, slot_live, first_slot, blocks):
    heads, buckets = global_bias.shape
    pairs = heads // 2
    slots = slot_segments.shape[0]
    wide = 8 * buckets + 8
    shape = (blocks * slots, wide)
    row = lax.broadcasted_iota(i32, shape, 0)
    column = lax.broadcasted_iota(i32, shape, 1)
    slot = row % slots
    query_slot = first_slot + (row // slots) * 8 + column // buckets
    code = jnp.tile(jnp.where(slot_live, slot_segments, 3), blocks)[:, None]
    picks = jnp.where(
        column < 8 * buckets,
        bucket_of(slot - query_slot) == column % buckets,
        code == column - 8 * buckets,
    ).astype(bf16)
    high = lax.reduce_precision(global_bias, 8, 7)
    middle = lax.reduce_precision(global_bias - high, 8, 7)
    lowest = lax.reduce_precision(global_bias - high - middle, 8, 7)
    parts = jnp.stack([high, middle, lowest]).reshape(3, pairs, 2, buckets)
    parts = parts.transpose(3, 1, 0, 2)
    same = jnp.eye(8, dtype=f32)[:, None, None, None, None, :]
    table = (parts[None, :, :, :, :, None] * same).reshape(8 * buckets, pairs, 48)
    table = jnp.pad(table, ((0, 8), (0, 0), (0, 80)))
    shape = (wide, 1, 128)
    lane = lax.broadcasted_iota(i32, shape, 2) - 48
    code_row = lax.broadcasted_iota(i32, shape, 0) - 8 * buckets
    barred = (code_row >= 0) & (lane >= 0) & (lane < 3) & (lane != code_row)
    table = jnp.where(barred, never, table).astype(bf16).reshape(wide, pairs * 128)
    return jnp.dot(picks, table, preferred_element_type=f32).astype(bf16)


def near_features(segments_ext, valid_ext):
    lane = lax.broadcasted_iota(i32, (segments_ext.shape[0], 128), 1)
    allowed = (segments_ext[:, None] == lane - 48) & (valid_ext[:, None] > 0)
    return jnp.where((lane >= 48) & (lane < 51) & ~allowed, never, 0.0).astype(bf16)


def query_features(own_segments):
    lane = lax.broadcasted_iota(i32, (own_segments.shape[0], 128), 1)
    return (own_segments[:, None] == lane - 48).astype(bf16)


def pick(values, index, dim):
    return lax.dynamic_index_in_dim(values, index, dim, keepdims=False)


def ring(size, hop):
    return [(i, (i + hop) % size) for i in range(size)]


def add_up(parts):
    if len(parts) == 1:
        return parts[0]
    return sum((part.astype(f32) for part in parts[1:]), parts[0].astype(f32))


def split_stage(side, labels, axis, join):
    size, me = lax.axis_size(axis), lax.axis_index(axis)
    dim = labels.index(axis) - len(labels) - 2 + side[0][0].ndim
    chosen = []
    for hop in range(size):
        pieces = [
            add_up([pick(part, (me + hop) % size, dim) for part in piece]).astype(bf16) for piece in side
        ]
        chosen.append(pieces[0] if len(pieces) == 1 else jnp.concatenate(pieces, axis=join))
    return chosen[1:], chosen[0]


def send_all(axis, pieces):
    size = lax.axis_size(axis)
    return [lax.ppermute(piece, axis, ring(size, hop + 1)) for hop, piece in enumerate(pieces)]


def place_stage(values, pieces, axis, dim):
    size, me = lax.axis_size(axis), lax.axis_index(axis)
    shape = values.shape[:dim] + (size,) + values.shape[dim:]
    out = lax.dynamic_update_index_in_dim(jnp.zeros(shape, values.dtype), values, me, dim)
    for hop, piece in enumerate(pieces):
        out = lax.dynamic_update_index_in_dim(out, piece, (me - hop - 1) % size, dim)
    return out


def half_of(width):
    return (width // 256) * 128


def scatter_steps(sides, labels, stages, join):
    labels = [list(labels) for _ in sides]
    for axes in stages:
        if axes == ("all z",):
            merged = [add_up(piece).astype(bf16) for side in sides for piece in side]
            merged = yield jnp.concatenate(merged, axis=join)
            dim = merged.ndim - 3
            got = yield lax.all_to_all(merged, "z", dim, dim, tiled=True)
            return jnp.sum(got.astype(f32), axis=dim)
        if len(axes) < len(sides):
            sides, labels = [[piece for side in sides for piece in side]], labels[:1]
        split = [split_stage(side, names, axis, join) for side, names, axis in zip(sides, labels, axes)]
        sends = yield [send for send, _ in split]
        gots = yield [send_all(axis, send) for axis, send in zip(axes, sends)]
        sides = [[[keep] + got] for (_, keep), got in zip(split, gots)]
        for names, axis in zip(labels, axes):
            names.remove(axis)
    return add_up(sides[0][0])


across = (("x", "y"), ("y", "x"))


stages = (("x", "y"), ("y", "x"), ("z",))
labels = ("y", "x", "z")


def core_steps(pairs, part):
    y, x, z, _ = (lax.axis_size(axis) for axis in everyone)
    keeps, sends = zip(*pairs)
    if part != keeps[0].shape[1] // 16:
        keeps, sends = zip(*(regroup(keep, send, part) for keep, send in pairs))
    sends = yield sends
    gots = yield [lax.ppermute(send, "core", ring(2, 1)) for send in sends]
    sides = [[], []]
    for keep, got in zip(keeps, gots):
        lead, _, width = keep.shape
        held, new = (values.reshape(lead, y, x, z, part, width) for values in (keep, got))
        sides[0].append([held[: lead // 2], new[: lead // 2]])
        sides[1].append([held[lead // 2 :], new[lead // 2 :]])
    return sides


def sum_rows(pairs, part, join):
    sides = yield from core_steps(pairs, part)
    return (yield from scatter_steps(sides, labels, across + (("all z",),), join))


def regroup(keep, send, part):
    lead, half, width = keep.shape
    both = jnp.stack([keep.reshape(lead, 16, -1, width), send.reshape(lead, 16, -1, width)], axis=2)
    both = both.reshape(lead, half // part, 2, part, width)
    me = lax.axis_index("core")
    return tuple(pick(both, index, 2).reshape(keep.shape) for index in (me, 1 - me))


def all_rows(shard, last):
    width = shard.shape[1]
    half = half_of(width)
    others = lax.axis_size("z") - 1
    shard = yield shard
    pieces = yield send_all("z", [shard] * others)
    values = place_stage(shard, pieces, "z", 0)
    left, right = values[..., :half], values[..., half:]
    for left_axis, right_axis in across:
        dim = 1 if right_axis == "x" else 0
        left, right = yield left, right
        got = yield (
            send_all(left_axis, [left] * (lax.axis_size(left_axis) - 1)),
            send_all(right_axis, [right] * (lax.axis_size(right_axis) - 1)),
        )
        left = place_stage(left, got[0], left_axis, 0)
        right = place_stage(right, got[1], right_axis, dim)
    values = yield jnp.concatenate([left, right], axis=-1)
    got = yield send_all("core", [values])
    if not last:
        return values.reshape(-1, *values.shape[-2:]), got[0].reshape(-1, *values.shape[-2:])
    return place_stage(values, got, "core", 3).reshape(-1, width)


class Chain:
    def __init__(self, steps):
        self.steps = steps
        self.value = next(steps)
        self.done = False

    def advance(self):
        try:
            self.value = self.steps.send(self.value)
        except StopIteration as end:
            self.value, self.done = end.value, True


def phase(operand, work, launch=(), collect=None):
    collect = launch if collect is None else collect
    values, operand = lax.optimization_barrier(([chain.value for chain in launch], operand))
    for chain, value in zip(launch, values):
        chain.value = value
        chain.advance()
    result = work(operand)
    values, result = lax.optimization_barrier(([chain.value for chain in collect], result))
    for chain, value in zip(collect, values):
        chain.value = value
        chain.advance()
    return result


def on_device(
    hidden_state,
    segment_ids,
    valid_mask,
    cotangent,
    norm_gain,
    pool_gain,
    feed_gain,
    query_weight,
    key_weight,
    value_weight,
    output_weight,
    local_bias,
    global_bias,
    gate_weight,
    up_weight,
    down_weight,
):
    model_width = hidden_state.shape[2]
    hidden = gate_weight.shape[1]
    tok_rows = hidden_state.shape[1]
    own_part = norm_gain.shape[0]
    buckets = local_bias.shape[1]
    pairs = local_bias.shape[0] // 2
    blocks = tok_rows // 128
    own_slots = tok_rows // 16
    seq_count = lax.axis_size(seq)
    slot_count = own_slots * seq_count
    row_start = lax.axis_index(seq) * tok_rows
    first_slot = row_start // 16
    source = hidden_state[0]
    upstream = cotangent[0]
    own_segments = segment_ids[0]
    valid_float = valid_mask[0].astype(f32)

    aligned = own_part * 32 == model_width
    place = jnp.stack([lax.axis_index("core"), first_slot]).astype(i32)
    gain_columns = jnp.pad(jnp.stack([norm_gain, pool_gain, feed_gain], axis=1), ((0, 0), (0, 125)))
    packed, packed_second = pack_all(
        query_weight, key_weight, value_weight, output_weight, gain_columns, gate_weight, up_weight, down_weight, aligned
    )
    first = Chain(all_rows(packed, True))
    later = [Chain(all_rows(packed_second, False))] if aligned else []

    def share(operands):
        source, segments, valid = operands
        marks = jnp.concatenate([segments.reshape(-1, 128), valid.reshape(-1, 128)])
        shared = pack_shared(source, valid[0].astype(f32)[:, None], marks, seq_count)
        return lax.all_to_all(shared, seq, 0, 0, tiled=True)

    held = []
    phase(
        (source, segment_ids, valid_mask), lambda operands: held.append(share(operands)), [first] + later, [first]
    )

    def near_parts(operands):
        shared, local_bias = operands
        me = lax.axis_index(seq)
        edge = own_slots + 2 * (tok_rows // 128)
        raw_pool = shared[:, :own_slots].reshape(slot_count, model_width)
        all_marks = shared[:, own_slots:edge, :128].astype(i32).reshape(seq_count, 2, tok_rows)
        before, after = (
            jnp.where((near >= 0) & (near < seq_count), pick(shared[:, edge:], jnp.clip(near, 0, seq_count - 1), 0), 0)
            for near in (me - 1, me + 1)
        )
        all_segments, all_valid = all_marks[:, 0].reshape(-1), all_marks[:, 1].reshape(-1)
        slot_segments = all_segments.reshape(slot_count, 16)[:, 0]
        slot_live = jnp.sum(all_valid.reshape(slot_count, 16), axis=1) > 0
        segments_ext = lax.dynamic_slice_in_dim(
            jnp.pad(all_segments, 128, constant_values=-1), row_start, tok_rows + 256
        )
        valid_ext = lax.dynamic_slice_in_dim(jnp.pad(all_valid, 128), row_start, tok_rows + 256)
        feat_near = near_features(segments_ext, valid_ext)
        source_ext = jnp.concatenate([before, source, after], axis=0)
        return raw_pool, slot_segments, slot_live, feat_near, near_offsets(local_bias), source_ext

    raw_pool, slot_segments, slot_live, feat_near, bias_near, source_ext = phase(
        (held[0], local_bias), near_parts, [first], [first] + later
    )
    feat_query = query_features(own_segments)
    feat_far = phase(
        (global_bias, slot_segments, slot_live),
        lambda operands: far_features(*operands, first_slot, blocks),
        [first],
        [],
    )
    feat_far = phase(feat_far, lambda operands: operands, later, [first])
    phase((), lambda nothing: nothing, [first], [first] + later)
    weights = first.value

    bias, mixture, logs, queries, keys, vals, gkeys, gvals, normed, gains, turned, pooled = phase(
        (source_ext, raw_pool, weights, bias_near, feat_near, feat_far, feat_query),
        lambda operands: attention_forward(*operands),
        later,
    )
    phase((), lambda nothing: nothing, later)
    if aligned:
        held, other = later[0].value
        kernel_place = place
    else:
        wide = lax.all_gather(jnp.concatenate([gate_weight, up_weight], axis=1), everyone, axis=0, tiled=True)
        tall = lax.all_gather(down_weight, everyone, axis=0, tiled=True)
        tall = fold_rows(tall.reshape(32, -1, model_width))
        both = jnp.concatenate([wide.reshape(32, -1, 2 * hidden), tall], axis=2)
        both = both.reshape(16, 2, -1, 3 * hidden)
        held, other = both[:, 0], both[:, 1]
        kernel_place = place * jnp.array([0, 1], i32)
    layer_output, middle_grad, mixture_grad, small, out_keep, out_send, wide_keep, wide_send, down_keep, down_send = (
        feed_forward_both(source, mixture, weights, gains, upstream, held, other, kernel_place)
    )
    rest = []
    if aligned:
        pieces = [(wide_keep, wide_send), (down_keep, down_send), (out_keep, out_send)]
        rest = [Chain(sum_rows(pieces, own_part, -1))]
    table = jnp.zeros((32, 128), f32)
    count = pairs // calls
    waiting, started = [], []
    dnormed, draw = gains, gains
    keep_column = valid_float[:, None]
    for call in range(calls):
        keep, send, dnormed, draw, small, table = phase(
            (mixture_grad, small, table, dnormed, draw),
            lambda operands: attention_backward(
                call * count, count, own_part, queries, operands[0], keys, vals, gkeys, gvals, normed, turned, pooled, weights,
                logs, bias, feat_near, feat_far, feat_query, raw_pool, gains, kernel_place, *operands[1:],
            ),
            rest + started,
        )
        waiting.append((keep, send))
        if call > 0:
            started.append(Chain(core_steps(waiting, own_part)))
            waiting = []

    def return_rows(payload):
        return [lax.ppermute(payload[hop], seq, ring(seq_count, hop)) for hop in range(1, seq_count)]

    held = []
    phase(draw, lambda operands: held.append(return_rows(operands)), started[1:] + rest, started[1:])
    operands = held[0]
    sides = [sum((chain.value[side] for chain in started), []) for side in range(2)]
    last = Chain(scatter_steps(sides, labels, stages, 0))
    operands = phase(operands, lambda operands: operands, [last])
    input_delta = phase(
        operands,
        lambda received: input_gradient(source, keep_column, middle_grad, gains, dnormed, draw, received),
        [last],
        rest + [last],
    )
    phase((), lambda nothing: nothing, [last])
    total = last.value
    half = total.shape[0] // 2
    sides = [total[:half], total[half:]]
    extra = jnp.concatenate([side[half - 1] for side in sides], axis=-1)
    blocks_of_table = -(-4 * pairs // own_part)
    tables = extra[:, 128 : 128 + buckets * blocks_of_table].reshape(own_part, blocks_of_table, buckets)
    tables = tables.transpose(1, 0, 2).reshape((2,) + local_bias.shape)
    query_delta, key_delta, value_delta = (
        jnp.concatenate(
            [sides[pair % count][3 * (pair // count) + index] for pair in range(pairs)],
            axis=-1,
        )
        for index in range(3)
    )
    if aligned:
        total = rest[0].value[0]
        side, fold, half = total.shape[1] // 2, hidden // 2, model_width // 2
        left, right = total[:, :side], total[:, side:]
        gate_delta, up_delta = left[:, :hidden], right[:, :hidden]
        tall = jnp.concatenate([left[:, hidden : hidden + fold], right[:, hidden : hidden + fold]], axis=1)
        down_delta = unfold_rows(tall[None])[0]
        output_delta = jnp.concatenate([left[:, hidden + fold :], right[:, hidden + fold :]], axis=1)
    else:

        def whole_rows(keep, send):
            width = keep.shape[-1]
            both = jnp.stack([keep.reshape(16, -1, width), send.reshape(16, -1, width)], axis=1)
            return both.reshape(32, -1, width)

        def join(halves):
            return jnp.concatenate([halves[0], halves[1]], axis=-1)

        def scatter(grads):
            grads = grads.reshape(-1, grads.shape[-1])
            return lax.psum_scatter(grads, everyone, scatter_dimension=0, tiled=True).astype(f32)

        gate_delta = scatter(whole_rows(wide_keep[0], wide_send[0]))
        up_delta = scatter(whole_rows(wide_keep[1], wide_send[1]))
        output_delta = scatter(whole_rows(join(out_keep), join(out_send)))
        down_delta = scatter(unfold_rows(whole_rows(join(down_keep), join(down_send))))
    return (
        layer_output[None],
        input_delta[None],
        extra[:, 0],
        extra[:, 1],
        extra[:, 2],
        query_delta,
        key_delta,
        value_delta,
        output_delta,
        tables[0],
        tables[1],
        gate_delta,
        up_delta,
        down_delta,
    )


def solution(mesh):
    seq_size, batch_size = mesh.shape["seq"], mesh.shape["batch"]
    chips = Mesh(mesh.devices.reshape(2, seq_size // 2, batch_size // 2, 2), everyone)
    tokens = P(batch, seq, None)
    marks = P(batch, seq)
    row = P(everyone)
    matrix = P(everyone, None)
    whole = P()
    return jax.shard_map(
        on_device,
        mesh=chips,
        in_specs=(tokens, marks, marks, tokens, row, row, row)
        + (matrix,) * 4
        + (whole,) * 2
        + (matrix,) * 3,
        out_specs=(tokens, tokens, row, row, row)
        + (matrix,) * 4
        + (whole,) * 2
        + (matrix,) * 3,
        check_vma=False,
    )
```

```python
import functools

import jax
import jax.numpy as jnp
from jax import lax
from jax.experimental import pallas as pl
from jax.experimental.pallas import tpu as pltpu
from jax.sharding import Mesh
from jax.sharding import PartitionSpec as P

epsilon = 1e-06
boundaries = (12, 16, 23, 32, 46, 64, 91)
never = -1e30
seq = ("y", "x")
batch = ("z", "core")
everyone = seq + batch
bf16 = jnp.bfloat16
f32 = jnp.float32
i32 = jnp.int32
highest = lax.Precision.HIGHEST
calls = 3


def bucket_of(offset):
    distance = jnp.abs(offset)
    far_part = 8 + sum(((distance >= boundary).astype(i32) for boundary in boundaries))
    return 16 * (offset > 0).astype(i32) + jnp.where(distance < 8, distance, far_part)


def dot_nt(left, right):
    return lax.dot_general(left, right, (((1,), (1,)), ((), ())), preferred_element_type=f32)


def dot_nn(left, right):
    return lax.dot_general(left, right, (((1,), (0,)), ((), ())), preferred_element_type=f32)


def inverse_rms(values):
    return lax.rsqrt(jnp.mean(values * values, axis=-1, keepdims=True) + epsilon)


def norm_gradient(values, inverse, gain, grad):
    weighted = grad * gain
    mean = jnp.mean(weighted * values, axis=-1, keepdims=True)
    return inverse * weighted - (inverse * inverse * inverse * mean) * values


def store_halves(keep_ref, send_ref, index, value, core, part):
    rows, width = value.shape
    value = value.reshape(rows // (2 * part), 2, part, width)
    first, second = value[:, 0].reshape(rows // 2, width), value[:, 1].reshape(rows // 2, width)
    keep_ref[index] = jnp.where(core == 0, first, second).astype(bf16)
    send_ref[index] = jnp.where(core == 0, second, first).astype(bf16)


def stack_heads(rows):
    lane = lax.broadcasted_iota(i32, rows.shape, 1)
    zero = jnp.zeros_like(rows)
    return jnp.concatenate(
        [jnp.where(lane < 64, rows, zero), jnp.where(lane < 64, zero, rows)], axis=0
    )


def unstack_heads(wide):
    row = lax.broadcasted_iota(i32, (128, 128), 0)
    return jnp.where(row < 64, wide[:, :128], wide[:, 128:]).T


def upper_band():
    key = lax.broadcasted_iota(i32, (128, 256), 0)
    query = lax.broadcasted_iota(i32, (128, 256), 1) & 127
    return key > query


def spread_band(upper, own, merged):
    zero = jnp.zeros_like(merged)
    return jnp.concatenate(
        [jnp.where(upper, merged, zero), own, jnp.where(upper, zero, merged)], axis=0
    ).astype(bf16)


def window_of(block):
    return pl.ds(pl.multiple_of(block * 128, 128), 384)


def rows_of(block):
    return pl.ds(pl.multiple_of(block * 128, 128), 128)


def slot_lanes():
    row = lax.broadcasted_iota(i32, (256, 128), 0)
    lane = lax.broadcasted_iota(i32, (256, 128), 1)
    hit = (lane < 48) & ((lane & 15) == (row // 128) * 8 + (row % 128) // 16)
    return hit.astype(f32).astype(bf16)


def block_scores(block, upper, on_slot, query_two, key_ref, gkey_ref, bias_ref, klocal_ref, kglobal_ref, qfeat_ref):
    slots = gkey_ref.shape[0]
    window = window_of(block)
    segment_lanes = qfeat_ref[rows_of(block), :]
    features = jnp.concatenate([segment_lanes, segment_lanes], axis=0) + on_slot
    query_wide = jnp.concatenate([query_two, features], axis=1)
    key_wide = jnp.concatenate([key_ref[window, :], klocal_ref[window, :]], axis=1)
    local = dot_nt(key_wide, query_wide)
    own = local[128:256] + bias_ref[0, 0:128]
    merged = jnp.where(upper, local[0:128], local[256:384]) + bias_ref[0, 128:256]
    far_rows = pl.ds(pl.multiple_of(block * slots, 128), slots)
    gkey_wide = jnp.concatenate([gkey_ref[...], kglobal_ref[far_rows, :]], axis=1)
    return own, merged, dot_nt(gkey_wide, query_wide)


def attend_forward(
    source_ref, raw_ref, gain_ref, wq_ref, wk_ref, wv_ref, offsets_ref, klocal_ref, kglobal_ref, qfeat_ref,
    bias_ref, out_ref, log_ref, query_ref, key_ref, value_ref, gkey_ref, gvalue_ref, normed_ref, gains_ref,
    normed_turned, pooled_turned, pooled_ref, value_turned, gvalue_turned,
):
    rows = query_ref.shape[0]
    slots = gkey_ref.shape[0]

    @pl.when(pl.program_id(0) == 0)
    def start():
        turned = gain_ref[...].astype(f32).T
        gains_ref[...] = turned[0:8]
        gain_one, gain_pool = turned[0:1], turned[1:2]

        def norm_rows(index, carry):
            part = pl.ds(pl.multiple_of(index * 128, 128), 128)
            values = source_ref[part, :].astype(f32)
            low = (values * inverse_rms(values) * gain_one).astype(bf16)
            normed_ref[part, :] = low
            normed_turned[:, part] = low.T
            return carry

        lax.fori_loop(0, (rows + 256) // 128, norm_rows, 0)

        def pool_rows(index, carry):
            part = pl.ds(pl.multiple_of(index * 128, 128), 128)
            values = raw_ref[part, :].astype(f32) * gain_one
            low = (values * inverse_rms(values) * gain_pool).astype(bf16)
            pooled_ref[part, :] = low
            pooled_turned[:, part] = low.T
            return carry

        lax.fori_loop(0, slots // 128, pool_rows, 0)

    lane = lax.broadcasted_iota(i32, (256, 128), 1)
    spread = []
    for head in range(2):
        mine = jnp.where(lane == 2 * pl.program_id(0) + head, offsets_ref[...], 0.0)
        spread.append(jnp.broadcast_to(jnp.sum(mine, axis=1, keepdims=True), (256, 128)))
    lane_of = lax.broadcasted_iota(i32, (256, 256), 1)
    bias_ref[0] = align_offsets(jnp.concatenate(spread, axis=1), lane_of & 127, 7, -1)

    query_ref[...] = dot_nn(normed_ref[128 : 128 + rows, :], wq_ref[...]).astype(bf16)
    w_two = jnp.concatenate([wk_ref[...], wv_ref[...]], axis=1)
    two = dot_nn(normed_ref[...], w_two).astype(bf16)
    key_ref[...] = two[:, :128]
    value_ref[...] = two[:, 128:]
    value_turned[...] = two[:, 128:].T
    two = dot_nn(pooled_ref[...], w_two).astype(bf16)
    gkey_ref[...] = two[:, :128]
    gvalue_ref[...] = two[:, 128:]
    gvalue_turned[...] = two[:, 128:].T
    upper = upper_band()
    on_slot = slot_lanes()

    def step(block, carry):
        window = window_of(block)
        query_two = stack_heads(query_ref[rows_of(block), :])
        own, merged, far = block_scores(
            block, upper, on_slot, query_two, key_ref, gkey_ref, bias_ref, klocal_ref, kglobal_ref, qfeat_ref
        )
        peak = jnp.maximum(
            jnp.maximum(
                jnp.max(own, axis=0, keepdims=True), jnp.max(merged, axis=0, keepdims=True)
            ),
            jnp.max(far, axis=0, keepdims=True),
        )
        own, merged, far = jnp.exp(own - peak), jnp.exp(merged - peak), jnp.exp(far - peak)
        total = (
            jnp.sum(own, axis=0, keepdims=True)
            + jnp.sum(merged, axis=0, keepdims=True)
            + jnp.sum(far, axis=0, keepdims=True)
        )
        near_low = spread_band(upper, own, merged)
        wide = dot_nn(value_turned[:, window], near_low) + dot_nn(
            gvalue_turned[...], far.astype(bf16)
        )
        out_ref[rows_of(block), :] = unstack_heads(wide * (1.0 / total)).astype(bf16)
        log_ref[0, pl.ds(block, 1), :] = peak + jnp.log(total)
        return carry

    lax.fori_loop(0, rows // 128, step, 0, unroll=8)


def align_offsets(sums, step_of_lane, bits, sign):
    for bit in range(bits):
        shift = sign * (1 << bit)
        moved = jnp.concatenate([sums[shift:], sums[:shift]], axis=0)
        sums = jnp.where((step_of_lane >> bit) & 1 == 1, moved, sums)
    return sums


def two_totals(left, right):
    lane = lax.broadcasted_iota(i32, (left.shape[0], 128), 1)
    first = jnp.sum(left, axis=1, keepdims=True)
    second = jnp.sum(right, axis=1, keepdims=True)
    return jnp.where(lane == 0, first, jnp.where(lane == 1, second, 0.0))


def add_buckets(table_ref, sums, offset, head):
    hit = (bucket_of(offset) == lax.broadcasted_iota(i32, sums.shape, 1)).astype(f32)
    totals = lax.dot_general(
        sums, hit, (((0,), (0,)), ((), ())), precision=highest, preferred_element_type=f32
    )
    row = lax.broadcasted_iota(i32, table_ref.shape, 0)
    table_ref[...] += jnp.where(
        row == head, totals[0:1], jnp.where(row == head + 1, totals[1:2], 0.0)
    )


def attend_backward(
    last, part, own_part, first_pair, query_ref, grad_ref, key_ref, value_ref, gkey_ref, gvalue_ref, normed_ref, normed_turned, pooled_turned, wq_ref, wk_ref, wv_ref,
    log_ref, bias_ref, klocal_ref, kglobal_ref, qfeat_ref, raw_ref, gains_ref, place_ref, old_small_ref, old_table_ref, old_dnormed_ref, old_draw_ref,
    keep_ref, send_ref, dnormed_ref, draw_ref, small_ref, table_ref,
    dnormed_sum, dpooled_sum, draw_sum, key_turned, gkey_turned, dquery, key_sum, value_sum, gkey_sum, gvalue_sum, near_sum, far_sum,
):
    rows = query_ref.shape[0]
    slots = gkey_ref.shape[0]

    @pl.when(pl.program_id(0) == 0)
    def start():
        dnormed_sum[...] = jnp.zeros_like(dnormed_sum)
        dpooled_sum[...] = jnp.zeros_like(dpooled_sum)
        table_ref[...] = old_table_ref[...]

    key_turned[...] = key_ref[...].T
    gkey_turned[...] = gkey_ref[...].T
    for total_ref in (key_sum, value_sum, gkey_sum, gvalue_sum, near_sum, far_sum):
        total_ref[...] = jnp.zeros_like(total_ref)
    upper = upper_band()
    on_slot = slot_lanes()
    lane = lax.broadcasted_iota(i32, (256, 128), 0)
    column = lax.broadcasted_iota(i32, (256, 128), 1)
    slot_column = (lane // 128) * 64 + (lane % 128) // 16

    def step(block, carry):
        window = window_of(block)
        query_two = stack_heads(query_ref[rows_of(block), :])
        grad_two = stack_heads(grad_ref[rows_of(block), :])
        own, merged, far = block_scores(
            block, upper, on_slot, query_two, key_ref, gkey_ref, bias_ref, klocal_ref, kglobal_ref, qfeat_ref
        )
        logs = log_ref[0, pl.ds(block, 1), :]
        own, merged, far = jnp.exp(own - logs), jnp.exp(merged - logs), jnp.exp(far - logs)
        value_sum[window, :] += dot_nn(spread_band(upper, own, merged), grad_two)
        gvalue_sum[...] += dot_nn(far.astype(bf16), grad_two)
        near_dot = dot_nt(value_ref[window, :], grad_two)
        own_dot = near_dot[128:256]
        merged_dot = jnp.where(upper, near_dot[0:128], near_dot[256:384])
        far_dot = dot_nt(gvalue_ref[...], grad_two)
        centre = (
            jnp.sum(own * own_dot, axis=0, keepdims=True)
            + jnp.sum(merged * merged_dot, axis=0, keepdims=True)
            + jnp.sum(far * far_dot, axis=0, keepdims=True)
        )
        own = own * (own_dot - centre)
        merged = merged * (merged_dot - centre)
        far = (far * (far_dot - centre)).astype(bf16)
        near_sum[0:128, :] += own
        near_sum[128:256, :] += merged
        choose = (column == slot_column + block * 8).astype(bf16)
        far_sum[...] += dot_nn(far, choose)
        near_low = spread_band(upper, own, merged)
        key_sum[window, :] += dot_nn(near_low, query_two)
        gkey_sum[...] += dot_nn(far, query_two)
        wide = dot_nn(key_turned[:, window], near_low) + dot_nn(gkey_turned[...], far)
        dquery[rows_of(block), :] = unstack_heads(wide).astype(bf16)
        return carry

    lax.fori_loop(0, rows // 128, step, 0, unroll=8)

    core, first_slot = place_ref[0], place_ref[1]
    head = 2 * (first_pair + pl.program_id(0))
    lane_of = lax.broadcasted_iota(i32, (256, 256), 1)
    near = align_offsets(near_sum[...], lane_of & 127, 7, 1)
    near = two_totals(near[:, :128], near[:, 128:])
    place = lax.broadcasted_iota(i32, (256, 128), 0)
    add_buckets(table_ref, near, ((place + 128) & 255) - 128, head)
    lane_of = lax.broadcasted_iota(i32, (slots + 64, 128), 1)
    far = jnp.concatenate([far_sum[...], jnp.zeros((64, 128), f32)], axis=0)
    far = align_offsets(far, lane_of & 63, 6, 1)
    far = two_totals(jnp.where(lane_of < 64, far, 0.0), jnp.where(lane_of < 64, 0.0, far))
    place = lax.broadcasted_iota(i32, (slots + 64, 128), 0)
    heads = normed_ref.shape[1] // 64
    add_buckets(table_ref, far, jnp.where(place < slots, place, place - slots - 64) - first_slot, heads + head)

    width = normed_ref.shape[1]
    grad_low = dquery[...]
    dwq = dot_nn(normed_turned[:, 128 : 128 + rows], grad_low)
    planes = 4 if last else 3
    lead = pl.program_id(0) * planes
    store_halves(keep_ref, send_ref, lead, dwq, core, part)
    dnormed_sum[128 : 128 + rows, :] += dot_nt(grad_low, wq_ref[...])
    two = jnp.concatenate([key_sum[...], value_sum[...]], axis=1).astype(bf16)
    gtwo = jnp.concatenate([gkey_sum[...], gvalue_sum[...]], axis=1).astype(bf16)
    w_two = jnp.concatenate([wk_ref[...], wv_ref[...]], axis=1)
    dw_two = dot_nn(normed_turned[...], two) + dot_nn(pooled_turned[...], gtwo)
    store_halves(keep_ref, send_ref, lead + 1, dw_two[:, :128], core, part)
    store_halves(keep_ref, send_ref, lead + 2, dw_two[:, 128:], core, part)
    dnormed_sum[...] += dot_nt(two, w_two)
    dpooled_sum[...] += dot_nt(gtwo, w_two)

    @pl.when(pl.program_id(0) == pl.num_programs(0) - 1)
    def finish():
        gain_one, gain_pool = gains_ref[0:1, :], gains_ref[1:2, :]
        small_ref[...] = old_small_ref[...]

        def norm_rows(index, carry):
            part = pl.ds(pl.multiple_of(index * 128, 128), 128)
            grad = dnormed_sum[part, :]
            total = grad if first_pair == 0 else grad + old_dnormed_ref[part, :].astype(f32)
            dnormed_ref[part, :] = total.astype(bf16)
            return carry + jnp.sum(grad * normed_ref[part, :].astype(f32), axis=0, keepdims=True)

        norm_part = lax.fori_loop(0, (rows + 256) // 128, norm_rows, jnp.zeros((1, width), f32))
        norm_part = norm_part / gain_one

        def pool_rows(index, carry):
            norm_part, pool_part = carry
            part = pl.ds(pl.multiple_of(index * 128, 128), 128)
            raw = raw_ref[part, :].astype(f32)
            values = raw * gain_one
            inverse = inverse_rms(values)
            grad = dpooled_sum[part, :]
            back = norm_gradient(values, inverse, gain_pool, grad)
            total = back if first_pair == 0 else back + old_draw_ref[part, :].astype(f32)
            draw_sum[part, :] = total.astype(bf16)
            return (
                norm_part + jnp.sum(back * raw, axis=0, keepdims=True),
                pool_part + jnp.sum(grad * values * inverse, axis=0, keepdims=True),
            )

        norm_part, pool_part = lax.fori_loop(
            0, slots // 128, pool_rows, (norm_part, jnp.zeros((1, width), f32))
        )
        small_ref[0:1, :] += norm_part
        small_ref[1:2, :] += pool_part
        if not last:
            draw_ref[...] = draw_sum[...]
            return
        own_slots = rows // 16
        me = lax.axis_index("y") * lax.axis_size("x") + lax.axis_index("x")
        for hop in range(draw_ref.shape[0]):
            target = lax.rem(me + hop, draw_ref.shape[0])
            draw_ref[hop, :own_slots, :] = draw_sum[
                pl.ds(pl.multiple_of(target * own_slots, own_slots), own_slots), :
            ]
            before = target == me - 1

            @pl.when(before)
            def head():
                draw_ref[hop, own_slots:, :] = dnormed_ref[:128, :]

            @pl.when(jnp.logical_not(before))
            def tail():
                draw_ref[hop, own_slots:, :] = dnormed_ref[rows + 128 :, :]

        rows_of_small = jnp.concatenate([small_ref[...], jnp.zeros((120, width), f32)], axis=0)
        tables = jnp.zeros((width, 128), f32)
        row = lax.broadcasted_iota(i32, (width, 32), 0)
        column = lax.broadcasted_iota(i32, (width, 32), 1)
        for block in range(-(-2 * heads // own_part)):
            chosen = (column == row % own_part + block * own_part).astype(f32)
            shifted = table_ref[...]
            if block:
                shifted = jnp.concatenate(
                    [shifted[:, 128 - 32 * block :], shifted[:, : 128 - 32 * block]], axis=1
                )
            tables = tables + jnp.dot(
                chosen, shifted, precision=highest, preferred_element_type=f32
            )
        store_halves(keep_ref, send_ref, 3, rows_of_small.T, core, part)
        store_halves(keep_ref, send_ref, keep_ref.shape[0] - 1, tables, core, part)


def columns(rows, first):
    return pl.BlockSpec((rows, 128), lambda pair: (0, pair + first))


def of_pair(first, *shape):
    zeros = (0,) * len(shape)
    return pl.BlockSpec((1,) + shape, lambda pair: (pair + first,) + zeros)


def fixed(*shape):
    zeros = (0,) * len(shape)
    return pl.BlockSpec(shape, lambda pair: zeros, pipeline_mode=pl.Buffered(1))


def fixed_out(*shape):
    zeros = (0,) * len(shape)
    return pl.BlockSpec(shape, lambda pair: zeros)


def attention_forward(source_ext, raw_pool, weights, bias, klocal, kglobal, qfeat):
    width = source_ext.shape[1]
    rows = source_ext.shape[0] - 256
    slots = raw_pool.shape[0]
    blocks = rows // 128
    pairs = width // 128
    return pl.pallas_call(
        attend_forward,
        grid=(pairs,),
        in_specs=[
            fixed(rows + 256, width),
            fixed(slots, width),
            pl.BlockSpec((width, 128), lambda pair: (0, 4 * pairs), pipeline_mode=pl.Buffered(1)),
            columns(width, 0),
            columns(width, pairs),
            columns(width, 2 * pairs),
            fixed(256, 128),
            fixed(rows + 256, 128),
            columns(blocks * slots, 0),
            fixed(rows, 128),
        ],
        out_specs=[
            of_pair(0, 256, 256),
            columns(rows, 0),
            of_pair(0, blocks, 256),
            columns(rows, 0),
            columns(rows + 256, 0),
            columns(rows + 256, 0),
            columns(slots, 0),
            columns(slots, 0),
            fixed_out(rows + 256, width),
            fixed_out(8, width),
            fixed_out(width, rows + 256),
            fixed_out(width, slots),
        ],
        out_shape=[
            jax.ShapeDtypeStruct((pairs, 256, 256), f32),
            jax.ShapeDtypeStruct((rows, width), bf16),
            jax.ShapeDtypeStruct((pairs, blocks, 256), f32),
            jax.ShapeDtypeStruct((rows, width), bf16),
            jax.ShapeDtypeStruct((rows + 256, width), bf16),
            jax.ShapeDtypeStruct((rows + 256, width), bf16),
            jax.ShapeDtypeStruct((slots, width), bf16),
            jax.ShapeDtypeStruct((slots, width), bf16),
            jax.ShapeDtypeStruct((rows + 256, width), bf16),
            jax.ShapeDtypeStruct((8, width), f32),
            jax.ShapeDtypeStruct((width, rows + 256), bf16),
            jax.ShapeDtypeStruct((width, slots), bf16),
        ],
        scratch_shapes=[pltpu.VMEM((slots, width), bf16), pltpu.VMEM((128, rows + 256), bf16), pltpu.VMEM((128, slots), bf16)],
        compiler_params=pltpu.CompilerParams(vmem_limit_bytes=52 << 20),
        cost_estimate=pl.CostEstimate(
            flops=30 * rows * (384 + slots) * width, bytes_accessed=24 << 20, transcendentals=0
        ),
        name="attend_forward",
    )(source_ext, raw_pool, weights, weights, weights, weights, bias, klocal, kglobal, qfeat)


def attention_backward(
    first, count, part, queries, grads, keys, values, gkeys, gvalues, normed, turned, pooled, weights, logs, bias, klocal,
    kglobal, qfeat, raw_pool, gains, place, old_small, old_table, old_dnormed, old_draw,
):
    rows, width = queries.shape
    slots = gkeys.shape[0]
    blocks = rows // 128
    pairs = width // 128
    lead = count * (4 if first + count == pairs else 3)
    own_slots = rows // 16
    draw_shape = (slots // own_slots, own_slots + 128, width) if first + count == pairs else (slots, width)
    return pl.pallas_call(
        functools.partial(attend_backward, first + count == pairs, width // 32, part, first),
        grid=(count,),
        in_specs=[
            columns(rows, first),
            columns(rows, first),
            columns(rows + 256, first),
            columns(rows + 256, first),
            columns(slots, first),
            columns(slots, first),
            fixed(rows + 256, width),
            fixed(width, rows + 256),
            fixed(width, slots),
            columns(width, first),
            columns(width, pairs + first),
            columns(width, 2 * pairs + first),
            of_pair(first, blocks, 256),
            of_pair(first, 256, 256),
            fixed(rows + 256, 128),
            columns(blocks * slots, first),
            fixed(rows, 128),
            fixed(slots, width),
            fixed(8, width),
            pl.BlockSpec(memory_space=pltpu.SMEM),
            fixed(8, width),
            fixed(32, 128),
            fixed(rows + 256, width) if first else fixed(8, width),
            fixed(slots, width) if first else fixed(8, width),
        ],
        out_specs=[
            fixed_out(lead, width // 2, 128),
            fixed_out(lead, width // 2, 128),
            fixed_out(rows + 256, width),
            fixed_out(*draw_shape),
            fixed_out(8, width),
            fixed_out(32, 128),
        ],
        out_shape=[
            jax.ShapeDtypeStruct((lead, width // 2, 128), bf16),
            jax.ShapeDtypeStruct((lead, width // 2, 128), bf16),
            jax.ShapeDtypeStruct((rows + 256, width), bf16),
            jax.ShapeDtypeStruct(draw_shape, bf16),
            jax.ShapeDtypeStruct((8, width), f32),
            jax.ShapeDtypeStruct((32, 128), f32),
        ],
        scratch_shapes=[
            pltpu.VMEM((rows + 256, width), f32),
            pltpu.VMEM((slots, width), f32),
            pltpu.VMEM((slots, width), bf16),
            pltpu.VMEM((128, rows + 256), bf16),
            pltpu.VMEM((128, slots), bf16),
            pltpu.VMEM((rows, 128), bf16),
            pltpu.VMEM((rows + 256, 128), f32),
            pltpu.VMEM((rows + 256, 128), f32),
            pltpu.VMEM((slots, 128), f32),
            pltpu.VMEM((slots, 128), f32),
            pltpu.VMEM((256, 256), f32),
            pltpu.VMEM((slots, 128), f32),
        ],
        compiler_params=pltpu.CompilerParams(vmem_limit_bytes=52 << 20),
        cost_estimate=pl.CostEstimate(
            flops=60 * rows * (384 + slots) * 128 * count, bytes_accessed=count << 22, transcendentals=0
        ),
        name="attend_backward",
    )(
        queries, grads, keys, values, gkeys, gvalues, normed, turned, pooled, weights, weights, weights, logs, bias, klocal,
        kglobal, qfeat, raw_pool, gains, place, old_small, old_table, old_dnormed, old_draw,
    )


def interleave(held, other, core):
    held, other = held.astype(f32), other.astype(f32)
    both = jnp.stack([jnp.where(core == 0, held, other), jnp.where(core == 0, other, held)], axis=1)
    return both.reshape(-1, both.shape[-1])


def fold_rows(tall):
    rows, width = tall.shape[1:]
    return jnp.concatenate(
        [
            jnp.concatenate(
                [tall[:, r : r + 8, c : c + 256] for r in range(0, rows, 8)], axis=2
            )
            for c in range(0, width, 256)
        ],
        axis=1,
    )


unfold_rows = fold_rows


def pack_weights(wq_ref, wk_ref, wv_ref, wo_ref, gains_ref, gate_ref, up_ref, down_ref, first_ref, second_ref):
    width = wq_ref.shape[1]
    for index, weight_ref in enumerate((wq_ref, wk_ref, wv_ref, wo_ref)):
        first_ref[:, index * width : (index + 1) * width] = weight_ref[...]
    first_ref[:, 4 * width :] = gains_ref[...]
    if second_ref.shape[1] > 128:
        hidden = gate_ref.shape[1]
        second_ref[:, :hidden] = gate_ref[...]
        second_ref[:, hidden : 2 * hidden] = up_ref[...]
        second_ref[:, 2 * hidden :] = fold_rows(down_ref[...].astype(f32)[None])[0].astype(bf16)


def pack_tokens(source_ref, keep_ref, marks_ref, shared_ref):
    width = source_ref.shape[1]
    slots = source_ref.shape[0] // 16
    for slot in range(0, slots, 16):
        rows = slice(slot * 16, slot * 16 + 256)
        values = source_ref[rows, :].astype(f32)
        values = values * (inverse_rms(values) * keep_ref[rows, :])
        shared_ref[0, slot : slot + 16, :] = jnp.sum(values.reshape(16, 16, width), axis=1).astype(bf16)
    marks = marks_ref[...].astype(f32)
    rest = jnp.zeros((marks.shape[0], width - 128), f32)
    count = slots + marks.shape[0]
    shared_ref[0, slots:count, :] = jnp.concatenate([marks, rest], axis=1).astype(bf16)
    for target in range(1, shared_ref.shape[0]):
        shared_ref[target, :count, :] = shared_ref[0, :count, :]
    for target in range(shared_ref.shape[0]):
        before = target == lax.axis_index("y") * lax.axis_size("x") + lax.axis_index("x") - 1

        @pl.when(before)
        def head():
            shared_ref[target, count:, :] = source_ref[:128, :]

        @pl.when(jnp.logical_not(before))
        def tail():
            shared_ref[target, count:, :] = source_ref[source_ref.shape[0] - 128 :, :]


def pack_all(wq, wk, wv, wo, gains, gate, up, down, aligned):
    part, width = wq.shape
    return pl.pallas_call(
        pack_weights,
        out_shape=[
            jax.ShapeDtypeStruct((part, 4 * width + 128), bf16),
            jax.ShapeDtypeStruct((part, 3 * gate.shape[1] if aligned else 128), bf16),
        ],
        compiler_params=pltpu.CompilerParams(vmem_limit_bytes=60 << 20),
        name="pack_weights",
    )(wq, wk, wv, wo, gains, gate, up, down)


def pack_shared(source, keep, marks, count):
    rows, width = source.shape
    return pl.pallas_call(
        pack_tokens,
        out_shape=jax.ShapeDtypeStruct((count, rows // 16 + marks.shape[0] + 128, width), bf16),
        compiler_params=pltpu.CompilerParams(vmem_limit_bytes=60 << 20),
        name="pack_tokens",
    )(source, keep, marks)


def feed_forward(
    source_ref, mixture_ref, wo_ref, gains_ref, cot_ref, gate_held, gate_other, up_held, up_other, down_held, down_other,
    place_ref,
    out_ref, middle_grad_ref, dmixture_ref, dgain_ref, keep_out, send_out, keep_wide, send_wide, keep_down, send_down,
    middle, normed, turned, out_sum, grad_sum, product, gate_low, lift_low, wg_ref, wu_ref, wd_ref,
):
    rows, width = source_ref.shape
    part_rows = 256
    parts = rows // part_rows
    gain = gains_ref[2:3, :]
    core = place_ref[0]
    wg_ref[...] = interleave(gate_held[...], gate_other[...], core).astype(bf16)
    wu_ref[...] = interleave(up_held[...], up_other[...], core).astype(bf16)
    wd_ref[...] = interleave(
        unfold_rows(down_held[...].astype(f32)), unfold_rows(down_other[...].astype(f32)), core
    ).astype(bf16)

    @pl.when(pl.program_id(0) == 0)
    def start():
        def norm_rows(index, carry):
            part = pl.ds(pl.multiple_of(index * 256, 256), 256)
            values = source_ref[part, :].astype(f32) + dot_nn(mixture_ref[part, :], wo_ref[...])
            middle[part, :] = values
            low = (values * inverse_rms(values) * gain).astype(bf16)
            normed[part, :] = low
            turned[:, part] = low.T
            return carry

        lax.fori_loop(0, rows // 256, norm_rows, 0, unroll=True)
        out_sum[...] = jnp.zeros_like(out_sum)
        grad_sum[...] = jnp.zeros_like(grad_sum)

    root = 0.7978845608028654
    for index in range(parts):
        part = slice(index * part_rows, (index + 1) * part_rows)
        low = normed[part, :]
        gate_pre = dot_nn(low, wg_ref[...])
        lift_pre = dot_nn(low, wu_ref[...])
        grad = dot_nt(cot_ref[part, :], wd_ref[...])
        square = gate_pre * gate_pre
        bent = jnp.tanh(gate_pre * (root + (root * 0.044715) * square))
        half = 0.5 + 0.5 * bent
        gelu = gate_pre * half
        slope = half + gelu * (1.0 - bent) * (root + (3 * root * 0.044715) * square)
        product[part, :] = (gelu * lift_pre).astype(bf16)
        lift_low[part, :] = (grad * gelu).astype(bf16)
        gate_low[part, :] = (grad * lift_pre * slope).astype(bf16)
        out_sum[part, :] += dot_nn(product[part, :], wd_ref[...])
        grad_sum[part, :] += dot_nt(gate_low[part, :], wg_ref[...]) + dot_nt(
            lift_low[part, :], wu_ref[...]
        )
    wide_part, down_part = width // 32, down_held.shape[1] * down_held.shape[2] // width
    store_halves(keep_wide, send_wide, 0, dot_nn(turned[...], gate_low[...]), core, wide_part)
    store_halves(keep_wide, send_wide, 1, dot_nn(turned[...], lift_low[...]), core, wide_part)
    value = dot_nn(product[...].T, cot_ref[...]).reshape(-1, 2, down_part, width)
    first, second = value[:, 0], value[:, 1]
    for half_ref, chosen in (
        (keep_down, jnp.where(core == 0, first, second)),
        (send_down, jnp.where(core == 0, second, first)),
    ):
        folded = fold_rows(chosen)
        folded = folded.reshape(-1, folded.shape[2]).astype(bf16)
        half_ref[0], half_ref[1] = folded[:, : folded.shape[1] // 2], folded[:, folded.shape[1] // 2 :]

    @pl.when(pl.program_id(0) == pl.num_programs(0) - 1)
    def finish():
        dgain_ref[...] = jnp.zeros_like(dgain_ref)

        def back_rows(index, carry):
            part = pl.ds(pl.multiple_of(index * 256, 256), 256)
            values = middle[part, :]
            out_ref[part, :] = (values + out_sum[part, :]).astype(bf16)
            inverse = inverse_rms(values)
            grad = grad_sum[part, :]
            dgain_ref[2:3, :] += jnp.sum(grad * values * inverse, axis=0, keepdims=True)
            total = cot_ref[part, :].astype(f32) + norm_gradient(values, inverse, gain, grad)
            middle_grad_ref[part, :] = total
            low = total.astype(bf16)
            normed[part, :] = low
            dmixture_ref[part, :] = dot_nt(low, wo_ref[...]).astype(bf16)
            turned[:, part] = mixture_ref[part, :].T
            return carry

        lax.fori_loop(0, rows // 256, back_rows, 0, unroll=True)
        for side in range(2):
            half = slice(side * width // 2, (side + 1) * width // 2)
            store_halves(keep_out, send_out, side, dot_nn(turned[...], normed[:, half]), core, width // 32)


def feed_forward_both(source, mixture, weights, gains, cotangent, held, other, place):
    rows, width = source.shape
    groups, part, total = held.shape
    hidden = total // 3
    tile = 512
    tiles = hidden // tile
    step_groups = groups // tiles
    gate_spec = pl.BlockSpec((groups, part, tile), lambda step: (0, 0, step))
    up_spec = pl.BlockSpec((groups, part, tile), lambda step: (0, 0, step + tiles))
    down_spec = pl.BlockSpec((step_groups, part, hidden), lambda step: (step, 0, 2))
    wide_spec = pl.BlockSpec((2, width // 2, tile), lambda step: (0, 0, step))
    fold_spec = pl.BlockSpec((2, step_groups * part, hidden // 2), lambda step: (0, step, 0))
    out_spec = fixed_out(2, width // 2, width // 2)
    return pl.pallas_call(
        feed_forward,
        grid=(tiles,),
        in_specs=[
            fixed(rows, width),
            fixed(rows, width),
            pl.BlockSpec((width, width), lambda step: (0, 3), pipeline_mode=pl.Buffered(1)),
            fixed(8, width),
            fixed(rows, width),
            gate_spec,
            gate_spec,
            up_spec,
            up_spec,
            down_spec,
            down_spec,
            pl.BlockSpec(memory_space=pltpu.SMEM),
        ],
        out_specs=[
            fixed_out(rows, width),
            fixed_out(rows, width),
            fixed_out(rows, width),
            fixed_out(8, width),
            out_spec,
            out_spec,
            wide_spec,
            wide_spec,
            fold_spec,
            fold_spec,
        ],
        out_shape=[
            jax.ShapeDtypeStruct((rows, width), bf16),
            jax.ShapeDtypeStruct((rows, width), f32),
            jax.ShapeDtypeStruct((rows, width), bf16),
            jax.ShapeDtypeStruct((8, width), f32),
            jax.ShapeDtypeStruct((2, width // 2, width // 2), bf16),
            jax.ShapeDtypeStruct((2, width // 2, width // 2), bf16),
            jax.ShapeDtypeStruct((2, width // 2, hidden), bf16),
            jax.ShapeDtypeStruct((2, width // 2, hidden), bf16),
            jax.ShapeDtypeStruct((2, width // 2, hidden // 2), bf16),
            jax.ShapeDtypeStruct((2, width // 2, hidden // 2), bf16),
        ],
        scratch_shapes=[
            pltpu.VMEM((rows, width), f32),
            pltpu.VMEM((rows, width), bf16),
            pltpu.VMEM((width, rows), bf16),
            pltpu.VMEM((rows, width), f32),
            pltpu.VMEM((rows, width), f32),
            pltpu.VMEM((rows, tile), bf16),
            pltpu.VMEM((rows, tile), bf16),
            pltpu.VMEM((rows, tile), bf16),
            pltpu.VMEM((width, tile), bf16),
            pltpu.VMEM((width, tile), bf16),
            pltpu.VMEM((tile, width), bf16),
        ],
        compiler_params=pltpu.CompilerParams(vmem_limit_bytes=60 << 20),
        cost_estimate=pl.CostEstimate(
            flops=20 * rows * width * hidden, bytes_accessed=40 << 20, transcendentals=0
        ),
        name="feed_forward",
    )(source, mixture, weights, gains, cotangent, held, other, held, other, held, other, place)


def source_gradient(source_ref, keep_ref, middle_grad_ref, gains_ref, upper_ref, lower_ref, *refs):
    step, steps = pl.program_id(0), pl.num_programs(0)
    pooled_refs, edge_refs, out_ref = refs[:-5], refs[-5:-1], refs[-1]
    rows, width = source_ref.shape
    pooled = pooled_refs[0][0].astype(f32)
    for other_ref in pooled_refs[1:]:
        pooled = pooled + other_ref[...].astype(f32)
    pooled = jnp.broadcast_to(pooled[:, None, :], (rows // 16, 16, width)).reshape(rows, width)
    me = lax.axis_index("y") * lax.axis_size("x") + lax.axis_index("x")
    before = (step == 0) & (me > 0)
    after = (step == steps - 1) & (me < len(pooled_refs) - 1)
    head, tail = (
        jnp.concatenate([first[...], second[...]], axis=0).astype(f32)
        for first, second in (edge_refs[:2], edge_refs[2:])
    )
    grad = jnp.concatenate(
        [
            upper_ref[...].astype(f32) + jnp.where(before, head, 0.0),
            lower_ref[...].astype(f32) + jnp.where(after, tail, 0.0),
        ],
        axis=0,
    )
    grad = grad + pooled * keep_ref[...]
    values = source_ref[...].astype(f32)
    out_ref[...] = middle_grad_ref[...] + norm_gradient(values, inverse_rms(values), gains_ref[0:1, :], grad)


def input_gradient(source, keep, middle_grad, gains, dnormed, payload, received):
    rows, width = source.shape
    tile = 256
    own_slots = rows // 16
    row_spec = pl.BlockSpec((tile, width), lambda step: (step, 0))
    edges = [
        pl.BlockSpec((64, width), lambda step, index=index: (own_slots // 64 + index, 0), pipeline_mode=pl.Buffered(1))
        for index in range(2)
    ]
    return pl.pallas_call(
        source_gradient,
        grid=(rows // tile,),
        in_specs=[
            row_spec,
            pl.BlockSpec((tile, 1), lambda step: (step, 0)),
            row_spec,
            fixed(8, width),
            pl.BlockSpec((128, width), lambda step: (1 + 2 * step, 0)),
            pl.BlockSpec((128, width), lambda step: (2 + 2 * step, 0)),
            pl.BlockSpec((1, tile // 16, width), lambda step: (0, step, 0)),
        ]
        + [pl.BlockSpec((tile // 16, width), lambda step: (step, 0)) for _ in received]
        + edges * 2,
        out_specs=row_spec,
        out_shape=jax.ShapeDtypeStruct((rows, width), f32),
        compiler_params=pltpu.CompilerParams(vmem_limit_bytes=60 << 20),
        cost_estimate=pl.CostEstimate(
            flops=20 * rows * width, bytes_accessed=14 << 20, transcendentals=0
        ),
        name="source_gradient",
    )(
        source, keep, middle_grad, gains, dnormed, dnormed, payload, *received, received[0], received[0], received[-1],
        received[-1],
    )


def near_offsets(local_bias):
    heads, buckets = local_bias.shape
    offset = (jnp.arange(256, dtype=i32) + 128) % 256 - 128
    table = (bucket_of(offset)[:, None] == jnp.arange(buckets, dtype=i32)).astype(f32)
    chosen = jnp.einsum("ob,hb->oh", table, local_bias, precision=highest)
    chosen = jnp.where((offset == -128)[:, None], never, chosen)
    return jnp.pad(chosen, ((0, 0), (0, 128 - heads)))


def far_features(global_bias, slot_segments, slot_live, first_slot, blocks):
    heads, buckets = global_bias.shape
    pairs = heads // 2
    slots = slot_segments.shape[0]
    wide = 8 * buckets + 8
    shape = (blocks * slots, wide)
    row = lax.broadcasted_iota(i32, shape, 0)
    column = lax.broadcasted_iota(i32, shape, 1)
    slot = row % slots
    query_slot = first_slot + (row // slots) * 8 + column // buckets
    code = jnp.tile(jnp.where(slot_live, slot_segments, 3), blocks)[:, None]
    picks = jnp.where(
        column < 8 * buckets,
        bucket_of(slot - query_slot) == column % buckets,
        code == column - 8 * buckets,
    ).astype(bf16)
    high = lax.reduce_precision(global_bias, 8, 7)
    middle = lax.reduce_precision(global_bias - high, 8, 7)
    lowest = lax.reduce_precision(global_bias - high - middle, 8, 7)
    parts = jnp.stack([high, middle, lowest]).reshape(3, pairs, 2, buckets)
    parts = parts.transpose(3, 1, 0, 2)
    same = jnp.eye(8, dtype=f32)[:, None, None, None, None, :]
    table = (parts[None, :, :, :, :, None] * same).reshape(8 * buckets, pairs, 48)
    table = jnp.pad(table, ((0, 8), (0, 0), (0, 80)))
    shape = (wide, 1, 128)
    lane = lax.broadcasted_iota(i32, shape, 2) - 48
    code_row = lax.broadcasted_iota(i32, shape, 0) - 8 * buckets
    barred = (code_row >= 0) & (lane >= 0) & (lane < 3) & (lane != code_row)
    table = jnp.where(barred, never, table).astype(bf16).reshape(wide, pairs * 128)
    return jnp.dot(picks, table, preferred_element_type=f32).astype(bf16)


def near_features(segments_ext, valid_ext):
    lane = lax.broadcasted_iota(i32, (segments_ext.shape[0], 128), 1)
    allowed = (segments_ext[:, None] == lane - 48) & (valid_ext[:, None] > 0)
    return jnp.where((lane >= 48) & (lane < 51) & ~allowed, never, 0.0).astype(bf16)


def query_features(own_segments):
    lane = lax.broadcasted_iota(i32, (own_segments.shape[0], 128), 1)
    return (own_segments[:, None] == lane - 48).astype(bf16)


def pick(values, index, dim):
    return lax.dynamic_index_in_dim(values, index, dim, keepdims=False)


def ring(size, hop):
    return [(i, (i + hop) % size) for i in range(size)]


def add_up(parts):
    if len(parts) == 1:
        return parts[0]
    return sum((part.astype(f32) for part in parts[1:]), parts[0].astype(f32))


def split_stage(side, labels, axis, join):
    size, me = lax.axis_size(axis), lax.axis_index(axis)
    dim = labels.index(axis) - len(labels) - 2 + side[0][0].ndim
    chosen = []
    for hop in range(size):
        pieces = [
            add_up([pick(part, (me + hop) % size, dim) for part in piece]).astype(bf16) for piece in side
        ]
        chosen.append(pieces[0] if len(pieces) == 1 else jnp.concatenate(pieces, axis=join))
    return chosen[1:], chosen[0]


def send_all(axis, pieces):
    size = lax.axis_size(axis)
    return [lax.ppermute(piece, axis, ring(size, hop + 1)) for hop, piece in enumerate(pieces)]


def place_stage(values, pieces, axis, dim):
    size, me = lax.axis_size(axis), lax.axis_index(axis)
    shape = values.shape[:dim] + (size,) + values.shape[dim:]
    out = lax.dynamic_update_index_in_dim(jnp.zeros(shape, values.dtype), values, me, dim)
    for hop, piece in enumerate(pieces):
        out = lax.dynamic_update_index_in_dim(out, piece, (me - hop - 1) % size, dim)
    return out


def half_of(width):
    return (width // 256) * 128


def scatter_steps(sides, labels, stages, join):
    labels = [list(labels) for _ in sides]
    for axes in stages:
        if axes == ("all z",):
            merged = [add_up(piece).astype(bf16) for side in sides for piece in side]
            merged = yield jnp.concatenate(merged, axis=join)
            dim = merged.ndim - 3
            got = yield lax.all_to_all(merged, "z", dim, dim, tiled=True)
            return jnp.sum(got.astype(f32), axis=dim)
        if len(axes) < len(sides):
            sides, labels = [[piece for side in sides for piece in side]], labels[:1]
        split = [split_stage(side, names, axis, join) for side, names, axis in zip(sides, labels, axes)]
        sends = yield [send for send, _ in split]
        gots = yield [send_all(axis, send) for axis, send in zip(axes, sends)]
        sides = [[[keep] + got] for (_, keep), got in zip(split, gots)]
        for names, axis in zip(labels, axes):
            names.remove(axis)
    return add_up(sides[0][0])


across = (("x", "y"), ("y", "x"))


stages = (("x", "y"), ("y", "x"), ("z",))
labels = ("y", "x", "z")


def core_steps(pairs, part):
    y, x, z, _ = (lax.axis_size(axis) for axis in everyone)
    keeps, sends = zip(*pairs)
    if part != keeps[0].shape[1] // 16:
        keeps, sends = zip(*(regroup(keep, send, part) for keep, send in pairs))
    sends = yield sends
    gots = yield [lax.ppermute(send, "core", ring(2, 1)) for send in sends]
    sides = [[], []]
    for keep, got in zip(keeps, gots):
        lead, _, width = keep.shape
        held, new = (values.reshape(lead, y, x, z, part, width) for values in (keep, got))
        sides[0].append([held[: lead // 2], new[: lead // 2]])
        sides[1].append([held[lead // 2 :], new[lead // 2 :]])
    return sides


def sum_rows(pairs, part, join):
    sides = yield from core_steps(pairs, part)
    return (yield from scatter_steps(sides, labels, across + (("all z",),), join))


def regroup(keep, send, part):
    lead, half, width = keep.shape
    both = jnp.stack([keep.reshape(lead, 16, -1, width), send.reshape(lead, 16, -1, width)], axis=2)
    both = both.reshape(lead, half // part, 2, part, width)
    me = lax.axis_index("core")
    return tuple(pick(both, index, 2).reshape(keep.shape) for index in (me, 1 - me))


def all_rows(shard, last):
    width = shard.shape[1]
    half = half_of(width)
    others = lax.axis_size("z") - 1
    shard = yield shard
    pieces = yield send_all("z", [shard] * others)
    values = place_stage(shard, pieces, "z", 0)
    left, right = values[..., :half], values[..., half:]
    for left_axis, right_axis in across:
        dim = 1 if right_axis == "x" else 0
        left, right = yield left, right
        got = yield (
            send_all(left_axis, [left] * (lax.axis_size(left_axis) - 1)),
            send_all(right_axis, [right] * (lax.axis_size(right_axis) - 1)),
        )
        left = place_stage(left, got[0], left_axis, 0)
        right = place_stage(right, got[1], right_axis, dim)
    values = yield jnp.concatenate([left, right], axis=-1)
    got = yield send_all("core", [values])
    if not last:
        return values.reshape(-1, *values.shape[-2:]), got[0].reshape(-1, *values.shape[-2:])
    return place_stage(values, got, "core", 3).reshape(-1, width)


class Chain:
    def __init__(self, steps):
        self.steps = steps
        self.value = next(steps)
        self.done = False

    def advance(self):
        try:
            self.value = self.steps.send(self.value)
        except StopIteration as end:
            self.value, self.done = end.value, True


def phase(operand, work, launch=(), collect=None):
    collect = launch if collect is None else collect
    values, operand = lax.optimization_barrier(([chain.value for chain in launch], operand))
    for chain, value in zip(launch, values):
        chain.value = value
        chain.advance()
    result = work(operand)
    values, result = lax.optimization_barrier(([chain.value for chain in collect], result))
    for chain, value in zip(collect, values):
        chain.value = value
        chain.advance()
    return result


def on_device(
    hidden_state,
    segment_ids,
    valid_mask,
    cotangent,
    norm_gain,
    pool_gain,
    feed_gain,
    query_weight,
    key_weight,
    value_weight,
    output_weight,
    local_bias,
    global_bias,
    gate_weight,
    up_weight,
    down_weight,
):
    model_width = hidden_state.shape[2]
    hidden = gate_weight.shape[1]
    tok_rows = hidden_state.shape[1]
    own_part = norm_gain.shape[0]
    buckets = local_bias.shape[1]
    pairs = local_bias.shape[0] // 2
    blocks = tok_rows // 128
    own_slots = tok_rows // 16
    seq_count = lax.axis_size(seq)
    slot_count = own_slots * seq_count
    row_start = lax.axis_index(seq) * tok_rows
    first_slot = row_start // 16
    source = hidden_state[0]
    upstream = cotangent[0]
    own_segments = segment_ids[0]
    valid_float = valid_mask[0].astype(f32)

    aligned = own_part * 32 == model_width
    place = jnp.stack([lax.axis_index("core"), first_slot]).astype(i32)
    gain_columns = jnp.pad(jnp.stack([norm_gain, pool_gain, feed_gain], axis=1), ((0, 0), (0, 125)))
    packed, packed_second = pack_all(
        query_weight, key_weight, value_weight, output_weight, gain_columns, gate_weight, up_weight, down_weight, aligned
    )
    first = Chain(all_rows(packed, True))
    later = [Chain(all_rows(packed_second, False))] if aligned else []

    def share(operands):
        source, segments, valid = operands
        marks = jnp.concatenate([segments.reshape(-1, 128), valid.reshape(-1, 128)])
        shared = pack_shared(source, valid[0].astype(f32)[:, None], marks, seq_count)
        return lax.all_to_all(shared, seq, 0, 0, tiled=True)

    held = []
    phase(
        (source, segment_ids, valid_mask), lambda operands: held.append(share(operands)), [first] + later, [first]
    )

    def near_parts(operands):
        shared, local_bias = operands
        me = lax.axis_index(seq)
        edge = own_slots + 2 * (tok_rows // 128)
        raw_pool = shared[:, :own_slots].reshape(slot_count, model_width)
        all_marks = shared[:, own_slots:edge, :128].astype(i32).reshape(seq_count, 2, tok_rows)
        before, after = (
            jnp.where((near >= 0) & (near < seq_count), pick(shared[:, edge:], jnp.clip(near, 0, seq_count - 1), 0), 0)
            for near in (me - 1, me + 1)
        )
        all_segments, all_valid = all_marks[:, 0].reshape(-1), all_marks[:, 1].reshape(-1)
        slot_segments = all_segments.reshape(slot_count, 16)[:, 0]
        slot_live = jnp.sum(all_valid.reshape(slot_count, 16), axis=1) > 0
        segments_ext = lax.dynamic_slice_in_dim(
            jnp.pad(all_segments, 128, constant_values=-1), row_start, tok_rows + 256
        )
        valid_ext = lax.dynamic_slice_in_dim(jnp.pad(all_valid, 128), row_start, tok_rows + 256)
        feat_near = near_features(segments_ext, valid_ext)
        source_ext = jnp.concatenate([before, source, after], axis=0)
        return raw_pool, slot_segments, slot_live, feat_near, near_offsets(local_bias), source_ext

    raw_pool, slot_segments, slot_live, feat_near, bias_near, source_ext = phase(
        (held[0], local_bias), near_parts, [first], [first] + later
    )
    feat_query = query_features(own_segments)
    feat_far = phase(
        (global_bias, slot_segments, slot_live),
        lambda operands: far_features(*operands, first_slot, blocks),
        [first],
        [],
    )
    feat_far = phase(feat_far, lambda operands: operands, later, [first])
    phase((), lambda nothing: nothing, [first], [first] + later)
    weights = first.value

    bias, mixture, logs, queries, keys, vals, gkeys, gvals, normed, gains, turned, pooled = phase(
        (source_ext, raw_pool, weights, bias_near, feat_near, feat_far, feat_query),
        lambda operands: attention_forward(*operands),
        later,
    )
    phase((), lambda nothing: nothing, later)
    if aligned:
        held, other = later[0].value
        kernel_place = place
    else:
        wide = lax.all_gather(jnp.concatenate([gate_weight, up_weight], axis=1), everyone, axis=0, tiled=True)
        tall = lax.all_gather(down_weight, everyone, axis=0, tiled=True)
        tall = fold_rows(tall.reshape(32, -1, model_width))
        both = jnp.concatenate([wide.reshape(32, -1, 2 * hidden), tall], axis=2)
        both = both.reshape(16, 2, -1, 3 * hidden)
        held, other = both[:, 0], both[:, 1]
        kernel_place = place * jnp.array([0, 1], i32)
    layer_output, middle_grad, mixture_grad, small, out_keep, out_send, wide_keep, wide_send, down_keep, down_send = (
        feed_forward_both(source, mixture, weights, gains, upstream, held, other, kernel_place)
    )
    rest = []
    if aligned:
        pieces = [(wide_keep, wide_send), (down_keep, down_send), (out_keep, out_send)]
        rest = [Chain(sum_rows(pieces, own_part, -1))]
    table = jnp.zeros((32, 128), f32)
    count = pairs // calls
    waiting, started = [], []
    dnormed, draw = gains, gains
    keep_column = valid_float[:, None]
    for call in range(calls):
        keep, send, dnormed, draw, small, table = phase(
            (mixture_grad, small, table, dnormed, draw),
            lambda operands: attention_backward(
                call * count, count, own_part, queries, operands[0], keys, vals, gkeys, gvals, normed, turned, pooled, weights,
                logs, bias, feat_near, feat_far, feat_query, raw_pool, gains, kernel_place, *operands[1:],
            ),
            rest + started,
        )
        waiting.append((keep, send))
        if call > 0:
            started.append(Chain(core_steps(waiting, own_part)))
            waiting = []

    def return_rows(payload):
        return [lax.ppermute(payload[hop], seq, ring(seq_count, hop)) for hop in range(1, seq_count)]

    held = []
    phase(draw, lambda operands: held.append(return_rows(operands)), started[1:] + rest, started[1:])
    operands = held[0]
    sides = [sum((chain.value[side] for chain in started), []) for side in range(2)]
    last = Chain(scatter_steps(sides, labels, stages, 0))
    operands = phase(operands, lambda operands: operands, [last])
    input_delta = phase(
        operands,
        lambda received: input_gradient(source, keep_column, middle_grad, gains, dnormed, draw, received),
        [last],
        rest + [last],
    )
    phase((), lambda nothing: nothing, [last])
    total = last.value
    half = total.shape[0] // 2
    sides = [total[:half], total[half:]]
    extra = jnp.concatenate([side[half - 1] for side in sides], axis=-1)
    blocks_of_table = -(-4 * pairs // own_part)
    tables = extra[:, 128 : 128 + buckets * blocks_of_table].reshape(own_part, blocks_of_table, buckets)
    tables = tables.transpose(1, 0, 2).reshape((2,) + local_bias.shape)
    query_delta, key_delta, value_delta = (
        jnp.concatenate(
            [sides[pair % count][3 * (pair // count) + index] for pair in range(pairs)],
            axis=-1,
        )
        for index in range(3)
    )
    if aligned:
        total = rest[0].value[0]
        side, fold, half = total.shape[1] // 2, hidden // 2, model_width // 2
        left, right = total[:, :side], total[:, side:]
        gate_delta, up_delta = left[:, :hidden], right[:, :hidden]
        tall = jnp.concatenate([left[:, hidden : hidden + fold], right[:, hidden : hidden + fold]], axis=1)
        down_delta = unfold_rows(tall[None])[0]
        output_delta = jnp.concatenate([left[:, hidden + fold :], right[:, hidden + fold :]], axis=1)
    else:

        def whole_rows(keep, send):
            width = keep.shape[-1]
            both = jnp.stack([keep.reshape(16, -1, width), send.reshape(16, -1, width)], axis=1)
            return both.reshape(32, -1, width)

        def join(halves):
            return jnp.concatenate([halves[0], halves[1]], axis=-1)

        def scatter(grads):
            grads = grads.reshape(-1, grads.shape[-1])
            return lax.psum_scatter(grads, everyone, scatter_dimension=0, tiled=True).astype(f32)

        gate_delta = scatter(whole_rows(wide_keep[0], wide_send[0]))
        up_delta = scatter(whole_rows(wide_keep[1], wide_send[1]))
        output_delta = scatter(whole_rows(join(out_keep), join(out_send)))
        down_delta = scatter(unfold_rows(whole_rows(join(down_keep), join(down_send))))
    return (
        layer_output[None],
        input_delta[None],
        extra[:, 0],
        extra[:, 1],
        extra[:, 2],
        query_delta,
        key_delta,
        value_delta,
        output_delta,
        tables[0],
        tables[1],
        gate_delta,
        up_delta,
        down_delta,
    )


def solution(mesh):
    seq_size, batch_size = mesh.shape["seq"], mesh.shape["batch"]
    chips = Mesh(mesh.devices.reshape(2, seq_size // 2, batch_size // 2, 2), everyone)
    tokens = P(batch, seq, None)
    marks = P(batch, seq)
    row = P(everyone)
    matrix = P(everyone, None)
    whole = P()
    return jax.shard_map(
        on_device,
        mesh=chips,
        in_specs=(tokens, marks, marks, tokens, row, row, row)
        + (matrix,) * 4
        + (whole,) * 2
        + (matrix,) * 3,
        out_specs=(tokens, tokens, row, row, row)
        + (matrix,) * 4
        + (whole,) * 2
        + (matrix,) * 3,
        check_vma=False,
    )
```
